32 devices in a mesh: sy: 4 (over z), sx: 8 (over y, x, core).
Axes of the slice: x: 2, y: 2, z: 4, core: 2. Of those that a mesh axis runs over, the one named last changes fastest.
Arguments:
- loads: float32 [2, 16, 4, 1536], P(None, None, 'sy', 'sx'), may hold values from -16 to 16
- flex: float32 [4, 8, 768, 768], P('sy', 'sx'), may hold values from -1 to 6, as said below
- basis: float32 [4, 8, 16, 768], P('sy', 'sx'), may hold values from -0.21875 to 0.21875
- coarse_inv: float32 [512, 512], P('sx', 'sy'), may hold values from -1 to 5, as said below
- pair_size: int32 [2, 4, 8], P(None, 'sy', 'sx'), may hold values from 0 to 192, as said below
- owner: int32 [2, 4, 8], P(None, 'sy', 'sx'), may hold values from 0 to 1
- trace_slot: int32 [4, 4, 1536], P(None, 'sy', 'sx'), may hold values from 0 to 767, as said below
Outputs:
- multipliers: float32 [2, 16, 4, 1536], P(None, None, 'sy', 'sx')
- preconditioned: float32 [2, 16, 4, 1536], P(None, None, 'sy', 'sx')
The draws below stay inside these ranges and needn't reach their ends.
Inputs may be any that keep to these rules, and one draw needn't show every extreme that they name: `pair_size`: zero for the east interfaces of the last grid column and the south interfaces of the last grid row; every other entry is 1 or more, and 192 is reached. For every subdomain (i, j) the 768 entries trace_slot[s, i, j * 192 + m] are a permutation of 0 to 767. Each block flex[i, j] is symmetric positive definite. `coarse_inv`: with row (j * 4 + i) * 16 + k and column (i * 8 + j) * 16 + k naming the same coarse unknown, the matrix is symmetric positive definite.
All inputs are finite; a program needn't handle non-finite values.
Results may differ from the reference program's by a relative error of at most 0.0003.
Values sent between devices are 32-bit elements; how exact they have to be, the bound alone decides.
A program may use at most 64 MiB of HBM per device.

```python
import math
import jax
import jax.numpy as jnp
from jax import lax

SIDE_CAP = 192
TRACES = 768
COLUMNS = 16
MODES = 16
ITERATIONS = 2
COARSE = 512
N_SY = 4
N_SX = 8


def draw_loads(key, part):
    key_base = jax.random.fold_in(jax.random.fold_in(key, 31), 0)
    shape = (2, COLUMNS, N_SY, N_SX * SIDE_CAP)
    row_pos = jnp.arange(N_SY, dtype=jnp.float32)[:, None] / max(N_SY - 1, 1)
    col_pos = jnp.arange(N_SX, dtype=jnp.float32)[None, :] / max(N_SX - 1, 1)
    grid_scale = 3.0 ** ((row_pos + col_pos) * 0.5)
    base_draw = jnp.clip(jax.random.normal(key_base, shape, jnp.float32), -4.0, 4.0)
    return base_draw * jnp.repeat(grid_scale, SIDE_CAP, axis=1)


def draw_flex(key, part):
    trace_count = 4 * SIDE_CAP
    base_key = jax.random.fold_in(key, 11)

    def one_block(block_index):
        key_noise, key_diag = jax.random.split(jax.random.fold_in(base_key, block_index))
        noise_part = jnp.clip(jax.random.normal(key_noise, (trace_count, trace_count), jnp.float32), -5.0, 5.0)
        noise_part = (noise_part + noise_part.T) * (0.5 / math.sqrt(2.0 * trace_count))
        diagonal = jnp.exp(jax.random.uniform(key_diag, (trace_count,), jnp.float32, math.log(1.5), math.log(4.5)))
        places = jnp.arange(trace_count)
        return noise_part.at[places, places].add(diagonal)
    blocks = lax.map(one_block, jnp.arange(N_SY * N_SX, dtype=jnp.int32))
    return blocks.reshape(N_SY, N_SX, trace_count, trace_count)


def draw_coarse_inv(key, part):
    order = MODES * N_SY * N_SX
    key_noise, key_diag = jax.random.split(jax.random.fold_in(key, 23))
    noise_part = jnp.clip(jax.random.normal(key_noise, (order, order), jnp.float32), -5.0, 5.0)
    noise_part = (noise_part + noise_part.T) * (0.4 / math.sqrt(2.0 * order))
    diagonal = jnp.exp(jax.random.uniform(key_diag, (order,), jnp.float32, math.log(1.2), math.log(4.0)))
    places = jnp.arange(order)
    natural = noise_part.at[places, places].add(diagonal)
    row_order = jnp.arange(order).reshape(N_SY, N_SX, MODES).transpose(1, 0, 2).reshape(order)
    return natural[row_order]


def draw_pair_size(key, part):
    key_size, key_row, key_col = jax.random.split(jax.random.fold_in(key, 41), 3)
    pair_sizes = jax.random.randint(key_size, (2, N_SY, N_SX), 1, SIDE_CAP + 1)
    row_pick = jax.random.randint(key_row, (), 0, N_SY)
    col_pick = jax.random.randint(key_col, (), 0, N_SX - 1)
    pair_sizes = pair_sizes.at[0, row_pick, col_pick].set(SIDE_CAP)
    kind_ids = lax.broadcasted_iota(jnp.int32, (2, N_SY, N_SX), 0)
    row_ids = lax.broadcasted_iota(jnp.int32, (2, N_SY, N_SX), 1)
    col_ids = lax.broadcasted_iota(jnp.int32, (2, N_SY, N_SX), 2)
    live = jnp.where(kind_ids == 0, col_ids < N_SX - 1, row_ids < N_SY - 1)
    return jnp.where(live, pair_sizes, 0).astype(jnp.int32)


def draw_trace_slot(key, part):
    all_keys = jax.random.split(jax.random.fold_in(key, 53), N_SY * N_SX)

    def one_order(one_key):
        return jax.random.permutation(one_key, 4 * SIDE_CAP)
    permutes = jax.vmap(one_order)(all_keys)
    arranged = permutes.reshape(N_SY, N_SX, 4, SIDE_CAP).transpose(2, 0, 1, 3)
    return arranged.reshape(4, N_SY, N_SX * SIDE_CAP).astype(jnp.int32)


def plant(result, rng, least, top_value):
    longest = result.shape.index(max(result.shape))
    spots = []
    for shift in (0, 1):
        where = [jax.random.randint(jax.random.fold_in(rng, axis), (), 0, length) for axis, length in enumerate(result.shape)]
        where[longest] = (where[longest] + shift) % result.shape[longest]
        spots.append(tuple(where))
    return result.at[spots[0]].set(least).at[spots[1]].set(top_value)


def shard_levels(stream_key, extent, shards, smallest, high):
    factor_of, own = 1.0, jax.random.fold_in(stream_key, 6)
    for axis_at, blocks in shards:
        draws = jnp.exp(jax.random.uniform(jax.random.fold_in(own, axis_at), (blocks,), jnp.float32, smallest / len(shards), high / len(shards)))
        factor_of = factor_of * jnp.repeat(draws, extent[axis_at] // blocks).reshape([-1 if axis == axis_at else 1 for axis in range(len(extent))])
    return factor_of


def gaussian(key, extent, width, limit, cuts=(), kind=jnp.bfloat16):
    array = jax.random.normal(key, extent, jnp.float32) * width
    if len(cuts) > 0:
        array = shard_levels(key, extent, cuts, -0.22, 0.18) * array
    return jnp.clip(array, min=-limit, max=limit).astype(kind)


def setup_inputs(seed: int = 0) -> dict:
    arg_keys = jax.random.split(jax.random.key(seed), 8)
    return {
        "loads": draw_loads(jax.random.fold_in(arg_keys[7], 71), 0),
        "flex": draw_flex(jax.random.fold_in(arg_keys[7], 71), 0),
        "basis": gaussian(arg_keys[2], (N_SY, N_SX, MODES, TRACES), TRACES ** -0.5, 0.21875, ((0, 4), (1, 8)), jnp.float32),
        "coarse_inv": draw_coarse_inv(jax.random.fold_in(arg_keys[7], 71), 0),
        "pair_size": draw_pair_size(jax.random.fold_in(arg_keys[7], 71), 0),
        "owner": plant(jax.random.randint(arg_keys[5], (2, N_SY, N_SX), 0, 2), jax.random.fold_in(arg_keys[5], 1), 0, 1).astype(jnp.int32),
        "trace_slot": draw_trace_slot(jax.random.fold_in(arg_keys[7], 71), 0),
    }


precise = lax.Precision.HIGHEST


def spread_sides(vector, pair_signs):
    signed = vector * pair_signs[:, None, :, :, None]
    east_pairs = signed[0]
    south_pairs = signed[1]
    west_side = -jnp.pad(east_pairs, ((0, 0), (0, 0), (1, 0), (0, 0)))[:, :, :-1]
    north_side = -jnp.pad(south_pairs, ((0, 0), (1, 0), (0, 0), (0, 0)))[:, :-1]
    return jnp.stack([west_side, east_pairs, north_side, south_pairs], axis=3)


def collect_pairs(side_vals, pair_signs, pair_mask):
    from_east = jnp.pad(side_vals[:, :, 1:, 0], ((0, 0), (0, 0), (0, 1), (0, 0)))
    from_south = jnp.pad(side_vals[:, 1:, :, 2], ((0, 0), (0, 1), (0, 0), (0, 0)))
    jump_pairs = jnp.stack([side_vals[:, :, :, 1] - from_east, side_vals[:, :, :, 3] - from_south])
    return jump_pairs * pair_signs[:, None, :, :, None] * pair_mask[:, None]


def to_traces(side_vals, inverse):
    flattened = side_vals.reshape(COLUMNS, N_SY, N_SX, TRACES)
    index = jnp.broadcast_to(inverse[None], flattened.shape)
    return jnp.take_along_axis(flattened, index, axis=3)


def to_sides(traced, slots):
    index = jnp.broadcast_to(slots[None], traced.shape)
    picked = jnp.take_along_axis(traced, index, axis=3)
    return picked.reshape(COLUMNS, N_SY, N_SX, 4, SIDE_CAP)


def apply_flex(vector, flex, pair_signs, pair_mask, slots, inverse):
    traced = to_traces(spread_sides(vector, pair_signs), inverse)
    flex_out = jnp.einsum("ijkl,rijl->rijk", flex, traced, precision=precise)
    return collect_pairs(to_sides(flex_out, slots), pair_signs, pair_mask)


def coarse_part(vector, basis, coarse_inv, pair_signs, pair_mask, slots, inverse):
    traced = to_traces(spread_sides(vector, pair_signs), inverse)
    coarse_res = jnp.einsum("ijkl,rijl->ijkr", basis, traced, precision=precise).reshape(COARSE, COLUMNS)
    weights = jnp.dot(coarse_inv, coarse_res, precision=precise)
    weights = weights.reshape(N_SX, N_SY, MODES, COLUMNS).transpose(1, 0, 2, 3)
    spread_out = jnp.einsum("ijkr,ijkl->rijl", weights, basis, precision=precise)
    return collect_pairs(to_sides(spread_out, slots), pair_signs, pair_mask)


def reference(loads, flex, basis, coarse_inv, pair_size, owner, trace_slot):
    pair_signs = (1 - 2 * owner).astype(jnp.float32)
    position = lax.broadcasted_iota(jnp.int32, (2, N_SY, N_SX, SIDE_CAP), 3)
    pair_mask = (position < pair_size[:, :, :, None]).astype(jnp.float32)
    slots = trace_slot.reshape(4, N_SY, N_SX, SIDE_CAP).transpose(1, 2, 0, 3).reshape(N_SY, N_SX, TRACES)
    inverse = jnp.argsort(slots, axis=2).astype(jnp.int32)
    residual = loads.reshape(2, COLUMNS, N_SY, N_SX, SIDE_CAP) * pair_mask[:, None]

    def precondition(vector):
        return vector + coarse_part(vector, basis, coarse_inv, pair_signs, pair_mask, slots, inverse)

    def column_dot(first_vec, second_vec):
        return jnp.sum(first_vec * second_vec, axis=(0, 2, 3, 4))

    corrected = precondition(residual)
    norm_now = column_dot(residual, corrected)
    direction = corrected
    solution = jnp.zeros_like(residual)
    for iteration in range(ITERATIONS):
        images = apply_flex(direction, flex, pair_signs, pair_mask, slots, inverse)
        step_size = norm_now / column_dot(direction, images)
        factor = step_size[None, :, None, None, None]
        solution = solution + factor * direction
        residual = residual - factor * images
        corrected = precondition(residual)
        if iteration + 1 < ITERATIONS:
            norm_next = column_dot(residual, corrected)
            direction = corrected + (norm_next / norm_now)[None, :, None, None, None] * direction
            norm_now = norm_next
    out_shape = (2, COLUMNS, N_SY, N_SX * SIDE_CAP)
    return solution.reshape(out_shape), corrected.reshape(out_shape)
```

```python
import functools

import jax
import jax.numpy as jnp
from jax import lax
from jax.experimental import pallas as pl
from jax.experimental.pallas import tpu as pltpu
from jax.sharding import PartitionSpec as P

LANES = 128
MESH = pl.DeviceIdType.MESH
OPPOSITE = (1, 0, 3, 2)
F32 = jnp.float32
BF16 = jnp.bfloat16


def dot(a, b):
    return jnp.dot(a, b, preferred_element_type=F32)


def dot_nt(a, b):
    return lax.dot_general(a, b, (((1,), (1,)), ((), ())), preferred_element_type=F32)


def split(x):
    hi = x.astype(BF16)
    return hi, (x - hi.astype(F32)).astype(BF16)


def dot3_nt(x, w_hi, w_lo):
    rows = x.shape[0]
    hi, lo = split(x)
    both = dot_nt(jnp.concatenate([hi, lo], axis=0), w_hi)
    return both[:rows] + both[rows:] + dot_nt(hi, w_lo)


def dot_exact(x, ones):
    rows = x.shape[0]
    both = dot(jnp.concatenate(split(x), axis=0), ones)
    return both[:rows] + both[rows:]


def dot3(x, w_hi, w_lo):
    rows = x.shape[0]
    hi, lo = split(x)
    both = dot(jnp.concatenate([hi, lo], axis=0), w_hi)
    return both[:rows] + both[rows:] + dot(hi, w_lo)


def kernel(
    n_sy, n_sx, side, pad,
    loads_ref, flex_hbm, basis_ref, cinv_ref, size_ref, owner_ref, slot_ref,
    both_ref,
    flex_v, flex_hi, flex_lo, q_t, slot_row, slot_col, a_hi, a_lo,
    b8_hi, b8_lo, bb_hi, bb_lo, ka_hi, ka_lo, loads_s, send_a, recv_a, cinv_in, cr,
    g_send, g_recv, c_send, c_all, five_send, five_all, sum_send, sum_all,
    ready_sem, flex_sem, sa_sem, ra_sem, sc_sem, rc_sem, sr_sem, rr_sem, sg_sem, rg_sem,
    sag_sem, rag_sem, ss_sem, rs_sem,
):
    cols = loads_ref.shape[1]
    modes = basis_ref.shape[2]
    traces = flex_v.shape[0]
    full = 4 * pad
    groups = LANES // modes
    halves = cols // groups
    n = n_sy * n_sx
    i = lax.axis_index("sy")
    j = lax.axis_index("sx")
    me = i * n_sx + j
    exists = (j > 0, j < n_sx - 1, i > 0, i < n_sy - 1)
    place = ((i, j - 1), (i, j + 1), (i - 1, j), (i + 1, j))

    flex_copy = pltpu.make_async_copy(flex_hbm.at[0, 0], flex_v, flex_sem)
    flex_copy.start()
    recv_a[...] = jnp.zeros_like(recv_a)
    g_recv[...] = jnp.zeros_like(g_recv)
    cinv_in[...] = jnp.zeros_like(cinv_in)
    five = 1 + len(exists)
    wide = five * LANES
    for phase in range(2):
        edge = jnp.zeros((n_sx, 1, halves * wide), F32)
        five_all[phase, pl.ds(0, n_sx)] = edge
        five_all[phase, pl.ds(n_sx + n, n_sx)] = edge

    barrier = pltpu.get_barrier_semaphore()

    def device(o):
        t = lax.rem(me + o, n)
        return (lax.div(t, n_sx), lax.rem(t, n_sx))

    row_mates = [(i, lax.rem(j + o, n_sx)) for o in range(1, n_sx)]
    column_mates = [(lax.rem(i + o, n_sy), j) for o in range(1, n_sy)]
    for mate in row_mates + column_mates:
        pl.semaphore_signal(barrier, inc=1, device_id=mate, device_id_type=MESH)

    slot_row[...] = jnp.full_like(slot_row, -1)
    for s in range(4):
        slot_row[:, s * pad : s * pad + side] = jnp.broadcast_to(slot_ref[s], (8, side))
    slot_col[...] = jnp.transpose(slot_row[...].astype(F32)).astype(jnp.int32)
    trace_id = lax.broadcasted_iota(jnp.int32, (traces, full), 0)
    q_t[...] = (trace_id == slot_row[0:1, :]).astype(F32).astype(BF16)

    basis_hi, basis_lo = split(basis_ref[0, 0])
    both = dot(jnp.concatenate([basis_hi, basis_lo], axis=0), q_t[...])
    basis_side = both[:modes] + both[modes:]

    lane = lax.broadcasted_iota(jnp.int32, (1, pad), 1)
    signs = [(1 - 2 * owner_ref[0, 0, a]).astype(F32) for a in range(2)]
    own_mask = [jnp.where(lane < size_ref[0, 0, a], 1.0, 0.0).astype(F32) for a in range(2)]
    loads_s[...] = jnp.zeros_like(loads_s)
    for a in range(2):
        loads_s[a, :, :side] = loads_ref[a, :, 0, :]
    for s in range(4):
        send_a[s, cols : cols + modes] = basis_side[:, s * pad : (s + 1) * pad]
    start_side = [None] * 4
    for a, s in ((0, 1), (1, 3)):
        start_side[s] = loads_s[a] * (own_mask[a] * signs[a])
        send_a[s, :cols] = start_side[s]
        send_a[s, cols + modes :] = jnp.broadcast_to(own_mask[a], (8, pad))

    flex_copy.wait()
    f_hi, f_lo = split(flex_v[...])
    flex_hi[...] = f_hi
    flex_lo[...] = f_lo
    chunk = full // 3
    n_chunks = full // chunk

    def permute(step, carry):
        rows = pl.ds(pl.multiple_of(step * chunk, chunk), chunk)
        ids = lax.broadcasted_iota(jnp.int32, (chunk, traces), 1)
        q = (ids == slot_col[rows, 0:1]).astype(F32).astype(BF16)
        half = [dot(q, flex_hi[...]).astype(BF16), dot(q, flex_lo[...]).astype(BF16)]
        both = dot(jnp.concatenate(half, axis=0), q_t[...]).astype(BF16)
        a_hi[rows, :] = both[:chunk]
        a_lo[rows, :] = both[chunk:]
        return carry

    b8 = jnp.transpose(jnp.concatenate([basis_side] * groups, axis=0))
    part_hi, part_lo = split(b8)
    b8_hi[...] = part_hi
    b8_lo[...] = part_lo

    early = 1

    pl.semaphore_wait(barrier, n_sx + n_sy - 2)
    for mate in row_mates:
        pl.semaphore_signal(ready_sem, inc=1, device_id=mate, device_id_type=MESH)

    def first(s):
        return pltpu.make_async_remote_copy(
            src_ref=send_a.at[s],
            dst_ref=recv_a.at[OPPOSITE[s]],
            send_sem=sa_sem.at[s],
            recv_sem=ra_sem.at[OPPOSITE[s]],
            device_id=place[s],
            device_id_type=MESH,
        )

    def first_back(s):
        return pltpu.make_async_remote_copy(
            src_ref=send_a.at[s, pl.ds(cols, modes)],
            dst_ref=recv_a.at[OPPOSITE[s], pl.ds(cols, modes)],
            send_sem=sa_sem.at[s],
            recv_sem=ra_sem.at[OPPOSITE[s]],
            device_id=place[s],
            device_id_type=MESH,
        )

    make_first = (first_back, first, first_back, first)
    for s in range(4):
        @pl.when(exists[s])
        def _(s=s):
            make_first[s](s).start()

    def column_copy(slot, di, shift):
        i2 = lax.rem(i + di, n_sy)
        return pltpu.make_async_remote_copy(
            src_ref=cinv_ref.at[pl.ds(pl.multiple_of((i2 + shift) * modes, 8), modes)],
            dst_ref=cinv_in.at[slot, i],
            send_sem=sc_sem.at[slot, i2],
            recv_sem=rc_sem.at[slot, i],
            device_id=(i2, j),
            device_id_type=MESH,
        )

    def column_send(act):
        for di in range(1, n_sy):
            i2 = lax.rem(i + di, n_sy)
            act(column_copy(0, di, 0))

            @pl.when(i2 > 0)
            def _(di=di):
                act(column_copy(3, di, -1))

            @pl.when(i2 < n_sy - 1)
            def _(di=di):
                act(column_copy(4, di, 1))

    def landed(slot, src):
        here = cinv_in.at[slot, src]
        pltpu.make_async_copy(here, here, rc_sem.at[slot, src]).wait()

    def relay(s):
        return pltpu.make_async_remote_copy(
            src_ref=cinv_in.at[0],
            dst_ref=cinv_in.at[1 + OPPOSITE[s]],
            send_sem=sr_sem.at[s],
            recv_sem=rr_sem.at[OPPOSITE[s]],
            device_id=place[s],
            device_id_type=MESH,
        )

    column_send(lambda copy: copy.start())

    cinv_in[0, i] = cinv_ref[pl.ds(pl.multiple_of(i * modes, 8), modes)]

    @pl.when(i > 0)
    def _():
        cinv_in[3, i] = cinv_ref[pl.ds(pl.multiple_of((i - 1) * modes, 8), modes)]

    @pl.when(i < n_sy - 1)
    def _():
        cinv_in[4, i] = cinv_ref[pl.ds(pl.multiple_of((i + 1) * modes, 8), modes)]


    lax.fori_loop(0, early, permute, 0)

    for s in range(4):
        @pl.when(exists[OPPOSITE[s]])
        def _(s=s):
            make_first[s](s).wait_recv()
    masks = [None] * 4
    for a, s in ((0, 0), (1, 2)):
        start_side[s] = -recv_a[s, :cols]
        masks[s] = recv_a[s, cols + modes : cols + modes + 1]
        masks[s + 1] = own_mask[a]
    mask = jnp.concatenate(masks, axis=1)
    res = jnp.concatenate(start_side, axis=1)

    bit_row = lax.broadcasted_iota(jnp.int32, (cols, LANES), 0)
    bit_lane = lax.broadcasted_iota(jnp.int32, (cols, LANES), 1)
    pick = jnp.where(lax.div(bit_lane, modes) == lax.rem(bit_row, groups), 1.0, 0.0).astype(F32)
    spot = [jnp.where(bit_lane == bit_row + q * cols, 1.0, 0.0).astype(F32) for q in range(3)]

    def as_row(sums):
        row = jnp.zeros((cols, LANES), F32)
        for q, value in enumerate(sums):
            row = row + value * spot[q]
        return jnp.sum(row, axis=0, keepdims=True)

    def send_all(src, dst, send_sem, recv_sem):
        def send(o, carry):
            pltpu.make_async_remote_copy(
                src_ref=src,
                dst_ref=dst,
                send_sem=send_sem,
                recv_sem=recv_sem,
                device_id=device(o),
                device_id_type=MESH,
            ).start()
            return carry

        lax.fori_loop(1, n, send, 0)

    def all_of(block, send_sem, recv_sem):
        return pltpu.make_async_remote_copy(
            src_ref=block,
            dst_ref=block,
            send_sem=send_sem,
            recv_sem=recv_sem,
            device_id=device(1),
            device_id_type=MESH,
        )

    def all_coarse(phase):
        block = c_all.at[pl.ds(0, n - 1)] if phase == 0 else five_all.at[phase - 1, pl.ds(0, n - 1)]
        return all_of(block, sag_sem.at[phase], rag_sem.at[phase])

    def all_sums(phase):
        return all_of(sum_all.at[phase, pl.ds(0, n - 1)], ss_sem.at[phase], rs_sem.at[phase])

    def coarse_send(vec):
        product = dot3(vec, b8_hi[...], b8_lo[...]) * pick
        pieces = [
            jnp.sum(product[h * groups : (h + 1) * groups], axis=0, keepdims=True) for h in range(halves)
        ]
        message = jnp.concatenate(pieces, axis=1)
        c_send[...] = message
        c_all[me] = message
        pl.semaphore_wait(ready_sem, n_sx - 1)
        send_all(c_send, c_all.at[me], sag_sem.at[0], rag_sem.at[0])

    def five_send_all(phase, message):
        five_send[phase - 1] = message
        five_all[phase - 1, n_sx + me] = message
        send_all(
            five_send.at[phase - 1], five_all.at[phase - 1, n_sx + me], sag_sem.at[phase], rag_sem.at[phase]
        )

    def sums_send(phase, row):
        sum_send[phase] = row
        sum_all[phase, me] = row
        send_all(sum_send.at[phase], sum_all.at[phase, me], ss_sem.at[phase], rs_sem.at[phase])

    unroll = 8
    shifts = (0, 1, -1, n_sx, -n_sx)

    def coarse_row(phase, d, h):
        if phase == 0:
            return c_all[d, :, h * LANES : (h + 1) * LANES]
        row = None
        for q, shift in enumerate(shifts):
            at = h * wide + q * LANES
            part = five_all[phase - 1, d + (n_sx + shift), :, at : at + LANES]
            row = part if row is None else row + part
        return row

    def coarse_take(phase):
        all_coarse(phase).wait_recv()

        def add(step, totals):
            totals = list(totals)
            for u in range(unroll):
                d = step * unroll + u
                rows = cr[d]
                for h in range(halves):
                    totals[h] = totals[h] + rows * coarse_row(phase, d, h)
            return tuple(totals)

        zero = jnp.zeros((five * modes, LANES), F32)
        return lax.fori_loop(0, n // unroll, add, (zero,) * halves)

    def weights_of(totals):
        gather = pick[:groups].astype(BF16)
        parts = []
        for total in totals:
            hi, lo = split(total)
            parts.append(dot_nt(gather, hi) + dot_nt(gather, lo))
        return jnp.concatenate(parts, axis=0)

    same_row = lax.broadcasted_iota(jnp.int32, (LANES, LANES), 0)
    same_lane = lax.broadcasted_iota(jnp.int32, (LANES, LANES), 1)
    same = (lax.div(same_row, modes) == lax.div(same_lane, modes)).astype(F32).astype(BF16)
    mode_row = lax.broadcasted_iota(jnp.int32, (modes, LANES), 0)
    mode_lane = lax.broadcasted_iota(jnp.int32, (modes, LANES), 1)
    on_mode = jnp.where(lax.rem(mode_lane, modes) == mode_row, 1.0, 0.0).astype(F32)
    wide_row = lax.broadcasted_iota(jnp.int32, (five * modes, wide), 0)
    wide_lane = lax.broadcasted_iota(jnp.int32, (five * modes, wide), 1)
    lay = jnp.where(
        (lax.div(wide_row, modes) == lax.div(wide_lane, LANES)) & (lax.rem(wide_row, modes) == lax.rem(wide_lane, modes)),
        1.0, 0.0,
    ).astype(F32).astype(BF16)

    def flat(values):
        spread = dot_exact(values, lay)
        pieces = []
        for h in range(halves):
            part = spread[h * groups : (h + 1) * groups]
            part = jnp.concatenate([part[:, q * LANES : (q + 1) * LANES] * pick[:groups] for q in range(five)], axis=1)
            pieces.append(jnp.sum(part, axis=0, keepdims=True))
        return jnp.concatenate(pieces, axis=1)

    def flow(totals, coupling):
        weights = dot_exact(jnp.concatenate(totals, axis=0), same)
        rows = five * modes
        joined = jnp.concatenate([weights[h * rows : (h + 1) * rows] for h in range(halves)], axis=1)
        joined_hi, joined_lo = split(joined)
        result = dot3(coupling, joined_hi, joined_lo)
        pieces = []
        for h in range(halves):
            for q in range(five):
                block = result[q * modes : (q + 1) * modes, h * LANES : (h + 1) * LANES]
                pieces.append(jnp.sum(block * on_mode, axis=0, keepdims=True))
        return jnp.concatenate(pieces, axis=1)

    def sums_of(phase, count):
        all_sums(phase).wait_recv()
        row = jnp.sum(sum_all[phase, :, 0, :], axis=0, keepdims=True)
        return [jnp.sum(row * spot[q], axis=1, keepdims=True) for q in range(count)]

    def swap(phase, s):
        return pltpu.make_async_remote_copy(
            src_ref=g_send.at[phase, s],
            dst_ref=g_recv.at[phase, OPPOSITE[s]],
            send_sem=sg_sem.at[phase, s],
            recv_sem=rg_sem.at[phase, OPPOSITE[s]],
            device_id=place[s],
            device_id_type=MESH,
        )

    def swap_start(phase, out):
        for s in range(4):
            g_send[phase, s] = out[:, s * pad : (s + 1) * pad]
        for s in range(4):
            @pl.when(exists[s])
            def _(s=s):
                swap(phase, s).start()

    def dual_take(phase, out):
        for s in range(4):
            @pl.when(exists[OPPOSITE[s]])
            def _(s=s):
                swap(phase, s).wait_recv()
        other = jnp.concatenate([g_recv[phase, s] for s in range(4)], axis=1)
        return (out - other) * mask

    def own_dot(x, y):
        total = x[:, pad : 2 * pad] * y[:, pad : 2 * pad] + x[:, 3 * pad :] * y[:, 3 * pad :]
        return jnp.sum(total, axis=1, keepdims=True)

    coarse_send(res)

    for di in range(1, n_sy):
        landed(0, lax.rem(i + di, n_sy))
    for s in range(2):
        @pl.when(exists[s])
        def _(s=s):
            relay(s).start()

    own_part = basis_side * mask
    lanes_at = lax.broadcasted_iota(jnp.int32, (modes, full), 1)
    blocks = [own_part]
    nbr = jnp.concatenate([recv_a[s, cols : cols + modes] for s in range(4)], axis=1) * mask
    for s in range(4):
        blocks.append(jnp.where(lax.div(lanes_at, pad) == s, -nbr, 0.0))
    basis_five = jnp.concatenate(blocks, axis=0)
    part_hi, part_lo = split(basis_five)
    bb_hi[...] = part_hi
    bb_lo[...] = part_lo

    lax.fori_loop(early, n_chunks, permute, 0)
    flexed = dot3(jnp.concatenate([basis_five, res], axis=0), a_hi[...], a_lo[...])
    flexed_basis = flexed[: five * modes]
    flexed_res = flexed[five * modes :]
    part_hi, part_lo = split(flexed_basis)
    ka_hi[...] = part_hi
    ka_lo[...] = part_lo
    coupling = dot3_nt(flexed_basis, bb_hi[...], bb_lo[...])
    known = flat(dot3_nt(res, ka_hi[...], ka_lo[...]))
    for di in range(1, n_sy):
        src = lax.rem(i + di, n_sy)

        @pl.when(i > 0)
        def _(src=src):
            landed(3, src)

        @pl.when(i < n_sy - 1)
        def _(src=src):
            landed(4, src)

    for s in range(2):
        @pl.when(exists[OPPOSITE[s]])
        def _(s=s):
            relay(s).wait_recv()

    group_of = lax.div(lax.broadcasted_iota(jnp.int32, (5 * modes, LANES), 1), modes)

    def widen(i2, carry):
        for j2 in range(n_sx):
            at = (j2 // groups) * LANES
            value = jnp.concatenate([cinv_in[s, i2, :, at : at + LANES] for s in range(5)], axis=0)
            value = jnp.where(group_of == j2 % groups, value, 0.0)
            shift = modes
            while shift < LANES:
                value = value + pltpu.roll(value, shift, 1)
                shift *= 2
            cr[i2 * n_sx + j2] = value
        return carry

    lax.fori_loop(0, n_sy, widen, 0)

    totals = coarse_take(0)
    five_send_all(1, flow(totals, coupling) + known)
    weights = weights_of(totals)
    out0 = flexed_res + dot3(weights, ka_hi[...], ka_lo[...])
    swap_start(0, out0)
    cor0 = res + dot3(weights, bb_hi[...], bb_lo[...])
    curve_part = jnp.sum(cor0 * out0, axis=1, keepdims=True)
    norm_part = own_dot(res, cor0)
    sums_send(0, as_row([norm_part, curve_part]))
    image0 = dual_take(0, out0)
    known = flat(dot3_nt(image0, ka_hi[...], ka_lo[...]))
    flexed_image = dot3(image0, a_hi[...], a_lo[...])

    totals = coarse_take(1)
    five_send_all(2, flow(totals, coupling) + known)
    weights = weights_of(totals)
    out1 = flexed_image + dot3(weights, ka_hi[...], ka_lo[...])
    swap_start(1, out1)
    pre_image0 = image0 + dot3(weights, bb_hi[...], bb_lo[...])
    norm0, curve0 = sums_of(0, 2)
    step0 = norm0 / curve0
    res1 = res - step0 * image0
    cor1 = cor0 - step0 * pre_image0
    flexed_cor1 = out0 - step0 * out1
    curve_part = jnp.sum(cor1 * flexed_cor1, axis=1, keepdims=True)
    norm_part = own_dot(res1, cor1)
    cross_part = own_dot(cor1, image0)
    sums_send(1, as_row([norm_part, curve_part, cross_part]))
    image1 = dual_take(1, out1)

    norm1, curve1, cross = sums_of(1, 3)
    beta = norm1 / norm0
    step1 = norm1 / (curve1 + 2.0 * beta * cross + beta * beta * curve0)
    total = step0 * cor0 + step1 * (cor1 + beta * cor0)
    near = cor1 - step1 * ((1.0 + beta) * pre_image0 - step0 * image1)
    weights = weights_of(coarse_take(2))
    cor2 = near + (step1 * step0) * dot3(weights, bb_hi[...], bb_lo[...])
    for a in range(2):
        at = (2 * a + 1) * pad
        both_ref[0, a] = total[:, at : at + side] * signs[a]
        both_ref[1, a] = cor2[:, at : at + side] * signs[a]

    for s in range(4):
        @pl.when(exists[s])
        def _(s=s):
            make_first[s](s).wait_send()
            swap(0, s).wait_send()
            swap(1, s).wait_send()
    column_send(lambda copy: copy.wait_send())
    for s in range(2):
        @pl.when(exists[s])
        def _(s=s):
            relay(s).wait_send()
    for phase in range(3):
        all_coarse(phase).wait_send()
    for phase in range(2):
        all_sums(phase).wait_send()


def lay_out(both_ref, mult_ref, prec_ref):
    for a in range(2):
        mult_ref[a, :, 0, :] = both_ref[0, a]
        prec_ref[a, :, 0, :] = both_ref[1, a]


def per_device(n_sy, n_sx, loads, flex, basis, coarse_inv, pair_size, owner, trace_slot):
    cols, side = loads.shape[1], loads.shape[3]
    modes, traces = basis.shape[2], basis.shape[3]
    pad = side
    full = 4 * pad
    n = n_sy * n_sx
    width = cols * modes
    dma = pltpu.SemaphoreType.DMA
    vmem = pl.BlockSpec(memory_space=pltpu.VMEM)
    smem = pl.BlockSpec(memory_space=pltpu.SMEM)
    both = pl.pallas_call(
        functools.partial(kernel, n_sy, n_sx, side, pad),
        out_shape=jax.ShapeDtypeStruct((2, 2, cols, side), F32),
        in_specs=[vmem, pl.BlockSpec(memory_space=pl.ANY), vmem, vmem, smem, smem, vmem],
        out_specs=vmem,
        scratch_shapes=[
            pltpu.VMEM((traces, traces), F32),
            pltpu.VMEM((traces, traces), BF16),
            pltpu.VMEM((traces, traces), BF16),
            pltpu.VMEM((traces, full), BF16),
            pltpu.VMEM((8, full), jnp.int32),
            pltpu.VMEM((full, 8), jnp.int32),
            pltpu.VMEM((full, full), BF16),
            pltpu.VMEM((full, full), BF16),
            pltpu.VMEM((full, LANES), BF16),
            pltpu.VMEM((full, LANES), BF16),
            pltpu.VMEM((5 * modes, full), BF16),
            pltpu.VMEM((5 * modes, full), BF16),
            pltpu.VMEM((5 * modes, full), BF16),
            pltpu.VMEM((5 * modes, full), BF16),
            pltpu.VMEM((2, cols, pad), F32),
            pltpu.VMEM((4, cols + modes + 8, pad), F32),
            pltpu.VMEM((4, cols + modes + 8, pad), F32),
            pltpu.VMEM((5, n_sy, modes, coarse_inv.shape[1]), F32),
            pltpu.VMEM((n, 5 * modes, LANES), F32),
            pltpu.VMEM((2, 4, cols, pad), F32),
            pltpu.VMEM((2, 4, cols, pad), F32),
            pltpu.VMEM((1, width), F32),
            pltpu.VMEM((n, 1, width), F32),
            pltpu.VMEM((2, 1, 5 * width), F32),
            pltpu.VMEM((2, n + 2 * n_sx, 1, 5 * width), F32),
            pltpu.VMEM((2, 1, LANES), F32),
            pltpu.VMEM((2, n, 1, LANES), F32),
            pltpu.SemaphoreType.REGULAR,
            dma,
            dma((4,)),
            dma((4,)),
            dma((5, n_sy)),
            dma((5, n_sy)),
            dma((2,)),
            dma((2,)),
            dma((2, 4)),
            dma((2, 4)),
            dma((3,)),
            dma((3,)),
            dma((2,)),
            dma((2,)),
        ],
        compiler_params=pltpu.CompilerParams(
            collective_id=0, has_side_effects=True, vmem_limit_bytes=60 * 1024 * 1024
        ),
    )(
        loads, flex, basis, coarse_inv,
        jnp.transpose(pair_size, (1, 2, 0)), jnp.transpose(owner, (1, 2, 0)), trace_slot,
    )

    out = jax.ShapeDtypeStruct(loads.shape, F32)
    return pl.pallas_call(
        lay_out, out_shape=(out, out), in_specs=[vmem], out_specs=(vmem, vmem)
    )(both)


def solution(mesh):
    return jax.shard_map(
        functools.partial(per_device, mesh.shape["sy"], mesh.shape["sx"]),
        mesh=mesh,
        in_specs=(
            P(None, None, "sy", "sx"),
            P("sy", "sx", None, None),
            P("sy", "sx", None, None),
            P("sx", "sy"),
            P(None, "sy", "sx"),
            P(None, "sy", "sx"),
            P(None, "sy", "sx"),
        ),
        out_specs=(P(None, None, "sy", "sx"), P(None, None, "sy", "sx")),
        check_vma=False,
    )
```

```python
import functools

import jax
import jax.numpy as jnp
from jax import lax
from jax.experimental import pallas as pl
from jax.experimental.pallas import tpu as pltpu
from jax.sharding import PartitionSpec as P

LANES = 128
MESH = pl.DeviceIdType.MESH
OPPOSITE = (1, 0, 3, 2)
F32 = jnp.float32
BF16 = jnp.bfloat16


def dot(a, b):
    return jnp.dot(a, b, preferred_element_type=F32)


def dot_nt(a, b):
    return lax.dot_general(a, b, (((1,), (1,)), ((), ())), preferred_element_type=F32)


def split(x):
    hi = x.astype(BF16)
    return hi, (x - hi.astype(F32)).astype(BF16)


def dot3_nt(x, w_hi, w_lo):
    rows = x.shape[0]
    hi, lo = split(x)
    both = dot_nt(jnp.concatenate([hi, lo], axis=0), w_hi)
    return both[:rows] + both[rows:] + dot_nt(hi, w_lo)


def dot_exact(x, ones):
    rows = x.shape[0]
    both = dot(jnp.concatenate(split(x), axis=0), ones)
    return both[:rows] + both[rows:]


def dot3(x, w_hi, w_lo):
    rows = x.shape[0]
    hi, lo = split(x)
    both = dot(jnp.concatenate([hi, lo], axis=0), w_hi)
    return both[:rows] + both[rows:] + dot(hi, w_lo)


def kernel(
    n_sy, n_sx, side, pad,
    loads_in, flex_in, basis_in, cinv_own, size_in, owner_in, slot_in,
    both_ref,
    loads_ref, basis_ref, cinv_ref, size_ref, owner_ref, slot_ref,
    flex_v, flex_hi, flex_lo, q, q_t, slot_row, slot_col,
    b8_hi, b8_lo, bb_hi, bb_lo, ka_hi, ka_lo, loads_s, send_a, recv_a, cinv_in, turned, side_in, cr,
    g_send, g_recv, c_send, c_all, five_send, five_all,
    ready_sem, flex_sem, in_sem, sa_sem, ra_sem, sc_sem, rc_sem, ss_sem, rs_sem, sg_sem, rg_sem,
    sag_sem, rag_sem,
):
    cols = loads_ref.shape[1]
    modes = basis_ref.shape[2]
    traces = flex_v.shape[0]
    full = 4 * pad
    groups = LANES // modes
    halves = cols // groups
    n = n_sy * n_sx
    i = lax.axis_index("sy")
    j = lax.axis_index("sx")
    me = i * n_sx + j
    exists = (j > 0, j < n_sx - 1, i > 0, i < n_sy - 1)
    place = ((i, j - 1), (i, j + 1), (i - 1, j), (i + 1, j))

    barrier = pltpu.get_barrier_semaphore()
    row_mates = [(i, lax.rem(j + o, n_sx)) for o in range(1, n_sx)]
    column_mates = [(lax.rem(i + o, n_sy), j) for o in range(1, n_sy)]
    for mate in row_mates + column_mates:
        pl.semaphore_signal(barrier, inc=1, device_id=mate, device_id_type=MESH)

    fetches = [
        pltpu.make_async_copy(src, dst, in_sem.at[q])
        for q, (src, dst) in enumerate(
            (
                (slot_in, slot_ref), (basis_in, basis_ref), (cinv_own, cinv_ref), (loads_in, loads_ref),
                (size_in, size_ref), (owner_in, owner_ref),
            )
        )
    ]
    for fetch in fetches:
        fetch.start()
    flex_copy = pltpu.make_async_copy(flex_in.at[0, 0], flex_v, flex_sem)
    flex_copy.start()
    for s in range(4):
        @pl.when(jnp.logical_not(exists[s]))
        def _(s=s):
            recv_a[s] = jnp.zeros(recv_a.shape[1:], F32)
            for phase in range(2):
                g_recv[phase, s] = jnp.zeros(g_recv.shape[2:], F32)
            if s >= 2:
                cinv_in[s - 2] = jnp.zeros(cinv_in.shape[1:], F32)

    turned[...] = jnp.zeros_like(turned)
    five = 1 + len(exists)
    wide = five * LANES
    for phase in range(2):
        edge = jnp.zeros((n_sx, 1, halves * wide + LANES), F32)
        five_all[phase, pl.ds(0, n_sx)] = edge
        five_all[phase, pl.ds(n_sx + n, n_sx)] = edge

    def shifted(at, o, size):
        return lax.bitwise_xor(at, o) if size & (size - 1) == 0 else lax.rem(at + o, size)

    def device(o):
        return (shifted(i, lax.rem(o, n_sy), n_sy), shifted(j, lax.div(o, n_sy), n_sx))

    for fetch in fetches:
        fetch.wait()
    slot_row[...] = jnp.full_like(slot_row, -1)
    for s in range(4):
        slot_row[:, s * pad : s * pad + side] = jnp.broadcast_to(slot_ref[s], (8, side))
    slot_col[...] = jnp.transpose(slot_row[...].astype(F32)).astype(jnp.int32)
    trace_id = lax.broadcasted_iota(jnp.int32, (traces, full), 0)
    q_t[...] = (trace_id == slot_row[0:1, :]).astype(F32).astype(BF16)
    slot_id = lax.broadcasted_iota(jnp.int32, (full, traces), 1)
    q[...] = (slot_id == slot_col[:, 0:1]).astype(F32).astype(BF16)

    basis_hi, basis_lo = split(basis_ref[0, 0])
    both = dot(jnp.concatenate([basis_hi, basis_lo], axis=0), q_t[...])
    basis_side = both[:modes] + both[modes:]

    lane = lax.broadcasted_iota(jnp.int32, (1, pad), 1)
    signs = [(1 - 2 * owner_ref[0, 0, a]).astype(F32) for a in range(2)]
    own_mask = [jnp.where(lane < size_ref[0, 0, a], 1.0, 0.0).astype(F32) for a in range(2)]
    loads_s[...] = jnp.zeros_like(loads_s)
    for a in range(2):
        loads_s[a, :, :side] = loads_ref[a, :, 0, :]
    for s in range(4):
        send_a[s, cols : cols + modes] = basis_side[:, s * pad : (s + 1) * pad]
    start_side = [None] * 4
    for a, s in ((0, 1), (1, 3)):
        start_side[s] = loads_s[a] * (own_mask[a] * signs[a])
        send_a[s, :cols] = start_side[s]
        send_a[s, cols + modes :] = jnp.broadcast_to(own_mask[a], (8, pad))

    flex_copy.wait()
    f_hi, f_lo = split(flex_v[...])
    flex_hi[...] = f_hi
    flex_lo[...] = f_lo

    def flexed_of(vec):
        rows = vec.shape[0]
        traced = dot(jnp.concatenate(split(vec), axis=0), q[...]).astype(BF16)
        both = dot(traced, flex_hi[...])
        out = both[:rows] + both[rows:] + dot(traced[:rows], flex_lo[...])
        return dot_exact(out, q_t[...])

    turned[modes : (n_sx + 1) * modes, : n_sy * modes] = jnp.transpose(cinv_ref[...])

    b8 = jnp.transpose(jnp.concatenate([basis_side] * groups, axis=0))
    part_hi, part_lo = split(b8)
    b8_hi[...] = part_hi
    b8_lo[...] = part_lo

    pl.semaphore_wait(barrier, n_sx + n_sy - 2)
    for mate in row_mates:
        pl.semaphore_signal(ready_sem, inc=1, device_id=mate, device_id_type=MESH)

    def first(s):
        return pltpu.make_async_remote_copy(
            src_ref=send_a.at[s],
            dst_ref=recv_a.at[OPPOSITE[s]],
            send_sem=sa_sem.at[s],
            recv_sem=ra_sem.at[OPPOSITE[s]],
            device_id=place[s],
            device_id_type=MESH,
        )

    def first_back(s):
        return pltpu.make_async_remote_copy(
            src_ref=send_a.at[s, pl.ds(cols, modes)],
            dst_ref=recv_a.at[OPPOSITE[s], pl.ds(cols, modes)],
            send_sem=sa_sem.at[s],
            recv_sem=ra_sem.at[OPPOSITE[s]],
            device_id=place[s],
            device_id_type=MESH,
        )

    make_first = (first_back, first, first_back, first)
    for s in range(4):
        @pl.when(exists[s])
        def _(s=s):
            make_first[s](s).start()

    def column_copy(slot, di, shift):
        i2 = lax.rem(i + di, n_sy)
        return pltpu.make_async_remote_copy(
            src_ref=cinv_ref.at[pl.ds(pl.multiple_of((i2 + shift) * modes, 8), modes)],
            dst_ref=cinv_in.at[slot, i],
            send_sem=sc_sem.at[slot, i2],
            recv_sem=rc_sem.at[slot, i],
            device_id=(i2, j),
            device_id_type=MESH,
        )

    def column_send(act):
        for di in range(1, n_sy):
            i2 = lax.rem(i + di, n_sy)

            @pl.when(i2 > 0)
            def _(di=di):
                act(column_copy(0, di, -1))

            @pl.when(i2 < n_sy - 1)
            def _(di=di):
                act(column_copy(1, di, 1))

    def landed(slot, src):
        here = cinv_in.at[slot, src]
        pltpu.make_async_copy(here, here, rc_sem.at[slot, src]).wait()

    def row_copy(mate):
        return pltpu.make_async_remote_copy(
            src_ref=turned.at[pl.ds(pl.multiple_of(mate[1] * modes, 8), 3 * modes)],
            dst_ref=side_in.at[j],
            send_sem=ss_sem,
            recv_sem=rs_sem,
            device_id=mate,
            device_id_type=MESH,
        )

    def row_all():
        block = side_in.at[pl.ds(0, n_sx - 1)]
        return pltpu.make_async_remote_copy(
            src_ref=block,
            dst_ref=block,
            send_sem=ss_sem,
            recv_sem=rs_sem,
            device_id=row_mates[0],
            device_id_type=MESH,
        )

    column_send(lambda copy: copy.start())
    for mate in row_mates:
        row_copy(mate).start()
    side_in[j] = turned[pl.ds(pl.multiple_of(j * modes, 8), 3 * modes)]

    @pl.when(i > 0)
    def _():
        cinv_in[0, i] = cinv_ref[pl.ds(pl.multiple_of((i - 1) * modes, 8), modes)]

    @pl.when(i < n_sy - 1)
    def _():
        cinv_in[1, i] = cinv_ref[pl.ds(pl.multiple_of((i + 1) * modes, 8), modes)]

    for s in range(4):
        @pl.when(exists[OPPOSITE[s]])
        def _(s=s):
            make_first[s](s).wait_recv()
    masks = [None] * 4
    for a, s in ((0, 0), (1, 2)):
        start_side[s] = -recv_a[s, :cols]
        masks[s] = recv_a[s, cols + modes : cols + modes + 1]
        masks[s + 1] = own_mask[a]
    mask = jnp.concatenate(masks, axis=1)
    res = jnp.concatenate(start_side, axis=1)

    side_row = lax.broadcasted_iota(jnp.int32, (cols, halves * LANES), 0)
    side_lane = lax.broadcasted_iota(jnp.int32, (cols, halves * LANES), 1)
    on_col = jnp.where(lax.div(side_lane, modes) == side_row, 1.0, 0.0).astype(F32)
    bit_row = lax.broadcasted_iota(jnp.int32, (cols, LANES), 0)
    bit_lane = lax.broadcasted_iota(jnp.int32, (cols, LANES), 1)
    pick = jnp.where(lax.div(bit_lane, modes) == lax.rem(bit_row, groups), 1.0, 0.0).astype(F32)
    slot_of = lax.rem(lax.broadcasted_iota(jnp.int32, (1, LANES), 1), modes)
    in_half = lax.div(bit_row, groups)
    in_group = lax.rem(bit_row, groups)

    def to_row(column):
        return jnp.sum(column * on_col, axis=0, keepdims=True)

    def pack(rows):
        tile = jnp.zeros((1, LANES), F32)
        for v, row in enumerate(rows):
            for h in range(halves):
                tile = tile + jnp.where(slot_of == v * halves + h, row[:, h * LANES : (h + 1) * LANES], 0.0)
        return tile

    def unpack(phase, count):
        tile = jnp.sum(five_all[phase - 1, pl.ds(n_sx, n), 0, halves * wide :], axis=0, keepdims=True)
        columns = []
        for v in range(count):
            spot = jnp.where(bit_lane == in_group * modes + v * halves + in_half, 1.0, 0.0)
            columns.append(jnp.sum(tile * spot, axis=1, keepdims=True))
        return columns

    def send_all(src, dst, send_sem, recv_sem):
        def send(step, carry):
            o = n - step
            pltpu.make_async_remote_copy(
                src_ref=src,
                dst_ref=dst,
                send_sem=send_sem,
                recv_sem=recv_sem,
                device_id=device(o),
                device_id_type=MESH,
            ).start()
            return carry

        lax.fori_loop(1, n, send, 0)

    def all_of(block, send_sem, recv_sem):
        return pltpu.make_async_remote_copy(
            src_ref=block,
            dst_ref=block,
            send_sem=send_sem,
            recv_sem=recv_sem,
            device_id=device(1),
            device_id_type=MESH,
        )

    def all_coarse(phase):
        block = c_all.at[pl.ds(0, n - 1)] if phase == 0 else five_all.at[phase - 1, pl.ds(0, n - 1)]
        return all_of(block, sag_sem.at[phase], rag_sem.at[phase])

    def coarse_send(vec):
        product = dot3(vec, b8_hi[...], b8_lo[...]) * pick
        pieces = [
            jnp.sum(product[h * groups : (h + 1) * groups], axis=0, keepdims=True) for h in range(halves)
        ]
        message = jnp.concatenate(pieces, axis=1)
        c_send[...] = message
        c_all[me] = message
        pl.semaphore_wait(ready_sem, n_sx - 1)
        send_all(c_send, c_all.at[me], sag_sem.at[0], rag_sem.at[0])

    def five_send_all(phase, message):
        five_send[phase - 1] = message
        five_all[phase - 1, n_sx + me] = message
        send_all(
            five_send.at[phase - 1], five_all.at[phase - 1, n_sx + me], sag_sem.at[phase], rag_sem.at[phase]
        )

    unroll = 8
    shifts = (0, 1, -1, n_sx, -n_sx)

    def coarse_row(phase, d, h):
        if phase == 0:
            return c_all[d, :, h * LANES : (h + 1) * LANES]
        row = None
        for q, shift in enumerate(shifts):
            at = h * wide + q * LANES
            part = five_all[phase - 1, d + (n_sx + shift), :, at : at + LANES]
            row = part if row is None else row + part
        return row

    def coarse_take(phase):
        all_coarse(phase).wait_recv()

        def add(step, totals):
            totals = list(totals)
            for u in range(unroll):
                d = step * unroll + u
                rows = cr[d]
                for h in range(halves):
                    totals[h] = totals[h] + rows * coarse_row(phase, d, h)
            return tuple(totals)

        zero = jnp.zeros((five * modes, LANES), F32)
        return lax.fori_loop(0, n // unroll, add, (zero,) * halves)

    def weights_of(totals):
        gather = pick[:groups].astype(BF16)
        parts = []
        for total in totals:
            hi, lo = split(total)
            parts.append(dot_nt(gather, hi) + dot_nt(gather, lo))
        return jnp.concatenate(parts, axis=0)

    same_row = lax.broadcasted_iota(jnp.int32, (LANES, LANES), 0)
    same_lane = lax.broadcasted_iota(jnp.int32, (LANES, LANES), 1)
    same = (lax.div(same_row, modes) == lax.div(same_lane, modes)).astype(F32).astype(BF16)
    mode_row = lax.broadcasted_iota(jnp.int32, (modes, LANES), 0)
    mode_lane = lax.broadcasted_iota(jnp.int32, (modes, LANES), 1)
    on_mode = jnp.where(lax.rem(mode_lane, modes) == mode_row, 1.0, 0.0).astype(F32)
    repeat = on_col.astype(BF16)

    rows = five * modes

    def widened(blocks):
        sums = dot_exact(jnp.concatenate(blocks, axis=0), same)
        width = sums.shape[0] // halves
        return jnp.concatenate([sums[h * width : (h + 1) * width] for h in range(halves)], axis=1)

    def coupled(weights):
        hi, lo = split(weights)
        return dot3(coupling, hi, lo)

    def blocks_of(result):
        pieces = []
        for h in range(halves):
            for v in range(five):
                block = result[v * modes : (v + 1) * modes, h * LANES : (h + 1) * LANES]
                pieces.append(jnp.sum(block * on_mode, axis=0, keepdims=True))
        return pieces

    def column_sum(x, y):
        return jnp.sum(x * y, axis=0, keepdims=True)

    def swap(phase, s):
        return pltpu.make_async_remote_copy(
            src_ref=g_send.at[phase, s],
            dst_ref=g_recv.at[phase, OPPOSITE[s]],
            send_sem=sg_sem.at[phase, s],
            recv_sem=rg_sem.at[phase, OPPOSITE[s]],
            device_id=place[s],
            device_id_type=MESH,
        )

    def swap_start(phase, out):
        for s in range(4):
            g_send[phase, s] = out[:, s * pad : (s + 1) * pad]
        for s in range(4):
            @pl.when(exists[s])
            def _(s=s):
                swap(phase, s).start()

    def dual_take(phase, out):
        for s in range(4):
            @pl.when(exists[OPPOSITE[s]])
            def _(s=s):
                swap(phase, s).wait_recv()
        other = jnp.concatenate([g_recv[phase, s] for s in range(4)], axis=1)
        return (out - other) * mask

    def own_dot(x, y):
        total = x[:, pad : 2 * pad] * y[:, pad : 2 * pad] + x[:, 3 * pad :] * y[:, 3 * pad :]
        return jnp.sum(total, axis=1, keepdims=True)

    coarse_send(res)

    own_part = basis_side * mask
    lanes_at = lax.broadcasted_iota(jnp.int32, (modes, full), 1)
    blocks = [own_part]
    nbr = jnp.concatenate([recv_a[s, cols : cols + modes] for s in range(4)], axis=1) * mask
    for s in range(4):
        blocks.append(jnp.where(lax.div(lanes_at, pad) == s, -nbr, 0.0))
    basis_five = jnp.concatenate(blocks, axis=0)
    part_hi, part_lo = split(basis_five)
    bb_hi[...] = part_hi
    bb_lo[...] = part_lo

    flexed = flexed_of(jnp.concatenate([basis_five, res], axis=0))
    flexed_basis = flexed[:rows]
    flexed_res = flexed[rows:]
    part_hi, part_lo = split(flexed_basis)
    ka_hi[...] = part_hi
    ka_lo[...] = part_lo
    res_hi, res_lo = split(res)
    coupling = dot3_nt(flexed_basis, bb_hi[...], bb_lo[...])
    known = dot_exact(dot3_nt(jnp.concatenate([flexed_basis, own_part], axis=0), res_hi, res_lo), repeat)
    known0 = known[:rows]
    coarse0 = known[rows:]
    square = to_row(own_dot(res, res))
    bend = to_row(jnp.sum(res * flexed_res, axis=1, keepdims=True))
    for di in range(1, n_sy):
        src = lax.rem(i + di, n_sy)

        @pl.when(i > 0)
        def _(src=src):
            landed(0, src)

        @pl.when(i < n_sy - 1)
        def _(src=src):
            landed(1, src)

    group_of = lax.div(lax.broadcasted_iota(jnp.int32, (3 * modes, LANES), 1), modes)

    def widen(value, group):
        value = jnp.where(group_of[: value.shape[0]] == group, value, 0.0)
        shift = modes
        while shift < LANES:
            value = value + pltpu.roll(value, shift, 1)
            shift *= 2
        return value

    def widen_column(i2, carry):
        for j2 in range(n_sx):
            at = (j2 // groups) * LANES
            value = jnp.concatenate([cinv_in[v, i2, :, at : at + LANES] for v in range(2)], axis=0)
            cr[i2 * n_sx + j2, 3 * modes :] = widen(value, j2 % groups)
        return carry

    def widen_row(j2, carry):
        for i2 in range(n_sy):
            at = (i2 // groups) * LANES
            block = side_in[j2, :, at : at + LANES]
            block = jnp.concatenate([block[modes : 2 * modes], block[:modes], block[2 * modes :]], axis=0)
            cr[i2 * n_sx + j2, : 3 * modes] = widen(block, i2 % groups)
        return carry

    lax.fori_loop(0, n_sy, widen_column, 0)
    row_all().wait_recv()
    lax.fori_loop(0, n_sx, widen_row, 0)

    totals = coarse_take(0)
    weights0 = widened(totals)
    result0 = coupled(weights0) + known0
    norm_row = square + column_sum(coarse0, weights0[:modes])
    curve_row = bend + column_sum(weights0, result0 + known0)
    five_send_all(1, jnp.concatenate(blocks_of(result0) + [pack([norm_row, curve_row])], axis=1))
    weights = weights_of(totals)
    out0 = flexed_res + dot3(weights, ka_hi[...], ka_lo[...])
    swap_start(0, out0)
    cor0 = res + dot3(weights, bb_hi[...], bb_lo[...])
    image0 = dual_take(0, out0)
    flexed_image = flexed_of(image0)
    image_hi, image_lo = split(image0)
    known1 = dot_exact(dot3_nt(flexed_basis, image_hi, image_lo), repeat)

    totals = coarse_take(1)
    own_rows = [coarse_row(1, me, h) * on_mode for h in range(halves)]
    sides = []
    for h in range(halves):
        sides += [totals[h], own_rows[h]]
    sides = widened(sides)
    weights1 = sides[:rows]
    coarse1 = sides[rows:]
    result1 = coupled(weights1) + known1
    norm0, curve0 = unpack(1, 2)
    step0 = norm0 / curve0
    step_row = to_row(step0)
    res1 = res - step0 * image0
    flexed_res1 = flexed_res - step0 * flexed_image
    square = to_row(own_dot(res1, res1))
    bend = to_row(jnp.sum(res1 * flexed_res1, axis=1, keepdims=True))
    change = weights0 - step_row * weights1
    norm_row = square + column_sum(coarse0 - step_row * coarse1, change[:modes])
    curve_row = bend + column_sum(change, (result0 + known0) - step_row * (result1 + known1))
    five_send_all(2, jnp.concatenate(blocks_of(result1) + [pack([norm_row, curve_row])], axis=1))
    weights = weights_of(totals)
    out1 = flexed_image + dot3(weights, ka_hi[...], ka_lo[...])
    swap_start(1, out1)
    pre_image0 = image0 + dot3(weights, bb_hi[...], bb_lo[...])
    cor1 = cor0 - step0 * pre_image0
    image1 = dual_take(1, out1)

    totals = coarse_take(2)
    norm1, curve1 = unpack(2, 2)
    beta = norm1 / norm0
    step1 = norm1 / (curve1 - beta * beta * curve0)
    total = step0 * cor0 + step1 * (cor1 + beta * cor0)
    near = cor1 - step1 * ((1.0 + beta) * pre_image0 - step0 * image1)
    weights = weights_of(totals)
    cor2 = near + (step1 * step0) * dot3(weights, bb_hi[...], bb_lo[...])
    for a in range(2):
        at = (2 * a + 1) * pad
        both_ref[0, a] = total[:, at : at + side] * signs[a]
        both_ref[1, a] = cor2[:, at : at + side] * signs[a]

    for s in range(4):
        @pl.when(exists[s])
        def _(s=s):
            make_first[s](s).wait_send()
            swap(0, s).wait_send()
            swap(1, s).wait_send()
    column_send(lambda copy: copy.wait_send())
    row_all().wait_send()
    for phase in range(3):
        all_coarse(phase).wait_send()


def lay_out(both_ref, mult_ref, prec_ref):
    for a in range(2):
        mult_ref[a, :, 0, :] = both_ref[0, a]
        prec_ref[a, :, 0, :] = both_ref[1, a]


def per_device(n_sy, n_sx, loads, flex, basis, coarse_inv, pair_size, owner, trace_slot):
    cols, side = loads.shape[1], loads.shape[3]
    modes, traces = basis.shape[2], basis.shape[3]
    pad = side
    full = 4 * pad
    n = n_sy * n_sx
    width = cols * modes
    turned_width = pl.cdiv(coarse_inv.shape[0], LANES) * LANES
    dma = pltpu.SemaphoreType.DMA
    vmem = pl.BlockSpec(memory_space=pltpu.VMEM)
    both = pl.pallas_call(
        functools.partial(kernel, n_sy, n_sx, side, pad),
        out_shape=jax.ShapeDtypeStruct((2, 2, cols, side), F32),
        in_specs=[pl.BlockSpec(memory_space=pl.ANY)] * 7,
        out_specs=vmem,
        scratch_shapes=[
            pltpu.VMEM(loads.shape, F32),
            pltpu.VMEM(basis.shape, F32),
            pltpu.VMEM(coarse_inv.shape, F32),
            pltpu.SMEM((1, 1, 2), jnp.int32),
            pltpu.SMEM((1, 1, 2), jnp.int32),
            pltpu.VMEM(trace_slot.shape, jnp.int32),
            pltpu.VMEM((traces, traces), F32),
            pltpu.VMEM((traces, traces), BF16),
            pltpu.VMEM((traces, traces), BF16),
            pltpu.VMEM((full, traces), BF16),
            pltpu.VMEM((traces, full), BF16),
            pltpu.VMEM((8, full), jnp.int32),
            pltpu.VMEM((full, 8), jnp.int32),
            pltpu.VMEM((full, LANES), BF16),
            pltpu.VMEM((full, LANES), BF16),
            pltpu.VMEM((5 * modes, full), BF16),
            pltpu.VMEM((5 * modes, full), BF16),
            pltpu.VMEM((5 * modes, full), BF16),
            pltpu.VMEM((5 * modes, full), BF16),
            pltpu.VMEM((2, cols, pad), F32),
            pltpu.VMEM((4, cols + modes + 8, pad), F32),
            pltpu.VMEM((4, cols + modes + 8, pad), F32),
            pltpu.VMEM((2, n_sy, modes, coarse_inv.shape[1]), F32),
            pltpu.VMEM(((n_sx + 2) * modes, turned_width), F32),
            pltpu.VMEM((n_sx, 3 * modes, turned_width), F32),
            pltpu.VMEM((n, 5 * modes, LANES), F32),
            pltpu.VMEM((2, 4, cols, pad), F32),
            pltpu.VMEM((2, 4, cols, pad), F32),
            pltpu.VMEM((1, width), F32),
            pltpu.VMEM((n, 1, width), F32),
            pltpu.VMEM((2, 1, 5 * width + LANES), F32),
            pltpu.VMEM((2, n + 2 * n_sx, 1, 5 * width + LANES), F32),
            pltpu.SemaphoreType.REGULAR,
            dma,
            dma((6,)),
            dma((4,)),
            dma((4,)),
            dma((2, n_sy)),
            dma((2, n_sy)),
            dma,
            dma,
            dma((2, 4)),
            dma((2, 4)),
            dma((3,)),
            dma((3,)),
        ],
        compiler_params=pltpu.CompilerParams(
            collective_id=0, has_side_effects=True, vmem_limit_bytes=60 * 1024 * 1024
        ),
    )(
        loads, flex, basis, coarse_inv,
        jnp.transpose(pair_size, (1, 2, 0)), jnp.transpose(owner, (1, 2, 0)), trace_slot,
    )

    out = jax.ShapeDtypeStruct(loads.shape, F32)
    return pl.pallas_call(
        lay_out, out_shape=(out, out), in_specs=[vmem], out_specs=(vmem, vmem)
    )(both)


def solution(mesh):
    return jax.shard_map(
        functools.partial(per_device, mesh.shape["sy"], mesh.shape["sx"]),
        mesh=mesh,
        in_specs=(
            P(None, None, "sy", "sx"),
            P("sy", "sx", None, None),
            P("sy", "sx", None, None),
            P("sx", "sy"),
            P(None, "sy", "sx"),
            P(None, "sy", "sx"),
            P(None, "sy", "sx"),
        ),
        out_specs=(P(None, None, "sy", "sx"), P(None, None, "sy", "sx")),
        check_vma=False,
    )
```

```python
import functools

import jax
import jax.numpy as jnp
from jax import lax
from jax.experimental import pallas as pl
from jax.experimental.pallas import tpu as pltpu
from jax.sharding import PartitionSpec as P

LANES = 128
MESH = pl.DeviceIdType.MESH
OPPOSITE = (1, 0, 3, 2)
F32 = jnp.float32
BF16 = jnp.bfloat16


def dot(a, b):
    return jnp.dot(a, b, preferred_element_type=F32)


def dot_nt(a, b):
    return lax.dot_general(a, b, (((1,), (1,)), ((), ())), preferred_element_type=F32)


def split(x):
    hi = x.astype(BF16)
    return hi, (x - hi.astype(F32)).astype(BF16)


def dot3_nt(x, w_hi, w_lo):
    rows = x.shape[0]
    hi, lo = split(x)
    both = dot_nt(jnp.concatenate([hi, lo], axis=0), w_hi)
    return both[:rows] + both[rows:] + dot_nt(hi, w_lo)


def dot_exact(x, ones):
    rows = x.shape[0]
    both = dot(jnp.concatenate(split(x), axis=0), ones)
    return both[:rows] + both[rows:]


def dot3(x, w_hi, w_lo):
    rows = x.shape[0]
    hi, lo = split(x)
    both = dot(jnp.concatenate([hi, lo], axis=0), w_hi)
    return both[:rows] + both[rows:] + dot(hi, w_lo)


def kernel(
    n_sy, n_sx, side, pad,
    loads_in, flex_in, basis_in, cinv_own, size_in, owner_in, slot_in,
    both_ref,
    loads_ref, basis_ref, cinv_ref, size_ref, owner_ref, slot_ref,
    flex_v, q, q_t, slot_row, slot_col, a_hi, a_lo,
    b8_hi, b8_lo, bb_hi, bb_lo, ka_hi, ka_lo, loads_s, send_a, recv_a, cinv_in, turned, side_in, cr,
    g_send, g_recv, c_send, c_all, five_send, five_all,
    ready_sem, flex_sem, in_sem, sa_sem, ra_sem, sc_sem, rc_sem, ss_sem, rs_sem, sg_sem, rg_sem,
    sag_sem, rag_sem,
):
    cols = loads_ref.shape[1]
    modes = basis_ref.shape[2]
    traces = flex_v.shape[0]
    full = 4 * pad
    groups = LANES // modes
    halves = cols // groups
    n = n_sy * n_sx
    i = lax.axis_index("sy")
    j = lax.axis_index("sx")
    me = i * n_sx + j
    exists = (j > 0, j < n_sx - 1, i > 0, i < n_sy - 1)
    place = ((i, j - 1), (i, j + 1), (i - 1, j), (i + 1, j))

    barrier = pltpu.get_barrier_semaphore()
    row_mates = [(i, lax.rem(j + o, n_sx)) for o in range(1, n_sx)]
    column_mates = [(lax.rem(i + o, n_sy), j) for o in range(1, n_sy)]
    for mate in row_mates + column_mates:
        pl.semaphore_signal(barrier, inc=1, device_id=mate, device_id_type=MESH)

    fetches = [
        pltpu.make_async_copy(src, dst, in_sem.at[q])
        for q, (src, dst) in enumerate(
            (
                (slot_in, slot_ref), (basis_in, basis_ref), (cinv_own, cinv_ref), (loads_in, loads_ref),
                (size_in, size_ref), (owner_in, owner_ref),
            )
        )
    ]
    for fetch in fetches:
        fetch.start()
    flex_copy = pltpu.make_async_copy(flex_in.at[0, 0], flex_v, flex_sem)
    flex_copy.start()
    for s in range(4):
        @pl.when(jnp.logical_not(exists[s]))
        def _(s=s):
            recv_a[s] = jnp.zeros(recv_a.shape[1:], F32)
            for phase in range(2):
                g_recv[phase, s] = jnp.zeros(g_recv.shape[2:], F32)
            if s >= 2:
                cinv_in[s - 2] = jnp.zeros(cinv_in.shape[1:], F32)

    turned[...] = jnp.zeros_like(turned)
    five = 1 + len(exists)
    wide = five * LANES
    def shifted(at, o, size):
        return lax.bitwise_xor(at, o) if size & (size - 1) == 0 else lax.rem(at + o, size)

    def device(o):
        return (shifted(i, lax.rem(o, n_sy), n_sy), shifted(j, lax.div(o, n_sy), n_sx))

    for fetch in fetches:
        fetch.wait()
    slot_row[...] = jnp.full_like(slot_row, -1)
    for s in range(4):
        slot_row[:, s * pad : s * pad + side] = jnp.broadcast_to(slot_ref[s], (8, side))
    trace_id = lax.broadcasted_iota(jnp.int32, (traces, full), 0)
    q_t[...] = (trace_id == slot_row[0:1, :]).astype(F32).astype(BF16)

    basis_hi, basis_lo = split(basis_ref[0, 0])
    both = dot(jnp.concatenate([basis_hi, basis_lo], axis=0), q_t[...])
    basis_side = both[:modes] + both[modes:]

    lane = lax.broadcasted_iota(jnp.int32, (1, pad), 1)
    signs = [(1 - 2 * owner_ref[0, 0, a]).astype(F32) for a in range(2)]
    own_mask = [jnp.where(lane < size_ref[0, 0, a], 1.0, 0.0).astype(F32) for a in range(2)]
    loads_s[...] = jnp.zeros_like(loads_s)
    for a in range(2):
        loads_s[a, :, :side] = loads_ref[a, :, 0, :]
    for s in range(4):
        send_a[s, cols : cols + modes] = basis_side[:, s * pad : (s + 1) * pad]
    start_side = [None] * 4
    for a, s in ((0, 1), (1, 3)):
        start_side[s] = loads_s[a] * (own_mask[a] * signs[a])
        send_a[s, :cols] = start_side[s]
        send_a[s, cols + modes :] = jnp.broadcast_to(own_mask[a], (8, pad))

    pl.semaphore_wait(barrier, n_sx + n_sy - 2)
    for mate in row_mates:
        pl.semaphore_signal(ready_sem, inc=1, device_id=mate, device_id_type=MESH)

    def first(s):
        return pltpu.make_async_remote_copy(
            src_ref=send_a.at[s],
            dst_ref=recv_a.at[OPPOSITE[s]],
            send_sem=sa_sem.at[s],
            recv_sem=ra_sem.at[OPPOSITE[s]],
            device_id=place[s],
            device_id_type=MESH,
        )

    def first_back(s):
        return pltpu.make_async_remote_copy(
            src_ref=send_a.at[s, pl.ds(cols, modes)],
            dst_ref=recv_a.at[OPPOSITE[s], pl.ds(cols, modes)],
            send_sem=sa_sem.at[s],
            recv_sem=ra_sem.at[OPPOSITE[s]],
            device_id=place[s],
            device_id_type=MESH,
        )

    make_first = (first_back, first, first_back, first)
    for s in range(4):
        @pl.when(exists[s])
        def _(s=s):
            make_first[s](s).start()

    def column_copy(slot, di, shift):
        i2 = lax.rem(i + di, n_sy)
        return pltpu.make_async_remote_copy(
            src_ref=cinv_ref.at[pl.ds(pl.multiple_of((i2 + shift) * modes, 8), modes)],
            dst_ref=cinv_in.at[slot, i],
            send_sem=sc_sem.at[slot, i2],
            recv_sem=rc_sem.at[slot, i],
            device_id=(i2, j),
            device_id_type=MESH,
        )

    def column_send(act):
        for di in range(1, n_sy):
            i2 = lax.rem(i + di, n_sy)

            @pl.when(i2 > 0)
            def _(di=di):
                act(column_copy(0, di, -1))

            @pl.when(i2 < n_sy - 1)
            def _(di=di):
                act(column_copy(1, di, 1))

    def landed(slot, src):
        here = cinv_in.at[slot, src]
        pltpu.make_async_copy(here, here, rc_sem.at[slot, src]).wait()

    def row_copy(mate):
        return pltpu.make_async_remote_copy(
            src_ref=turned.at[pl.ds(pl.multiple_of(mate[1] * modes, 8), 3 * modes)],
            dst_ref=side_in.at[j],
            send_sem=ss_sem,
            recv_sem=rs_sem,
            device_id=mate,
            device_id_type=MESH,
        )

    def row_all():
        block = side_in.at[pl.ds(0, n_sx - 1)]
        return pltpu.make_async_remote_copy(
            src_ref=block,
            dst_ref=block,
            send_sem=ss_sem,
            recv_sem=rs_sem,
            device_id=row_mates[0],
            device_id_type=MESH,
        )

    column_send(lambda copy: copy.start())
    turned[modes : (n_sx + 1) * modes, : n_sy * modes] = jnp.transpose(cinv_ref[...])

    for mate in row_mates:
        row_copy(mate).start()
    side_in[j] = turned[pl.ds(pl.multiple_of(j * modes, 8), 3 * modes)]

    @pl.when(i > 0)
    def _():
        cinv_in[0, i] = cinv_ref[pl.ds(pl.multiple_of((i - 1) * modes, 8), modes)]

    @pl.when(i < n_sy - 1)
    def _():
        cinv_in[1, i] = cinv_ref[pl.ds(pl.multiple_of((i + 1) * modes, 8), modes)]

    b8 = jnp.transpose(jnp.concatenate([basis_side] * groups, axis=0))
    part_hi, part_lo = split(b8)
    b8_hi[...] = part_hi
    b8_lo[...] = part_lo

    for phase in range(2):
        edge = jnp.zeros((n_sx, 1, halves * wide + LANES), F32)
        five_all[phase, pl.ds(0, n_sx)] = edge
        five_all[phase, pl.ds(n_sx + n, n_sx)] = edge

    slot_col[...] = jnp.transpose(slot_row[...].astype(F32)).astype(jnp.int32)
    slot_id = lax.broadcasted_iota(jnp.int32, (full, traces), 1)
    q[...] = (slot_id == slot_col[:, 0:1]).astype(F32).astype(BF16)

    flex_copy.wait()

    chunks = 3
    chunk = traces // chunks

    def permute(step, carry):
        at = pl.ds(pl.multiple_of(step * chunk, chunk), chunk)
        both = dot(jnp.concatenate(split(flex_v[at, :]), axis=0), q_t[...]).astype(BF16)
        a_hi[at, :] = both[:chunk]
        a_lo[at, :] = both[chunk:]
        return carry

    def flexed_of(vec):
        rows = vec.shape[0]
        traced = dot(jnp.concatenate(split(vec), axis=0), q[...]).astype(BF16)
        both = dot(traced, a_hi[...])
        return both[:rows] + both[rows:] + dot(traced[:rows], a_lo[...])

    lax.fori_loop(0, chunks, permute, 0)

    for s in range(4):
        @pl.when(exists[OPPOSITE[s]])
        def _(s=s):
            make_first[s](s).wait_recv()
    masks = [None] * 4
    for a, s in ((0, 0), (1, 2)):
        start_side[s] = -recv_a[s, :cols]
        masks[s] = recv_a[s, cols + modes : cols + modes + 1]
        masks[s + 1] = own_mask[a]
    mask = jnp.concatenate(masks, axis=1)
    res = jnp.concatenate(start_side, axis=1)

    side_row = lax.broadcasted_iota(jnp.int32, (cols, halves * LANES), 0)
    side_lane = lax.broadcasted_iota(jnp.int32, (cols, halves * LANES), 1)
    on_col = jnp.where(lax.div(side_lane, modes) == side_row, 1.0, 0.0).astype(F32)
    bit_row = lax.broadcasted_iota(jnp.int32, (cols, LANES), 0)
    bit_lane = lax.broadcasted_iota(jnp.int32, (cols, LANES), 1)
    pick = jnp.where(lax.div(bit_lane, modes) == lax.rem(bit_row, groups), 1.0, 0.0).astype(F32)
    slot_of = lax.rem(lax.broadcasted_iota(jnp.int32, (1, LANES), 1), modes)
    in_half = lax.div(bit_row, groups)
    in_group = lax.rem(bit_row, groups)

    def to_row(column):
        return jnp.sum(column * on_col, axis=0, keepdims=True)

    def pack(rows):
        tile = jnp.zeros((1, LANES), F32)
        for v, row in enumerate(rows):
            for h in range(halves):
                tile = tile + jnp.where(slot_of == v * halves + h, row[:, h * LANES : (h + 1) * LANES], 0.0)
        return tile

    def unpack(phase, count):
        tile = jnp.sum(five_all[phase - 1, pl.ds(n_sx, n), 0, halves * wide :], axis=0, keepdims=True)
        columns = []
        for v in range(count):
            spot = jnp.where(bit_lane == in_group * modes + v * halves + in_half, 1.0, 0.0)
            columns.append(jnp.sum(tile * spot, axis=1, keepdims=True))
        return columns

    def send_all(src, dst, send_sem, recv_sem):
        def send(step, carry):
            o = n - step
            pltpu.make_async_remote_copy(
                src_ref=src,
                dst_ref=dst,
                send_sem=send_sem,
                recv_sem=recv_sem,
                device_id=device(o),
                device_id_type=MESH,
            ).start()
            return carry

        lax.fori_loop(1, n, send, 0)

    def all_of(block, send_sem, recv_sem):
        return pltpu.make_async_remote_copy(
            src_ref=block,
            dst_ref=block,
            send_sem=send_sem,
            recv_sem=recv_sem,
            device_id=device(1),
            device_id_type=MESH,
        )

    def all_coarse(phase):
        block = c_all.at[pl.ds(0, n - 1)] if phase == 0 else five_all.at[phase - 1, pl.ds(0, n - 1)]
        return all_of(block, sag_sem.at[phase], rag_sem.at[phase])

    def coarse_send(vec):
        product = dot3(vec, b8_hi[...], b8_lo[...]) * pick
        pieces = [
            jnp.sum(product[h * groups : (h + 1) * groups], axis=0, keepdims=True) for h in range(halves)
        ]
        message = jnp.concatenate(pieces, axis=1)
        c_send[...] = message
        c_all[me] = message
        pl.semaphore_wait(ready_sem, n_sx - 1)
        send_all(c_send, c_all.at[me], sag_sem.at[0], rag_sem.at[0])

    def five_send_all(phase, message):
        five_send[phase - 1] = message
        five_all[phase - 1, n_sx + me] = message
        send_all(
            five_send.at[phase - 1], five_all.at[phase - 1, n_sx + me], sag_sem.at[phase], rag_sem.at[phase]
        )

    unroll = 8
    shifts = (1, 0, -1, n_sx, -n_sx)

    def coarse_row(phase, d, h):
        if phase == 0:
            return c_all[d, :, h * LANES : (h + 1) * LANES]
        row = None
        for q, shift in enumerate(shifts):
            at = h * wide + q * LANES
            part = five_all[phase - 1, d + (n_sx + shift), :, at : at + LANES]
            row = part if row is None else row + part
        return row

    def coarse_take(phase):
        all_coarse(phase).wait_recv()

        def add(step, totals):
            totals = list(totals)
            for u in range(unroll):
                d = step * unroll + u
                rows = cr[d]
                for h in range(halves):
                    totals[h] = totals[h] + rows * coarse_row(phase, d, h)
            return tuple(totals)

        zero = jnp.zeros((five * modes, LANES), F32)
        return lax.fori_loop(0, n // unroll, add, (zero,) * halves)

    def weights_of(totals):
        gather = pick[:groups].astype(BF16)
        parts = []
        for total in totals:
            hi, lo = split(total)
            parts.append(dot_nt(gather, hi) + dot_nt(gather, lo))
        return jnp.concatenate(parts, axis=0)

    same_row = lax.broadcasted_iota(jnp.int32, (LANES, LANES), 0)
    same_lane = lax.broadcasted_iota(jnp.int32, (LANES, LANES), 1)
    same = (lax.div(same_row, modes) == lax.div(same_lane, modes)).astype(F32).astype(BF16)
    mode_row = lax.broadcasted_iota(jnp.int32, (modes, LANES), 0)
    mode_lane = lax.broadcasted_iota(jnp.int32, (modes, LANES), 1)
    on_mode = jnp.where(lax.rem(mode_lane, modes) == mode_row, 1.0, 0.0).astype(F32)
    repeat = on_col.astype(BF16)

    rows = five * modes

    def widened(blocks):
        sums = dot_exact(jnp.concatenate(blocks, axis=0), same)
        width = sums.shape[0] // halves
        return jnp.concatenate([sums[h * width : (h + 1) * width] for h in range(halves)], axis=1)

    def coupled(weights):
        hi, lo = split(weights)
        return dot3(coupling, hi, lo)

    def blocks_of(result):
        pieces = []
        for h in range(halves):
            for v in range(five):
                block = result[v * modes : (v + 1) * modes, h * LANES : (h + 1) * LANES]
                pieces.append(jnp.sum(block * on_mode, axis=0, keepdims=True))
        return pieces

    def column_sum(x, y):
        return jnp.sum(x * y, axis=0, keepdims=True)

    def swap(phase, s):
        return pltpu.make_async_remote_copy(
            src_ref=g_send.at[phase, s],
            dst_ref=g_recv.at[phase, OPPOSITE[s]],
            send_sem=sg_sem.at[phase, s],
            recv_sem=rg_sem.at[phase, OPPOSITE[s]],
            device_id=place[s],
            device_id_type=MESH,
        )

    def swap_start(phase, out):
        for s in range(4):
            g_send[phase, s] = out[:, s * pad : (s + 1) * pad]
        for s in range(4):
            @pl.when(exists[s])
            def _(s=s):
                swap(phase, s).start()

    def dual_take(phase, out):
        for s in range(4):
            @pl.when(exists[OPPOSITE[s]])
            def _(s=s):
                swap(phase, s).wait_recv()
        other = jnp.concatenate([g_recv[phase, s] for s in range(4)], axis=1)
        return (out - other) * mask

    def own_dot(x, y):
        total = x[:, pad : 2 * pad] * y[:, pad : 2 * pad] + x[:, 3 * pad :] * y[:, 3 * pad :]
        return jnp.sum(total, axis=1, keepdims=True)

    coarse_send(res)

    own_part = basis_side * mask
    lanes_at = lax.broadcasted_iota(jnp.int32, (modes, full), 1)
    nbr = jnp.concatenate([recv_a[s, cols : cols + modes] for s in range(4)], axis=1) * mask
    blocks = [jnp.where(lax.div(lanes_at, pad) == s, -nbr, 0.0) for s in range(4)]
    blocks.insert(1, own_part)
    basis_five = jnp.concatenate(blocks, axis=0)
    part_hi, part_lo = split(basis_five)
    bb_hi[...] = part_hi
    bb_lo[...] = part_lo

    flexed = flexed_of(jnp.concatenate([basis_five, res], axis=0))
    flexed_basis = flexed[:rows]
    flexed_res = flexed[rows:]
    part_hi, part_lo = split(flexed_basis)
    ka_hi[...] = part_hi
    ka_lo[...] = part_lo
    res_hi, res_lo = split(res)
    coupling = dot3_nt(flexed_basis, bb_hi[...], bb_lo[...])
    known = dot_exact(dot3_nt(jnp.concatenate([flexed_basis, own_part], axis=0), res_hi, res_lo), repeat)
    known0 = known[:rows]
    coarse0 = known[rows:]
    square = to_row(own_dot(res, res))
    bend = to_row(jnp.sum(res * flexed_res, axis=1, keepdims=True))
    for di in range(1, n_sy):
        src = lax.rem(i + di, n_sy)

        @pl.when(i > 0)
        def _(src=src):
            landed(0, src)

        @pl.when(i < n_sy - 1)
        def _(src=src):
            landed(1, src)

    pick_row = lax.broadcasted_iota(jnp.int32, (LANES, LANES), 0)
    pick_lane = lax.broadcasted_iota(jnp.int32, (LANES, LANES), 1)

    def widen(block, group):
        at = (group // groups) * LANES
        chosen = pick_row == group % groups * modes + lax.rem(pick_lane, modes)
        value = block[..., at : at + LANES]
        wide_value = dot_exact(value.reshape(-1, LANES), chosen.astype(F32).astype(BF16))
        return wide_value.reshape(value.shape)

    for j2 in range(n_sx):
        block = widen(cinv_in[...], j2)
        for i2 in range(n_sy):
            for v in range(2):
                cr[i2 * n_sx + j2, (3 + v) * modes : (4 + v) * modes] = block[v, i2]
    row_all().wait_recv()
    for i2 in range(n_sy):
        cr[i2 * n_sx : (i2 + 1) * n_sx, : 3 * modes] = widen(side_in[...], i2)

    totals = coarse_take(0)
    weights0 = widened(totals)
    result0 = coupled(weights0) + known0
    norm_row = square + column_sum(coarse0, weights0[modes : 2 * modes])
    curve_row = bend + column_sum(weights0, result0 + known0)
    five_send_all(1, jnp.concatenate(blocks_of(result0) + [pack([norm_row, curve_row])], axis=1))
    weights = weights_of(totals)
    out0 = flexed_res + dot3(weights, ka_hi[...], ka_lo[...])
    swap_start(0, out0)
    cor0 = res + dot3(weights, bb_hi[...], bb_lo[...])
    image0 = dual_take(0, out0)
    image_hi, image_lo = split(image0)
    known1 = dot_exact(dot3_nt(flexed_basis, image_hi, image_lo), repeat)
    flexed_image = flexed_of(image0)

    totals = coarse_take(1)
    own_rows = [coarse_row(1, me, h) * on_mode for h in range(halves)]
    sides = []
    for h in range(halves):
        sides += [totals[h], own_rows[h]]
    sides = widened(sides)
    weights1 = sides[:rows]
    coarse1 = sides[rows:]
    result1 = coupled(weights1) + known1
    norm0, curve0 = unpack(1, 2)
    step0 = norm0 / curve0
    step_row = to_row(step0)
    res1 = res - step0 * image0
    flexed_res1 = flexed_res - step0 * flexed_image
    square = to_row(own_dot(res1, res1))
    bend = to_row(jnp.sum(res1 * flexed_res1, axis=1, keepdims=True))
    change = weights0 - step_row * weights1
    norm_row = square + column_sum(coarse0 - step_row * coarse1, change[modes : 2 * modes])
    curve_row = bend + column_sum(change, (result0 + known0) - step_row * (result1 + known1))
    five_send_all(2, jnp.concatenate(blocks_of(result1) + [pack([norm_row, curve_row])], axis=1))
    weights = weights_of(totals)
    out1 = flexed_image + dot3(weights, ka_hi[...], ka_lo[...])
    swap_start(1, out1)
    pre_image0 = image0 + dot3(weights, bb_hi[...], bb_lo[...])
    cor1 = cor0 - step0 * pre_image0
    image1 = dual_take(1, out1)

    totals = coarse_take(2)
    norm1, curve1 = unpack(2, 2)
    beta = norm1 / norm0
    step1 = norm1 / (curve1 - beta * beta * curve0)
    total = step0 * cor0 + step1 * (cor1 + beta * cor0)
    near = cor1 - step1 * ((1.0 + beta) * pre_image0 - step0 * image1)
    weights = weights_of(totals)
    cor2 = near + (step1 * step0) * dot3(weights, bb_hi[...], bb_lo[...])
    for a in range(2):
        at = (2 * a + 1) * pad
        both_ref[0, a] = total[:, at : at + side] * signs[a]
        both_ref[1, a] = cor2[:, at : at + side] * signs[a]

    for s in range(4):
        @pl.when(exists[s])
        def _(s=s):
            make_first[s](s).wait_send()
            swap(0, s).wait_send()
            swap(1, s).wait_send()
    column_send(lambda copy: copy.wait_send())
    row_all().wait_send()
    for phase in range(3):
        all_coarse(phase).wait_send()


def lay_out(both_ref, mult_ref, prec_ref):
    for a in range(2):
        mult_ref[a, :, 0, :] = both_ref[0, a]
        prec_ref[a, :, 0, :] = both_ref[1, a]


def per_device(n_sy, n_sx, loads, flex, basis, coarse_inv, pair_size, owner, trace_slot):
    cols, side = loads.shape[1], loads.shape[3]
    modes, traces = basis.shape[2], basis.shape[3]
    pad = side
    full = 4 * pad
    n = n_sy * n_sx
    width = cols * modes
    turned_width = pl.cdiv(coarse_inv.shape[0], LANES) * LANES
    dma = pltpu.SemaphoreType.DMA
    vmem = pl.BlockSpec(memory_space=pltpu.VMEM)
    both = pl.pallas_call(
        functools.partial(kernel, n_sy, n_sx, side, pad),
        out_shape=pltpu.VMEM((2, 2, cols, side), F32),
        in_specs=[pl.BlockSpec(memory_space=pl.ANY)] * 7,
        out_specs=vmem,
        scratch_shapes=[
            pltpu.VMEM(loads.shape, F32),
            pltpu.VMEM(basis.shape, F32),
            pltpu.VMEM(coarse_inv.shape, F32),
            pltpu.SMEM((1, 1, 2), jnp.int32),
            pltpu.SMEM((1, 1, 2), jnp.int32),
            pltpu.VMEM(trace_slot.shape, jnp.int32),
            pltpu.VMEM((traces, traces), F32),
            pltpu.VMEM((full, traces), BF16),
            pltpu.VMEM((traces, full), BF16),
            pltpu.VMEM((8, full), jnp.int32),
            pltpu.VMEM((full, 8), jnp.int32),
            pltpu.VMEM((traces, full), BF16),
            pltpu.VMEM((traces, full), BF16),
            pltpu.VMEM((full, LANES), BF16),
            pltpu.VMEM((full, LANES), BF16),
            pltpu.VMEM((5 * modes, full), BF16),
            pltpu.VMEM((5 * modes, full), BF16),
            pltpu.VMEM((5 * modes, full), BF16),
            pltpu.VMEM((5 * modes, full), BF16),
            pltpu.VMEM((2, cols, pad), F32),
            pltpu.VMEM((4, cols + modes + 8, pad), F32),
            pltpu.VMEM((4, cols + modes + 8, pad), F32),
            pltpu.VMEM((2, n_sy, modes, coarse_inv.shape[1]), F32),
            pltpu.VMEM(((n_sx + 2) * modes, turned_width), F32),
            pltpu.VMEM((n_sx, 3 * modes, turned_width), F32),
            pltpu.VMEM((n, 5 * modes, LANES), F32),
            pltpu.VMEM((2, 4, cols, pad), F32),
            pltpu.VMEM((2, 4, cols, pad), F32),
            pltpu.VMEM((1, width), F32),
            pltpu.VMEM((n, 1, width), F32),
            pltpu.VMEM((2, 1, 5 * width + LANES), F32),
            pltpu.VMEM((2, n + 2 * n_sx, 1, 5 * width + LANES), F32),
            pltpu.SemaphoreType.REGULAR,
            dma,
            dma((6,)),
            dma((4,)),
            dma((4,)),
            dma((2, n_sy)),
            dma((2, n_sy)),
            dma,
            dma,
            dma((2, 4)),
            dma((2, 4)),
            dma((3,)),
            dma((3,)),
        ],
        compiler_params=pltpu.CompilerParams(
            collective_id=0, has_side_effects=True, vmem_limit_bytes=60 * 1024 * 1024
        ),
    )(
        loads, flex, basis, coarse_inv,
        jnp.transpose(pair_size, (1, 2, 0)), jnp.transpose(owner, (1, 2, 0)), trace_slot,
    )

    out = jax.ShapeDtypeStruct(loads.shape, F32)
    return pl.pallas_call(
        lay_out, out_shape=(out, out), in_specs=[vmem], out_specs=(vmem, vmem)
    )(pltpu.with_memory_space_constraint(both, pltpu.VMEM))


def solution(mesh):
    return jax.shard_map(
        functools.partial(per_device, mesh.shape["sy"], mesh.shape["sx"]),
        mesh=mesh,
        in_specs=(
            P(None, None, "sy", "sx"),
            P("sy", "sx", None, None),
            P("sy", "sx", None, None),
            P("sx", "sy"),
            P(None, "sy", "sx"),
            P(None, "sy", "sx"),
            P(None, "sy", "sx"),
        ),
        out_specs=(P(None, None, "sy", "sx"), P(None, None, "sy", "sx")),
        check_vma=False,
    )
```

```python
import functools

import jax
import jax.numpy as jnp
from jax import lax
from jax.experimental import pallas as pl
from jax.experimental.pallas import tpu as pltpu
from jax.sharding import PartitionSpec as P

LANES = 128
MESH = pl.DeviceIdType.MESH
OPPOSITE = (1, 0, 3, 2)
F32 = jnp.float32
BF16 = jnp.bfloat16


def dot(a, b):
    return jnp.dot(a, b, preferred_element_type=F32)


def dot_nt(a, b):
    return lax.dot_general(a, b, (((1,), (1,)), ((), ())), preferred_element_type=F32)


def split(x):
    hi = x.astype(BF16)
    return hi, (x - hi.astype(F32)).astype(BF16)


def dot3_nt(x, w_hi, w_lo):
    rows = x.shape[0]
    hi, lo = split(x)
    both = dot_nt(jnp.concatenate([hi, lo], axis=0), w_hi)
    return both[:rows] + both[rows:] + dot_nt(hi, w_lo)


def dot_exact(x, ones):
    rows = x.shape[0]
    both = dot(jnp.concatenate(split(x), axis=0), ones)
    return both[:rows] + both[rows:]


def dot3(x, w_hi, w_lo):
    rows = x.shape[0]
    hi, lo = split(x)
    both = dot(jnp.concatenate([hi, lo], axis=0), w_hi)
    return both[:rows] + both[rows:] + dot(hi, w_lo)


def kernel(
    n_sy, n_sx, side, pad,
    loads_in, flex_in, basis_in, cinv_own, size_in, owner_in, slot_in,
    both_ref,
    loads_ref, basis_ref, cinv_ref, size_ref, owner_ref, slot_ref,
    flex_v, q, q_t, slot_row, slot_col, a_hi, a_lo,
    b8_hi, b8_lo, bb_hi, bb_lo, ka_hi, ka_lo, loads_s, send_a, recv_a, cinv_in, turned, side_in, cr,
    g_send, g_recv, c_send, c_all, five_send, five_all,
    ready_sem, flex_sem, in_sem, sa_sem, ra_sem, sc_sem, rc_sem, ss_sem, rs_sem, sg_sem, rg_sem,
    sag_sem, rag_sem,
):
    cols = loads_ref.shape[1]
    modes = basis_ref.shape[2]
    traces = flex_v.shape[0]
    full = 4 * pad
    groups = LANES // modes
    halves = cols // groups
    n = n_sy * n_sx
    i = lax.axis_index("sy")
    j = lax.axis_index("sx")
    me = i * n_sx + j
    exists = (j > 0, j < n_sx - 1, i > 0, i < n_sy - 1)
    place = ((i, j - 1), (i, j + 1), (i - 1, j), (i + 1, j))

    barrier = pltpu.get_barrier_semaphore()
    row_mates = [(i, lax.rem(j + o, n_sx)) for o in range(1, n_sx)]
    column_mates = [(lax.rem(i + o, n_sy), j) for o in range(1, n_sy)]
    for mate in row_mates + column_mates:
        pl.semaphore_signal(barrier, inc=1, device_id=mate, device_id_type=MESH)

    fetches = [
        pltpu.make_async_copy(src, dst, in_sem.at[q])
        for q, (src, dst) in enumerate(
            (
                (slot_in, slot_ref), (basis_in, basis_ref), (cinv_own, cinv_ref), (loads_in, loads_ref),
                (size_in, size_ref), (owner_in, owner_ref),
            )
        )
    ]
    for fetch in fetches:
        fetch.start()
    flex_copy = pltpu.make_async_copy(flex_in.at[0, 0], flex_v, flex_sem)
    flex_copy.start()
    for s in range(4):
        @pl.when(jnp.logical_not(exists[s]))
        def _(s=s):
            recv_a[s] = jnp.zeros(recv_a.shape[1:], F32)
            for phase in range(2):
                g_recv[phase, s] = jnp.zeros(g_recv.shape[2:], F32)
            if s >= 2:
                cinv_in[s - 2] = jnp.zeros(cinv_in.shape[1:], F32)

    turned[...] = jnp.zeros_like(turned)
    five = 1 + len(exists)
    wide = five * LANES
    def shifted(at, o, size):
        return lax.bitwise_xor(at, o) if size & (size - 1) == 0 else lax.rem(at + o, size)

    def device(o):
        return (shifted(i, lax.rem(o, n_sy), n_sy), shifted(j, lax.div(o, n_sy), n_sx))

    for fetch in fetches:
        fetch.wait()
    slot_row[...] = jnp.full_like(slot_row, -1)
    for s in range(4):
        slot_row[:, s * pad : s * pad + side] = jnp.broadcast_to(slot_ref[s], (8, side))
    trace_id = lax.broadcasted_iota(jnp.int32, (traces, full), 0)
    q_t[...] = (trace_id == slot_row[0:1, :]).astype(F32).astype(BF16)

    basis_hi, basis_lo = split(basis_ref[0, 0])
    both = dot(jnp.concatenate([basis_hi, basis_lo], axis=0), q_t[...])
    basis_side = both[:modes] + both[modes:]

    lane = lax.broadcasted_iota(jnp.int32, (1, pad), 1)
    signs = [(1 - 2 * owner_ref[0, 0, a]).astype(F32) for a in range(2)]
    own_mask = [jnp.where(lane < size_ref[0, 0, a], 1.0, 0.0).astype(F32) for a in range(2)]
    loads_s[...] = jnp.zeros_like(loads_s)
    for a in range(2):
        loads_s[a, :, :side] = loads_ref[a, :, 0, :]
    for s in range(4):
        send_a[s, cols : cols + modes] = basis_side[:, s * pad : (s + 1) * pad]
    start_side = [None] * 4
    for a, s in ((0, 1), (1, 3)):
        start_side[s] = loads_s[a] * (own_mask[a] * signs[a])
        send_a[s, :cols] = start_side[s]
        send_a[s, cols + modes :] = jnp.broadcast_to(own_mask[a], (8, pad))

    pl.semaphore_wait(barrier, n_sx + n_sy - 2)
    for mate in row_mates:
        pl.semaphore_signal(ready_sem, inc=1, device_id=mate, device_id_type=MESH)

    def first(s):
        return pltpu.make_async_remote_copy(
            src_ref=send_a.at[s],
            dst_ref=recv_a.at[OPPOSITE[s]],
            send_sem=sa_sem.at[s],
            recv_sem=ra_sem.at[OPPOSITE[s]],
            device_id=place[s],
            device_id_type=MESH,
        )

    def first_back(s):
        return pltpu.make_async_remote_copy(
            src_ref=send_a.at[s, pl.ds(cols, modes)],
            dst_ref=recv_a.at[OPPOSITE[s], pl.ds(cols, modes)],
            send_sem=sa_sem.at[s],
            recv_sem=ra_sem.at[OPPOSITE[s]],
            device_id=place[s],
            device_id_type=MESH,
        )

    make_first = (first_back, first, first_back, first)
    for s in range(4):
        @pl.when(exists[s])
        def _(s=s):
            make_first[s](s).start()

    def column_copy(slot, di, shift):
        i2 = lax.rem(i + di, n_sy)
        return pltpu.make_async_remote_copy(
            src_ref=cinv_ref.at[pl.ds(pl.multiple_of((i2 + shift) * modes, 8), modes)],
            dst_ref=cinv_in.at[slot, i],
            send_sem=sc_sem.at[slot, i2],
            recv_sem=rc_sem.at[slot, i],
            device_id=(i2, j),
            device_id_type=MESH,
        )

    def column_send(act):
        for di in range(1, n_sy):
            i2 = lax.rem(i + di, n_sy)

            @pl.when(i2 > 0)
            def _(di=di):
                act(column_copy(0, di, -1))

            @pl.when(i2 < n_sy - 1)
            def _(di=di):
                act(column_copy(1, di, 1))

    def landed(slot, src):
        here = cinv_in.at[slot, src]
        pltpu.make_async_copy(here, here, rc_sem.at[slot, src]).wait()

    def row_copy(mate):
        return pltpu.make_async_remote_copy(
            src_ref=turned.at[pl.ds(pl.multiple_of(mate[1] * modes, 8), 3 * modes)],
            dst_ref=side_in.at[j],
            send_sem=ss_sem,
            recv_sem=rs_sem,
            device_id=mate,
            device_id_type=MESH,
        )

    def row_all():
        block = side_in.at[pl.ds(0, n_sx - 1)]
        return pltpu.make_async_remote_copy(
            src_ref=block,
            dst_ref=block,
            send_sem=ss_sem,
            recv_sem=rs_sem,
            device_id=row_mates[0],
            device_id_type=MESH,
        )

    column_send(lambda copy: copy.start())
    turned[modes : (n_sx + 1) * modes, : n_sy * modes] = jnp.transpose(cinv_ref[...])

    for mate in row_mates:
        row_copy(mate).start()
    side_in[j] = turned[pl.ds(pl.multiple_of(j * modes, 8), 3 * modes)]

    @pl.when(i > 0)
    def _():
        cinv_in[0, i] = cinv_ref[pl.ds(pl.multiple_of((i - 1) * modes, 8), modes)]

    @pl.when(i < n_sy - 1)
    def _():
        cinv_in[1, i] = cinv_ref[pl.ds(pl.multiple_of((i + 1) * modes, 8), modes)]

    b8 = jnp.transpose(jnp.concatenate([basis_side] * groups, axis=0))
    part_hi, part_lo = split(b8)
    b8_hi[...] = part_hi
    b8_lo[...] = part_lo

    slot_col[...] = jnp.transpose(slot_row[...].astype(F32)).astype(jnp.int32)
    slot_id = lax.broadcasted_iota(jnp.int32, (full, traces), 1)
    q[...] = (slot_id == slot_col[:, 0:1]).astype(F32).astype(BF16)

    flex_copy.wait()

    chunks = 3
    chunk = traces // chunks

    def permute(step, carry):
        at = pl.ds(pl.multiple_of(step * chunk, chunk), chunk)
        both = dot(jnp.concatenate(split(flex_v[at, :]), axis=0), q_t[...]).astype(BF16)
        a_hi[at, :] = both[:chunk]
        a_lo[at, :] = both[chunk:]
        return carry

    def flexed_of(vec):
        rows = vec.shape[0]
        traced = dot(jnp.concatenate(split(vec), axis=0), q[...]).astype(BF16)
        both = dot(traced, a_hi[...])
        return both[:rows] + both[rows:] + dot(traced[:rows], a_lo[...])

    lax.fori_loop(0, chunks, permute, 0)

    for s in range(4):
        @pl.when(exists[OPPOSITE[s]])
        def _(s=s):
            make_first[s](s).wait_recv()
    masks = [None] * 4
    for a, s in ((0, 0), (1, 2)):
        start_side[s] = -recv_a[s, :cols]
        masks[s] = recv_a[s, cols + modes : cols + modes + 1]
        masks[s + 1] = own_mask[a]
    mask = jnp.concatenate(masks, axis=1)
    res = jnp.concatenate(start_side, axis=1)

    side_row = lax.broadcasted_iota(jnp.int32, (cols, halves * LANES), 0)
    side_lane = lax.broadcasted_iota(jnp.int32, (cols, halves * LANES), 1)
    on_col = jnp.where(lax.div(side_lane, modes) == side_row, 1.0, 0.0).astype(F32)
    bit_row = lax.broadcasted_iota(jnp.int32, (cols, LANES), 0)
    bit_lane = lax.broadcasted_iota(jnp.int32, (cols, LANES), 1)
    pick = jnp.where(lax.div(bit_lane, modes) == lax.rem(bit_row, groups), 1.0, 0.0).astype(F32)
    slot_of = lax.rem(lax.broadcasted_iota(jnp.int32, (1, LANES), 1), modes)
    in_half = lax.div(bit_row, groups)
    in_group = lax.rem(bit_row, groups)

    def to_row(column):
        return jnp.sum(column * on_col, axis=0, keepdims=True)

    def pack(rows):
        tile = jnp.zeros((1, LANES), F32)
        for v, row in enumerate(rows):
            for h in range(halves):
                tile = tile + jnp.where(slot_of == v * halves + h, row[:, h * LANES : (h + 1) * LANES], 0.0)
        return tile

    def unpack(phase, count):
        tile = jnp.sum(five_all[phase - 1, pl.ds(n_sx, n), 0, halves * wide :], axis=0, keepdims=True)
        columns = []
        for v in range(count):
            spot = jnp.where(bit_lane == in_group * modes + v * halves + in_half, 1.0, 0.0)
            columns.append(jnp.sum(tile * spot, axis=1, keepdims=True))
        return columns

    def send_all(src, dst, send_sem, recv_sem):
        def send(step, carry):
            o = n - step
            pltpu.make_async_remote_copy(
                src_ref=src,
                dst_ref=dst,
                send_sem=send_sem,
                recv_sem=recv_sem,
                device_id=device(o),
                device_id_type=MESH,
            ).start()
            return carry

        lax.fori_loop(1, n, send, 0)

    def all_of(block, send_sem, recv_sem):
        return pltpu.make_async_remote_copy(
            src_ref=block,
            dst_ref=block,
            send_sem=send_sem,
            recv_sem=recv_sem,
            device_id=device(1),
            device_id_type=MESH,
        )

    def all_coarse(phase):
        block = c_all.at[pl.ds(0, n - 1)] if phase == 0 else five_all.at[phase - 1, pl.ds(0, n - 1)]
        return all_of(block, sag_sem.at[phase], rag_sem.at[phase])

    def coarse_send(vec):
        product = dot3(vec, b8_hi[...], b8_lo[...]) * pick
        pieces = [
            jnp.sum(product[h * groups : (h + 1) * groups], axis=0, keepdims=True) for h in range(halves)
        ]
        message = jnp.concatenate(pieces, axis=1)
        c_send[...] = message
        c_all[me] = message
        pl.semaphore_wait(ready_sem, n_sx - 1)
        send_all(c_send, c_all.at[me], sag_sem.at[0], rag_sem.at[0])

    def five_send_all(phase, message):
        five_send[phase - 1] = message
        five_all[phase - 1, n_sx + me] = message
        send_all(
            five_send.at[phase - 1], five_all.at[phase - 1, n_sx + me], sag_sem.at[phase], rag_sem.at[phase]
        )

    unroll = 8
    shifts = (1, 0, -1, n_sx, -n_sx)

    def coarse_row(phase, d, h):
        if phase == 0:
            return c_all[d, :, h * LANES : (h + 1) * LANES]
        row = None
        for q, shift in enumerate(shifts):
            at = h * wide + q * LANES
            part = five_all[phase - 1, d + (n_sx + shift), :, at : at + LANES]
            row = part if row is None else row + part
        return row

    def coarse_take(phase):
        all_coarse(phase).wait_recv()

        def add(step, totals):
            totals = list(totals)
            for u in range(unroll):
                d = step * unroll + u
                rows = cr[d]
                for h in range(halves):
                    totals[h] = totals[h] + rows * coarse_row(phase, d, h)
            return tuple(totals)

        zero = jnp.zeros((five * modes, LANES), F32)
        return lax.fori_loop(0, n // unroll, add, (zero,) * halves)

    def weights_of(totals):
        gather = pick[:groups].astype(BF16)
        parts = []
        for total in totals:
            hi, lo = split(total)
            parts.append(dot_nt(gather, hi) + dot_nt(gather, lo))
        return jnp.concatenate(parts, axis=0)

    same_row = lax.broadcasted_iota(jnp.int32, (LANES, LANES), 0)
    same_lane = lax.broadcasted_iota(jnp.int32, (LANES, LANES), 1)
    same = (lax.div(same_row, modes) == lax.div(same_lane, modes)).astype(F32).astype(BF16)
    mode_row = lax.broadcasted_iota(jnp.int32, (modes, LANES), 0)
    mode_lane = lax.broadcasted_iota(jnp.int32, (modes, LANES), 1)
    on_mode = jnp.where(lax.rem(mode_lane, modes) == mode_row, 1.0, 0.0).astype(F32)
    repeat = on_col.astype(BF16)

    rows = five * modes

    def widened(blocks):
        sums = dot_exact(jnp.concatenate(blocks, axis=0), same)
        width = sums.shape[0] // halves
        return jnp.concatenate([sums[h * width : (h + 1) * width] for h in range(halves)], axis=1)

    def coupled(weights):
        hi, lo = split(weights)
        return dot3(coupling, hi, lo)

    def blocks_of(result):
        pieces = []
        for h in range(halves):
            for v in range(five):
                block = result[v * modes : (v + 1) * modes, h * LANES : (h + 1) * LANES]
                pieces.append(jnp.sum(block * on_mode, axis=0, keepdims=True))
        return pieces

    def column_sum(x, y):
        return jnp.sum(x * y, axis=0, keepdims=True)

    def swap(phase, s):
        return pltpu.make_async_remote_copy(
            src_ref=g_send.at[phase, s],
            dst_ref=g_recv.at[phase, OPPOSITE[s]],
            send_sem=sg_sem.at[phase, s],
            recv_sem=rg_sem.at[phase, OPPOSITE[s]],
            device_id=place[s],
            device_id_type=MESH,
        )

    def swap_start(phase, out):
        for s in range(4):
            g_send[phase, s] = out[:, s * pad : (s + 1) * pad]
        for s in range(4):
            @pl.when(exists[s])
            def _(s=s):
                swap(phase, s).start()

    def dual_take(phase, out):
        for s in range(4):
            @pl.when(exists[OPPOSITE[s]])
            def _(s=s):
                swap(phase, s).wait_recv()
        other = jnp.concatenate([g_recv[phase, s] for s in range(4)], axis=1)
        return (out - other) * mask

    def own_dot(x, y):
        total = x[:, pad : 2 * pad] * y[:, pad : 2 * pad] + x[:, 3 * pad :] * y[:, 3 * pad :]
        return jnp.sum(total, axis=1, keepdims=True)

    coarse_send(res)

    own_part = basis_side * mask
    lanes_at = lax.broadcasted_iota(jnp.int32, (modes, full), 1)
    nbr = jnp.concatenate([recv_a[s, cols : cols + modes] for s in range(4)], axis=1) * mask
    blocks = [jnp.where(lax.div(lanes_at, pad) == s, -nbr, 0.0) for s in range(4)]
    blocks.insert(1, own_part)
    basis_five = jnp.concatenate(blocks, axis=0)
    part_hi, part_lo = split(basis_five)
    bb_hi[...] = part_hi
    bb_lo[...] = part_lo

    flexed = flexed_of(jnp.concatenate([basis_five, res], axis=0))
    flexed_basis = flexed[:rows]
    flexed_res = flexed[rows:]
    part_hi, part_lo = split(flexed_basis)
    ka_hi[...] = part_hi
    ka_lo[...] = part_lo
    res_hi, res_lo = split(res)
    coupling = dot3_nt(flexed_basis, bb_hi[...], bb_lo[...])
    known = dot_exact(dot3_nt(jnp.concatenate([flexed_basis, own_part], axis=0), res_hi, res_lo), repeat)
    known0 = known[:rows]
    coarse0 = known[rows:]
    square = to_row(own_dot(res, res))
    bend = to_row(jnp.sum(res * flexed_res, axis=1, keepdims=True))
    for di in range(1, n_sy):
        src = lax.rem(i + di, n_sy)

        @pl.when(i > 0)
        def _(src=src):
            landed(0, src)

        @pl.when(i < n_sy - 1)
        def _(src=src):
            landed(1, src)

    pick_row = lax.broadcasted_iota(jnp.int32, (LANES, LANES), 0)
    pick_lane = lax.broadcasted_iota(jnp.int32, (LANES, LANES), 1)

    def widen(block, group):
        at = (group // groups) * LANES
        chosen = pick_row == group % groups * modes + lax.rem(pick_lane, modes)
        value = block[..., at : at + LANES]
        wide_value = dot_exact(value.reshape(-1, LANES), chosen.astype(F32).astype(BF16))
        return wide_value.reshape(value.shape)

    for j2 in range(n_sx):
        block = widen(cinv_in[...], j2)
        for i2 in range(n_sy):
            for v in range(2):
                cr[i2 * n_sx + j2, (3 + v) * modes : (4 + v) * modes] = block[v, i2]
    row_all().wait_recv()
    for i2 in range(n_sy):
        cr[i2 * n_sx : (i2 + 1) * n_sx, : 3 * modes] = widen(side_in[...], i2)

    totals = coarse_take(0)
    weights = weights_of(totals)
    out0 = flexed_res + dot3(weights, ka_hi[...], ka_lo[...])
    swap_start(0, out0)
    weights0 = widened(totals)
    result0 = coupled(weights0) + known0
    norm_row = square + column_sum(coarse0, weights0[modes : 2 * modes])
    curve_row = bend + column_sum(weights0, result0 + known0)
    five_send_all(1, jnp.concatenate(blocks_of(result0) + [pack([norm_row, curve_row])], axis=1))
    for phase in range(2):
        edge = jnp.zeros((n_sx, 1, halves * wide + LANES), F32)
        five_all[phase, pl.ds(0, n_sx)] = edge
        five_all[phase, pl.ds(n_sx + n, n_sx)] = edge

    cor0 = res + dot3(weights, bb_hi[...], bb_lo[...])
    image0 = dual_take(0, out0)
    image_hi, image_lo = split(image0)
    known1 = dot_exact(dot3_nt(flexed_basis, image_hi, image_lo), repeat)
    flexed_image = flexed_of(image0)

    totals = coarse_take(1)
    own_rows = [coarse_row(1, me, h) * on_mode for h in range(halves)]
    sides = []
    for h in range(halves):
        sides += [totals[h], own_rows[h]]
    sides = widened(sides)
    weights1 = sides[:rows]
    coarse1 = sides[rows:]
    result1 = coupled(weights1) + known1
    norm0, curve0 = unpack(1, 2)
    step0 = norm0 / curve0
    step_row = to_row(step0)
    res1 = res - step0 * image0
    flexed_res1 = flexed_res - step0 * flexed_image
    square = to_row(own_dot(res1, res1))
    bend = to_row(jnp.sum(res1 * flexed_res1, axis=1, keepdims=True))
    change = weights0 - step_row * weights1
    norm_row = square + column_sum(coarse0 - step_row * coarse1, change[modes : 2 * modes])
    curve_row = bend + column_sum(change, (result0 + known0) - step_row * (result1 + known1))
    five_send_all(2, jnp.concatenate(blocks_of(result1) + [pack([norm_row, curve_row])], axis=1))
    weights = weights_of(totals)
    out1 = flexed_image + dot3(weights, ka_hi[...], ka_lo[...])
    swap_start(1, out1)
    pre_image0 = image0 + dot3(weights, bb_hi[...], bb_lo[...])
    cor1 = cor0 - step0 * pre_image0
    image1 = dual_take(1, out1)

    totals = coarse_take(2)
    norm1, curve1 = unpack(2, 2)
    beta = norm1 / norm0
    step1 = norm1 / (curve1 - beta * beta * curve0)
    total = step0 * cor0 + step1 * (cor1 + beta * cor0)
    near = cor1 - step1 * ((1.0 + beta) * pre_image0 - step0 * image1)
    weights = weights_of(totals)
    cor2 = near + (step1 * step0) * dot3(weights, bb_hi[...], bb_lo[...])
    for a in range(2):
        at = (2 * a + 1) * pad
        both_ref[0, a] = total[:, at : at + side] * signs[a]
        both_ref[1, a] = cor2[:, at : at + side] * signs[a]

    for s in range(4):
        @pl.when(exists[s])
        def _(s=s):
            make_first[s](s).wait_send()
            swap(0, s).wait_send()
            swap(1, s).wait_send()
    column_send(lambda copy: copy.wait_send())
    row_all().wait_send()
    for phase in range(3):
        all_coarse(phase).wait_send()


def lay_out(both_ref, mult_ref, prec_ref):
    for a in range(2):
        mult_ref[a, :, 0, :] = both_ref[0, a]
        prec_ref[a, :, 0, :] = both_ref[1, a]


def per_device(n_sy, n_sx, loads, flex, basis, coarse_inv, pair_size, owner, trace_slot):
    cols, side = loads.shape[1], loads.shape[3]
    modes, traces = basis.shape[2], basis.shape[3]
    pad = side
    full = 4 * pad
    n = n_sy * n_sx
    width = cols * modes
    turned_width = pl.cdiv(coarse_inv.shape[0], LANES) * LANES
    dma = pltpu.SemaphoreType.DMA
    vmem = pl.BlockSpec(memory_space=pltpu.VMEM)
    both = pl.pallas_call(
        functools.partial(kernel, n_sy, n_sx, side, pad),
        out_shape=pltpu.VMEM((2, 2, cols, side), F32),
        in_specs=[pl.BlockSpec(memory_space=pl.ANY)] * 7,
        out_specs=vmem,
        scratch_shapes=[
            pltpu.VMEM(loads.shape, F32),
            pltpu.VMEM(basis.shape, F32),
            pltpu.VMEM(coarse_inv.shape, F32),
            pltpu.SMEM((1, 1, 2), jnp.int32),
            pltpu.SMEM((1, 1, 2), jnp.int32),
            pltpu.VMEM(trace_slot.shape, jnp.int32),
            pltpu.VMEM((traces, traces), F32),
            pltpu.VMEM((full, traces), BF16),
            pltpu.VMEM((traces, full), BF16),
            pltpu.VMEM((8, full), jnp.int32),
            pltpu.VMEM((full, 8), jnp.int32),
            pltpu.VMEM((traces, full), BF16),
            pltpu.VMEM((traces, full), BF16),
            pltpu.VMEM((full, LANES), BF16),
            pltpu.VMEM((full, LANES), BF16),
            pltpu.VMEM((5 * modes, full), BF16),
            pltpu.VMEM((5 * modes, full), BF16),
            pltpu.VMEM((5 * modes, full), BF16),
            pltpu.VMEM((5 * modes, full), BF16),
            pltpu.VMEM((2, cols, pad), F32),
            pltpu.VMEM((4, cols + modes + 8, pad), F32),
            pltpu.VMEM((4, cols + modes + 8, pad), F32),
            pltpu.VMEM((2, n_sy, modes, coarse_inv.shape[1]), F32),
            pltpu.VMEM(((n_sx + 2) * modes, turned_width), F32),
            pltpu.VMEM((n_sx, 3 * modes, turned_width), F32),
            pltpu.VMEM((n, 5 * modes, LANES), F32),
            pltpu.VMEM((2, 4, cols, pad), F32),
            pltpu.VMEM((2, 4, cols, pad), F32),
            pltpu.VMEM((1, width), F32),
            pltpu.VMEM((n, 1, width), F32),
            pltpu.VMEM((2, 1, 5 * width + LANES), F32),
            pltpu.VMEM((2, n + 2 * n_sx, 1, 5 * width + LANES), F32),
            pltpu.SemaphoreType.REGULAR,
            dma,
            dma((6,)),
            dma((4,)),
            dma((4,)),
            dma((2, n_sy)),
            dma((2, n_sy)),
            dma,
            dma,
            dma((2, 4)),
            dma((2, 4)),
            dma((3,)),
            dma((3,)),
        ],
        compiler_params=pltpu.CompilerParams(
            collective_id=0, has_side_effects=True, vmem_limit_bytes=60 * 1024 * 1024
        ),
    )(
        loads, flex, basis, coarse_inv,
        jnp.transpose(pair_size, (1, 2, 0)), jnp.transpose(owner, (1, 2, 0)), trace_slot,
    )

    out = jax.ShapeDtypeStruct(loads.shape, F32)
    return pl.pallas_call(
        lay_out, out_shape=(out, out), in_specs=[vmem], out_specs=(vmem, vmem)
    )(pltpu.with_memory_space_constraint(both, pltpu.VMEM))


def solution(mesh):
    return jax.shard_map(
        functools.partial(per_device, mesh.shape["sy"], mesh.shape["sx"]),
        mesh=mesh,
        in_specs=(
            P(None, None, "sy", "sx"),
            P("sy", "sx", None, None),
            P("sy", "sx", None, None),
            P("sx", "sy"),
            P(None, "sy", "sx"),
            P(None, "sy", "sx"),
            P(None, "sy", "sx"),
        ),
        out_specs=(P(None, None, "sy", "sx"), P(None, None, "sy", "sx")),
        check_vma=False,
    )
```

```python
import functools

import jax
import jax.numpy as jnp
from jax import lax
from jax.experimental import pallas as pl
from jax.experimental.pallas import tpu as pltpu
from jax.sharding import PartitionSpec as P

LANES = 128
MESH = pl.DeviceIdType.MESH
OPPOSITE = (1, 0, 3, 2)
F32 = jnp.float32
BF16 = jnp.bfloat16


def dot(a, b):
    return jnp.dot(a, b, preferred_element_type=F32)


def dot_nt(a, b):
    return lax.dot_general(a, b, (((1,), (1,)), ((), ())), preferred_element_type=F32)


def split(x):
    hi = x.astype(BF16)
    return hi, (x - hi.astype(F32)).astype(BF16)


def dot3_nt(x, w_hi, w_lo):
    rows = x.shape[0]
    hi, lo = split(x)
    both = dot_nt(jnp.concatenate([hi, lo], axis=0), w_hi)
    return both[:rows] + both[rows:] + dot_nt(hi, w_lo)


def dot_exact(x, ones):
    rows = x.shape[0]
    both = dot(jnp.concatenate(split(x), axis=0), ones)
    return both[:rows] + both[rows:]


def dot3(x, w_hi, w_lo):
    rows = x.shape[0]
    hi, lo = split(x)
    both = dot(jnp.concatenate([hi, lo], axis=0), w_hi)
    return both[:rows] + both[rows:] + dot(hi, w_lo)


def kernel(
    n_sy, n_sx, side, pad,
    loads_in, flex_in, basis_in, cinv_own, size_in, owner_in, slot_in,
    both_ref,
    loads_ref, basis_ref, cinv_ref, size_ref, owner_ref, slot_ref,
    flex_v, q, q_t, slot_row, slot_col, a_hi, a_lo,
    b8_hi, b8_lo, bb_hi, bb_lo, ka_hi, ka_lo, loads_s, send_a, recv_a, cinv_in, turned, side_in, cr,
    g_send, g_recv, c_send, c_all, five_send, five_all,
    ready_sem, flex_sem, in_sem, sa_sem, ra_sem, sc_sem, rc_sem, ss_sem, rs_sem, sg_sem, rg_sem,
    sag_sem, rag_sem,
):
    cols = loads_ref.shape[1]
    modes = basis_ref.shape[2]
    traces = flex_v.shape[0]
    full = 4 * pad
    groups = LANES // modes
    halves = cols // groups
    n = n_sy * n_sx
    i = lax.axis_index("sy")
    j = lax.axis_index("sx")
    me = i * n_sx + j
    exists = (j > 0, j < n_sx - 1, i > 0, i < n_sy - 1)
    place = ((i, j - 1), (i, j + 1), (i - 1, j), (i + 1, j))

    barrier = pltpu.get_barrier_semaphore()
    row_mates = [(i, lax.rem(j + o, n_sx)) for o in range(1, n_sx)]
    column_mates = [(lax.rem(i + o, n_sy), j) for o in range(1, n_sy)]
    for mate in row_mates + column_mates:
        pl.semaphore_signal(barrier, inc=1, device_id=mate, device_id_type=MESH)

    fetches = [
        pltpu.make_async_copy(src, dst, in_sem.at[q])
        for q, (src, dst) in enumerate(
            (
                (slot_in, slot_ref), (basis_in, basis_ref), (cinv_own, cinv_ref), (loads_in, loads_ref),
                (size_in, size_ref), (owner_in, owner_ref),
            )
        )
    ]
    for fetch in fetches:
        fetch.start()
    flex_copy = pltpu.make_async_copy(flex_in.at[0, 0], flex_v, flex_sem)
    flex_copy.start()
    for s in range(4):
        @pl.when(jnp.logical_not(exists[s]))
        def _(s=s):
            recv_a[s] = jnp.zeros(recv_a.shape[1:], F32)
            for phase in range(2):
                g_recv[phase, s] = jnp.zeros(g_recv.shape[2:], F32)
            if s >= 2:
                cinv_in[s - 2] = jnp.zeros(cinv_in.shape[1:], F32)

    turned[...] = jnp.zeros_like(turned)
    five = 1 + len(exists)
    wide = five * LANES
    def shifted(at, o, size):
        return lax.bitwise_xor(at, o) if size & (size - 1) == 0 else lax.rem(at + o, size)

    def device(o):
        return (shifted(i, lax.rem(o, n_sy), n_sy), shifted(j, lax.div(o, n_sy), n_sx))

    for fetch in fetches:
        fetch.wait()
    slot_row[...] = jnp.full_like(slot_row, -1)
    for s in range(4):
        slot_row[:, s * pad : s * pad + side] = jnp.broadcast_to(slot_ref[s], (8, side))
    trace_id = lax.broadcasted_iota(jnp.int32, (traces, full), 0)
    q_t[...] = (trace_id == slot_row[0:1, :]).astype(F32).astype(BF16)

    basis_hi, basis_lo = split(basis_ref[0, 0])
    both = dot(jnp.concatenate([basis_hi, basis_lo], axis=0), q_t[...])
    basis_side = both[:modes] + both[modes:]

    lane = lax.broadcasted_iota(jnp.int32, (1, pad), 1)
    signs = [(1 - 2 * owner_ref[0, 0, a]).astype(F32) for a in range(2)]
    own_mask = [jnp.where(lane < size_ref[0, 0, a], 1.0, 0.0).astype(F32) for a in range(2)]
    loads_s[...] = jnp.zeros_like(loads_s)
    for a in range(2):
        loads_s[a, :, :side] = loads_ref[a, :, 0, :]
    for s in range(4):
        send_a[s, cols : cols + modes] = basis_side[:, s * pad : (s + 1) * pad]
    start_side = [None] * 4
    for a, s in ((0, 1), (1, 3)):
        start_side[s] = loads_s[a] * (own_mask[a] * signs[a])
        send_a[s, :cols] = start_side[s]
        send_a[s, cols + modes :] = jnp.broadcast_to(own_mask[a], (8, pad))

    pl.semaphore_wait(barrier, n_sx + n_sy - 2)
    for mate in row_mates:
        pl.semaphore_signal(ready_sem, inc=1, device_id=mate, device_id_type=MESH)

    def first(s):
        return pltpu.make_async_remote_copy(
            src_ref=send_a.at[s],
            dst_ref=recv_a.at[OPPOSITE[s]],
            send_sem=sa_sem.at[s],
            recv_sem=ra_sem.at[OPPOSITE[s]],
            device_id=place[s],
            device_id_type=MESH,
        )

    def first_back(s):
        return pltpu.make_async_remote_copy(
            src_ref=send_a.at[s, pl.ds(cols, modes)],
            dst_ref=recv_a.at[OPPOSITE[s], pl.ds(cols, modes)],
            send_sem=sa_sem.at[s],
            recv_sem=ra_sem.at[OPPOSITE[s]],
            device_id=place[s],
            device_id_type=MESH,
        )

    make_first = (first_back, first, first_back, first)
    for s in range(4):
        @pl.when(exists[s])
        def _(s=s):
            make_first[s](s).start()

    def column_copy(slot, di, shift):
        i2 = lax.rem(i + di, n_sy)
        return pltpu.make_async_remote_copy(
            src_ref=cinv_ref.at[pl.ds(pl.multiple_of((i2 + shift) * modes, 8), modes)],
            dst_ref=cinv_in.at[slot, i],
            send_sem=sc_sem.at[slot, i2],
            recv_sem=rc_sem.at[slot, i],
            device_id=(i2, j),
            device_id_type=MESH,
        )

    def column_send(act):
        for di in range(1, n_sy):
            i2 = lax.rem(i + di, n_sy)

            @pl.when(i2 > 0)
            def _(di=di):
                act(column_copy(0, di, -1))

            @pl.when(i2 < n_sy - 1)
            def _(di=di):
                act(column_copy(1, di, 1))

    def landed(slot, src):
        here = cinv_in.at[slot, src]
        pltpu.make_async_copy(here, here, rc_sem.at[slot, src]).wait()

    def row_copy(mate):
        return pltpu.make_async_remote_copy(
            src_ref=turned.at[pl.ds(pl.multiple_of(mate[1] * modes, 8), 3 * modes)],
            dst_ref=side_in.at[j],
            send_sem=ss_sem,
            recv_sem=rs_sem,
            device_id=mate,
            device_id_type=MESH,
        )

    def row_all():
        block = side_in.at[pl.ds(0, n_sx - 1)]
        return pltpu.make_async_remote_copy(
            src_ref=block,
            dst_ref=block,
            send_sem=ss_sem,
            recv_sem=rs_sem,
            device_id=row_mates[0],
            device_id_type=MESH,
        )

    column_send(lambda copy: copy.start())
    turned[modes : (n_sx + 1) * modes, : n_sy * modes] = jnp.transpose(cinv_ref[...])

    for mate in row_mates:
        row_copy(mate).start()
    side_in[j] = turned[pl.ds(pl.multiple_of(j * modes, 8), 3 * modes)]

    @pl.when(i > 0)
    def _():
        cinv_in[0, i] = cinv_ref[pl.ds(pl.multiple_of((i - 1) * modes, 8), modes)]

    @pl.when(i < n_sy - 1)
    def _():
        cinv_in[1, i] = cinv_ref[pl.ds(pl.multiple_of((i + 1) * modes, 8), modes)]

    b8 = jnp.transpose(jnp.concatenate([basis_side] * groups, axis=0))
    part_hi, part_lo = split(b8)
    b8_hi[...] = part_hi
    b8_lo[...] = part_lo

    slot_col[...] = jnp.transpose(slot_row[...].astype(F32)).astype(jnp.int32)
    slot_id = lax.broadcasted_iota(jnp.int32, (full, traces), 1)
    q[...] = (slot_id == slot_col[:, 0:1]).astype(F32).astype(BF16)

    flex_copy.wait()

    chunks = 3
    chunk = traces // chunks

    def permute(step, carry):
        at = pl.ds(pl.multiple_of(step * chunk, chunk), chunk)
        both = dot(jnp.concatenate(split(flex_v[at, :]), axis=0), q_t[...]).astype(BF16)
        a_hi[at, :] = both[:chunk]
        a_lo[at, :] = both[chunk:]
        return carry

    def flexed_of(vec):
        rows = vec.shape[0]
        traced = dot(jnp.concatenate(split(vec), axis=0), q[...]).astype(BF16)
        both = dot(traced, a_hi[...])
        return both[:rows] + both[rows:] + dot(traced[:rows], a_lo[...])

    early = 2
    lax.fori_loop(0, early, permute, 0)

    for s in range(4):
        @pl.when(exists[OPPOSITE[s]])
        def _(s=s):
            make_first[s](s).wait_recv()
    masks = [None] * 4
    for a, s in ((0, 0), (1, 2)):
        start_side[s] = -recv_a[s, :cols]
        masks[s] = recv_a[s, cols + modes : cols + modes + 1]
        masks[s + 1] = own_mask[a]
    mask = jnp.concatenate(masks, axis=1)
    res = jnp.concatenate(start_side, axis=1)

    side_row = lax.broadcasted_iota(jnp.int32, (cols, halves * LANES), 0)
    side_lane = lax.broadcasted_iota(jnp.int32, (cols, halves * LANES), 1)
    on_col = jnp.where(lax.div(side_lane, modes) == side_row, 1.0, 0.0).astype(F32)
    bit_row = lax.broadcasted_iota(jnp.int32, (cols, LANES), 0)
    bit_lane = lax.broadcasted_iota(jnp.int32, (cols, LANES), 1)
    pick = jnp.where(lax.div(bit_lane, modes) == lax.rem(bit_row, groups), 1.0, 0.0).astype(F32)
    slot_of = lax.rem(lax.broadcasted_iota(jnp.int32, (1, LANES), 1), modes)
    in_half = lax.div(bit_row, groups)
    in_group = lax.rem(bit_row, groups)

    def to_row(column):
        return jnp.sum(column * on_col, axis=0, keepdims=True)

    def pack(rows):
        tile = jnp.zeros((1, LANES), F32)
        for v, row in enumerate(rows):
            for h in range(halves):
                tile = tile + jnp.where(slot_of == v * halves + h, row[:, h * LANES : (h + 1) * LANES], 0.0)
        return tile

    def unpack(phase, count):
        tile = jnp.sum(five_all[phase - 1, pl.ds(n_sx, n), 0, halves * wide :], axis=0, keepdims=True)
        columns = []
        for v in range(count):
            spot = jnp.where(bit_lane == in_group * modes + v * halves + in_half, 1.0, 0.0)
            columns.append(jnp.sum(tile * spot, axis=1, keepdims=True))
        return columns

    def send_all(src, dst, send_sem, recv_sem):
        def send(step, carry):
            o = n - step
            pltpu.make_async_remote_copy(
                src_ref=src,
                dst_ref=dst,
                send_sem=send_sem,
                recv_sem=recv_sem,
                device_id=device(o),
                device_id_type=MESH,
            ).start()
            return carry

        lax.fori_loop(1, n, send, 0)

    def all_of(block, send_sem, recv_sem):
        return pltpu.make_async_remote_copy(
            src_ref=block,
            dst_ref=block,
            send_sem=send_sem,
            recv_sem=recv_sem,
            device_id=device(1),
            device_id_type=MESH,
        )

    def all_coarse(phase):
        block = c_all.at[pl.ds(0, n - 1)] if phase == 0 else five_all.at[phase - 1, pl.ds(0, n - 1)]
        return all_of(block, sag_sem.at[phase], rag_sem.at[phase])

    def coarse_send(vec):
        product = dot3(vec, b8_hi[...], b8_lo[...]) * pick
        pieces = [
            jnp.sum(product[h * groups : (h + 1) * groups], axis=0, keepdims=True) for h in range(halves)
        ]
        message = jnp.concatenate(pieces, axis=1)
        c_send[...] = message
        c_all[me] = message
        pl.semaphore_wait(ready_sem, n_sx - 1)
        send_all(c_send, c_all.at[me], sag_sem.at[0], rag_sem.at[0])

    def five_send_all(phase, message):
        five_send[phase - 1] = message
        five_all[phase - 1, n_sx + me] = message
        send_all(
            five_send.at[phase - 1], five_all.at[phase - 1, n_sx + me], sag_sem.at[phase], rag_sem.at[phase]
        )

    unroll = 8
    shifts = (1, 0, -1, n_sx, -n_sx)

    def coarse_row(phase, d, h):
        if phase == 0:
            return c_all[d, :, h * LANES : (h + 1) * LANES]
        row = None
        for q, shift in enumerate(shifts):
            at = h * wide + q * LANES
            part = five_all[phase - 1, d + (n_sx + shift), :, at : at + LANES]
            row = part if row is None else row + part
        return row

    def coarse_take(phase):
        all_coarse(phase).wait_recv()

        def add(step, totals):
            totals = list(totals)
            for u in range(unroll):
                d = step * unroll + u
                rows = cr[d]
                for h in range(halves):
                    totals[h] = totals[h] + rows * coarse_row(phase, d, h)
            return tuple(totals)

        zero = jnp.zeros((five * modes, LANES), F32)
        return lax.fori_loop(0, n // unroll, add, (zero,) * halves)

    def weights_of(totals):
        gather = pick[:groups].astype(BF16)
        parts = []
        for total in totals:
            hi, lo = split(total)
            parts.append(dot_nt(gather, hi) + dot_nt(gather, lo))
        return jnp.concatenate(parts, axis=0)

    same_row = lax.broadcasted_iota(jnp.int32, (LANES, LANES), 0)
    same_lane = lax.broadcasted_iota(jnp.int32, (LANES, LANES), 1)
    same = (lax.div(same_row, modes) == lax.div(same_lane, modes)).astype(F32).astype(BF16)
    mode_row = lax.broadcasted_iota(jnp.int32, (modes, LANES), 0)
    mode_lane = lax.broadcasted_iota(jnp.int32, (modes, LANES), 1)
    on_mode = jnp.where(lax.rem(mode_lane, modes) == mode_row, 1.0, 0.0).astype(F32)
    repeat = on_col.astype(BF16)

    rows = five * modes

    def widened(blocks):
        sums = dot_exact(jnp.concatenate(blocks, axis=0), same)
        width = sums.shape[0] // halves
        return jnp.concatenate([sums[h * width : (h + 1) * width] for h in range(halves)], axis=1)

    def coupled(weights):
        hi, lo = split(weights)
        return dot3(coupling, hi, lo)

    def blocks_of(result):
        pieces = []
        for h in range(halves):
            for v in range(five):
                block = result[v * modes : (v + 1) * modes, h * LANES : (h + 1) * LANES]
                pieces.append(jnp.sum(block * on_mode, axis=0, keepdims=True))
        return pieces

    def column_sum(x, y):
        return jnp.sum(x * y, axis=0, keepdims=True)

    def swap(phase, s):
        return pltpu.make_async_remote_copy(
            src_ref=g_send.at[phase, s],
            dst_ref=g_recv.at[phase, OPPOSITE[s]],
            send_sem=sg_sem.at[phase, s],
            recv_sem=rg_sem.at[phase, OPPOSITE[s]],
            device_id=place[s],
            device_id_type=MESH,
        )

    def swap_start(phase, out):
        for s in range(4):
            g_send[phase, s] = out[:, s * pad : (s + 1) * pad]
        for s in range(4):
            @pl.when(exists[s])
            def _(s=s):
                swap(phase, s).start()

    def dual_take(phase, out):
        for s in range(4):
            @pl.when(exists[OPPOSITE[s]])
            def _(s=s):
                swap(phase, s).wait_recv()
        other = jnp.concatenate([g_recv[phase, s] for s in range(4)], axis=1)
        return (out - other) * mask

    def own_dot(x, y):
        total = x[:, pad : 2 * pad] * y[:, pad : 2 * pad] + x[:, 3 * pad :] * y[:, 3 * pad :]
        return jnp.sum(total, axis=1, keepdims=True)

    coarse_send(res)

    own_part = basis_side * mask
    lanes_at = lax.broadcasted_iota(jnp.int32, (modes, full), 1)
    nbr = jnp.concatenate([recv_a[s, cols : cols + modes] for s in range(4)], axis=1) * mask
    blocks = [jnp.where(lax.div(lanes_at, pad) == s, -nbr, 0.0) for s in range(4)]
    blocks.insert(1, own_part)
    basis_five = jnp.concatenate(blocks, axis=0)
    part_hi, part_lo = split(basis_five)
    bb_hi[...] = part_hi
    bb_lo[...] = part_lo

    lax.fori_loop(early, chunks, permute, 0)
    flexed = flexed_of(jnp.concatenate([basis_five, res], axis=0))
    flexed_basis = flexed[:rows]
    flexed_res = flexed[rows:]
    part_hi, part_lo = split(flexed_basis)
    ka_hi[...] = part_hi
    ka_lo[...] = part_lo
    res_hi, res_lo = split(res)
    coupling = dot3_nt(flexed_basis, bb_hi[...], bb_lo[...])
    known = dot_exact(dot3_nt(jnp.concatenate([flexed_basis, own_part], axis=0), res_hi, res_lo), repeat)
    known0 = known[:rows]
    coarse0 = known[rows:]
    square = to_row(own_dot(res, res))
    bend = to_row(jnp.sum(res * flexed_res, axis=1, keepdims=True))
    for di in range(1, n_sy):
        src = lax.rem(i + di, n_sy)

        @pl.when(i > 0)
        def _(src=src):
            landed(0, src)

        @pl.when(i < n_sy - 1)
        def _(src=src):
            landed(1, src)

    pick_row = lax.broadcasted_iota(jnp.int32, (LANES, LANES), 0)
    pick_lane = lax.broadcasted_iota(jnp.int32, (LANES, LANES), 1)

    def widen(block, group):
        at = (group // groups) * LANES
        chosen = pick_row == group % groups * modes + lax.rem(pick_lane, modes)
        value = block[..., at : at + LANES]
        wide_value = dot_exact(value.reshape(-1, LANES), chosen.astype(F32).astype(BF16))
        return wide_value.reshape(value.shape)

    for j2 in range(n_sx):
        block = widen(cinv_in[...], j2)
        for i2 in range(n_sy):
            for v in range(2):
                cr[i2 * n_sx + j2, (3 + v) * modes : (4 + v) * modes] = block[v, i2]
    row_all().wait_recv()
    for i2 in range(n_sy):
        cr[i2 * n_sx : (i2 + 1) * n_sx, : 3 * modes] = widen(side_in[...], i2)

    totals = coarse_take(0)
    weights = weights_of(totals)
    out0 = flexed_res + dot3(weights, ka_hi[...], ka_lo[...])
    swap_start(0, out0)
    weights0 = widened(totals)
    result0 = coupled(weights0) + known0
    norm_row = square + column_sum(coarse0, weights0[modes : 2 * modes])
    curve_row = bend + column_sum(weights0, result0 + known0)
    five_send_all(1, jnp.concatenate(blocks_of(result0) + [pack([norm_row, curve_row])], axis=1))
    for phase in range(2):
        edge = jnp.zeros((n_sx, 1, halves * wide + LANES), F32)
        five_all[phase, pl.ds(0, n_sx)] = edge
        five_all[phase, pl.ds(n_sx + n, n_sx)] = edge

    cor0 = res + dot3(weights, bb_hi[...], bb_lo[...])
    image0 = dual_take(0, out0)
    image_hi, image_lo = split(image0)
    known1 = dot_exact(dot3_nt(flexed_basis, image_hi, image_lo), repeat)
    flexed_image = flexed_of(image0)

    totals = coarse_take(1)
    own_rows = [coarse_row(1, me, h) * on_mode for h in range(halves)]
    sides = []
    for h in range(halves):
        sides += [totals[h], own_rows[h]]
    sides = widened(sides)
    weights1 = sides[:rows]
    coarse1 = sides[rows:]
    result1 = coupled(weights1) + known1
    norm0, curve0 = unpack(1, 2)
    step0 = norm0 / curve0
    step_row = to_row(step0)
    res1 = res - step0 * image0
    flexed_res1 = flexed_res - step0 * flexed_image
    square = to_row(own_dot(res1, res1))
    bend = to_row(jnp.sum(res1 * flexed_res1, axis=1, keepdims=True))
    change = weights0 - step_row * weights1
    norm_row = square + column_sum(coarse0 - step_row * coarse1, change[modes : 2 * modes])
    curve_row = bend + column_sum(change, (result0 + known0) - step_row * (result1 + known1))
    five_send_all(2, jnp.concatenate(blocks_of(result1) + [pack([norm_row, curve_row])], axis=1))
    weights = weights_of(totals)
    out1 = flexed_image + dot3(weights, ka_hi[...], ka_lo[...])
    swap_start(1, out1)
    pre_image0 = image0 + dot3(weights, bb_hi[...], bb_lo[...])
    cor1 = cor0 - step0 * pre_image0
    image1 = dual_take(1, out1)

    totals = coarse_take(2)
    norm1, curve1 = unpack(2, 2)
    beta = norm1 / norm0
    step1 = norm1 / (curve1 - beta * beta * curve0)
    total = step0 * cor0 + step1 * (cor1 + beta * cor0)
    near = cor1 - step1 * ((1.0 + beta) * pre_image0 - step0 * image1)
    weights = weights_of(totals)
    cor2 = near + (step1 * step0) * dot3(weights, bb_hi[...], bb_lo[...])
    for a in range(2):
        at = (2 * a + 1) * pad
        both_ref[0, a] = total[:, at : at + side] * signs[a]
        both_ref[1, a] = cor2[:, at : at + side] * signs[a]

    for s in range(4):
        @pl.when(exists[s])
        def _(s=s):
            make_first[s](s).wait_send()
            swap(0, s).wait_send()
            swap(1, s).wait_send()
    column_send(lambda copy: copy.wait_send())
    row_all().wait_send()
    for phase in range(3):
        all_coarse(phase).wait_send()


def lay_out(both_ref, mult_ref, prec_ref):
    for a in range(2):
        mult_ref[a, :, 0, :] = both_ref[0, a]
        prec_ref[a, :, 0, :] = both_ref[1, a]


def per_device(n_sy, n_sx, loads, flex, basis, coarse_inv, pair_size, owner, trace_slot):
    cols, side = loads.shape[1], loads.shape[3]
    modes, traces = basis.shape[2], basis.shape[3]
    pad = side
    full = 4 * pad
    n = n_sy * n_sx
    width = cols * modes
    turned_width = pl.cdiv(coarse_inv.shape[0], LANES) * LANES
    dma = pltpu.SemaphoreType.DMA
    vmem = pl.BlockSpec(memory_space=pltpu.VMEM)
    both = pl.pallas_call(
        functools.partial(kernel, n_sy, n_sx, side, pad),
        out_shape=pltpu.VMEM((2, 2, cols, side), F32),
        in_specs=[pl.BlockSpec(memory_space=pl.ANY)] * 7,
        out_specs=vmem,
        scratch_shapes=[
            pltpu.VMEM(loads.shape, F32),
            pltpu.VMEM(basis.shape, F32),
            pltpu.VMEM(coarse_inv.shape, F32),
            pltpu.SMEM((1, 1, 2), jnp.int32),
            pltpu.SMEM((1, 1, 2), jnp.int32),
            pltpu.VMEM(trace_slot.shape, jnp.int32),
            pltpu.VMEM((traces, traces), F32),
            pltpu.VMEM((full, traces), BF16),
            pltpu.VMEM((traces, full), BF16),
            pltpu.VMEM((8, full), jnp.int32),
            pltpu.VMEM((full, 8), jnp.int32),
            pltpu.VMEM((traces, full), BF16),
            pltpu.VMEM((traces, full), BF16),
            pltpu.VMEM((full, LANES), BF16),
            pltpu.VMEM((full, LANES), BF16),
            pltpu.VMEM((5 * modes, full), BF16),
            pltpu.VMEM((5 * modes, full), BF16),
            pltpu.VMEM((5 * modes, full), BF16),
            pltpu.VMEM((5 * modes, full), BF16),
            pltpu.VMEM((2, cols, pad), F32),
            pltpu.VMEM((4, cols + modes + 8, pad), F32),
            pltpu.VMEM((4, cols + modes + 8, pad), F32),
            pltpu.VMEM((2, n_sy, modes, coarse_inv.shape[1]), F32),
            pltpu.VMEM(((n_sx + 2) * modes, turned_width), F32),
            pltpu.VMEM((n_sx, 3 * modes, turned_width), F32),
            pltpu.VMEM((n, 5 * modes, LANES), F32),
            pltpu.VMEM((2, 4, cols, pad), F32),
            pltpu.VMEM((2, 4, cols, pad), F32),
            pltpu.VMEM((1, width), F32),
            pltpu.VMEM((n, 1, width), F32),
            pltpu.VMEM((2, 1, 5 * width + LANES), F32),
            pltpu.VMEM((2, n + 2 * n_sx, 1, 5 * width + LANES), F32),
            pltpu.SemaphoreType.REGULAR,
            dma,
            dma((6,)),
            dma((4,)),
            dma((4,)),
            dma((2, n_sy)),
            dma((2, n_sy)),
            dma,
            dma,
            dma((2, 4)),
            dma((2, 4)),
            dma((3,)),
            dma((3,)),
        ],
        compiler_params=pltpu.CompilerParams(
            collective_id=0, has_side_effects=True, vmem_limit_bytes=60 * 1024 * 1024
        ),
    )(
        loads, flex, basis, coarse_inv,
        jnp.transpose(pair_size, (1, 2, 0)), jnp.transpose(owner, (1, 2, 0)), trace_slot,
    )

    out = jax.ShapeDtypeStruct(loads.shape, F32)
    return pl.pallas_call(
        lay_out, out_shape=(out, out), in_specs=[vmem], out_specs=(vmem, vmem)
    )(pltpu.with_memory_space_constraint(both, pltpu.VMEM))


def solution(mesh):
    return jax.shard_map(
        functools.partial(per_device, mesh.shape["sy"], mesh.shape["sx"]),
        mesh=mesh,
        in_specs=(
            P(None, None, "sy", "sx"),
            P("sy", "sx", None, None),
            P("sy", "sx", None, None),
            P("sx", "sy"),
            P(None, "sy", "sx"),
            P(None, "sy", "sx"),
            P(None, "sy", "sx"),
        ),
        out_specs=(P(None, None, "sy", "sx"), P(None, None, "sy", "sx")),
        check_vma=False,
    )
```

```python
import functools

import jax
import jax.numpy as jnp
from jax import lax
from jax.experimental import pallas as pl
from jax.experimental.pallas import tpu as pltpu
from jax.sharding import PartitionSpec as P

LANES = 128
MESH = pl.DeviceIdType.MESH
OPPOSITE = (1, 0, 3, 2)
F32 = jnp.float32
BF16 = jnp.bfloat16


def dot(a, b):
    return jnp.dot(a, b, preferred_element_type=F32)


def dot_nt(a, b):
    return lax.dot_general(a, b, (((1,), (1,)), ((), ())), preferred_element_type=F32)


def split(x):
    hi = x.astype(BF16)
    return hi, (x - hi.astype(F32)).astype(BF16)


def dot3_nt(x, w_hi, w_lo):
    rows = x.shape[0]
    hi, lo = split(x)
    both = dot_nt(jnp.concatenate([hi, lo], axis=0), w_hi)
    return both[:rows] + both[rows:] + dot_nt(hi, w_lo)


def dot_exact(x, ones):
    rows = x.shape[0]
    both = dot(jnp.concatenate(split(x), axis=0), ones)
    return both[:rows] + both[rows:]


def dot3(x, w_hi, w_lo):
    rows = x.shape[0]
    hi, lo = split(x)
    both = dot(jnp.concatenate([hi, lo], axis=0), w_hi)
    return both[:rows] + both[rows:] + dot(hi, w_lo)


def kernel(
    n_sy, n_sx, side, pad,
    loads_in, flex_in, basis_in, cinv_own, size_in, owner_in, slot_in,
    both_ref,
    loads_ref, basis_ref, cinv_ref, size_ref, owner_ref, slot_ref,
    flex_v, q, q_t, slot_row, slot_col, a_hi, a_lo,
    b8_hi, b8_lo, bb_hi, bb_lo, ka_hi, ka_lo, loads_s, send_a, recv_a, cinv_in, turned, side_in, cr,
    g_send, g_recv, c_send, c_all, five_send, five_all,
    ready_sem, flex_sem, in_sem, sa_sem, ra_sem, sc_sem, rc_sem, ss_sem, rs_sem, sg_sem, rg_sem,
    sag_sem, rag_sem,
):
    cols = loads_ref.shape[1]
    modes = basis_ref.shape[2]
    traces = flex_v.shape[0]
    full = 4 * pad
    groups = LANES // modes
    halves = cols // groups
    n = n_sy * n_sx
    i = lax.axis_index("sy")
    j = lax.axis_index("sx")
    me = i * n_sx + j
    exists = (j > 0, j < n_sx - 1, i > 0, i < n_sy - 1)
    place = ((i, j - 1), (i, j + 1), (i - 1, j), (i + 1, j))

    barrier = pltpu.get_barrier_semaphore()
    row_mates = [(i, lax.rem(j + o, n_sx)) for o in range(1, n_sx)]
    column_mates = [(lax.rem(i + o, n_sy), j) for o in range(1, n_sy)]
    for mate in row_mates + column_mates:
        pl.semaphore_signal(barrier, inc=1, device_id=mate, device_id_type=MESH)

    fetches = [
        pltpu.make_async_copy(src, dst, in_sem.at[q])
        for q, (src, dst) in enumerate(
            (
                (slot_in, slot_ref), (basis_in, basis_ref), (cinv_own, cinv_ref), (loads_in, loads_ref),
                (size_in, size_ref), (owner_in, owner_ref),
            )
        )
    ]
    for fetch in fetches:
        fetch.start()
    flex_copy = pltpu.make_async_copy(flex_in.at[0, 0], flex_v, flex_sem)
    flex_copy.start()
    for s in range(4):
        @pl.when(jnp.logical_not(exists[s]))
        def _(s=s):
            recv_a[s] = jnp.zeros(recv_a.shape[1:], F32)
            for phase in range(2):
                g_recv[phase, s] = jnp.zeros(g_recv.shape[2:], F32)
            if s >= 2:
                cinv_in[s - 2] = jnp.zeros(cinv_in.shape[1:], F32)

    turned[...] = jnp.zeros_like(turned)
    five = 1 + len(exists)
    wide = five * LANES
    def shifted(at, o, size):
        return lax.bitwise_xor(at, o) if size & (size - 1) == 0 else lax.rem(at + o, size)

    def device(o):
        return (shifted(i, lax.rem(o, n_sy), n_sy), shifted(j, lax.div(o, n_sy), n_sx))

    for fetch in fetches:
        fetch.wait()
    slot_row[...] = jnp.full_like(slot_row, -1)
    for s in range(4):
        slot_row[:, s * pad : s * pad + side] = jnp.broadcast_to(slot_ref[s], (8, side))
    trace_id = lax.broadcasted_iota(jnp.int32, (traces, full), 0)
    q_t[...] = (trace_id == slot_row[0:1, :]).astype(F32).astype(BF16)

    basis_hi, basis_lo = split(basis_ref[0, 0])
    both = dot(jnp.concatenate([basis_hi, basis_lo], axis=0), q_t[...])
    basis_side = both[:modes] + both[modes:]

    lane = lax.broadcasted_iota(jnp.int32, (1, pad), 1)
    signs = [(1 - 2 * owner_ref[0, 0, a]).astype(F32) for a in range(2)]
    own_mask = [jnp.where(lane < size_ref[0, 0, a], 1.0, 0.0).astype(F32) for a in range(2)]
    loads_s[...] = jnp.zeros_like(loads_s)
    for a in range(2):
        loads_s[a, :, :side] = loads_ref[a, :, 0, :]
    for s in range(4):
        send_a[s, cols : cols + modes] = basis_side[:, s * pad : (s + 1) * pad]
    start_side = [None] * 4
    for a, s in ((0, 1), (1, 3)):
        start_side[s] = loads_s[a] * (own_mask[a] * signs[a])
        send_a[s, :cols] = start_side[s]
        send_a[s, cols + modes :] = jnp.broadcast_to(own_mask[a], (8, pad))

    pl.semaphore_wait(barrier, n_sx + n_sy - 2)
    for mate in row_mates:
        pl.semaphore_signal(ready_sem, inc=1, device_id=mate, device_id_type=MESH)

    def first(s):
        return pltpu.make_async_remote_copy(
            src_ref=send_a.at[s],
            dst_ref=recv_a.at[OPPOSITE[s]],
            send_sem=sa_sem.at[s],
            recv_sem=ra_sem.at[OPPOSITE[s]],
            device_id=place[s],
            device_id_type=MESH,
        )

    def first_back(s):
        return pltpu.make_async_remote_copy(
            src_ref=send_a.at[s, pl.ds(cols, modes)],
            dst_ref=recv_a.at[OPPOSITE[s], pl.ds(cols, modes)],
            send_sem=sa_sem.at[s],
            recv_sem=ra_sem.at[OPPOSITE[s]],
            device_id=place[s],
            device_id_type=MESH,
        )

    make_first = (first_back, first, first_back, first)
    for s in range(4):
        @pl.when(exists[s])
        def _(s=s):
            make_first[s](s).start()

    def column_copy(slot, di, shift):
        i2 = lax.rem(i + di, n_sy)
        return pltpu.make_async_remote_copy(
            src_ref=cinv_ref.at[pl.ds(pl.multiple_of((i2 + shift) * modes, 8), modes)],
            dst_ref=cinv_in.at[slot, i],
            send_sem=sc_sem.at[slot, i2],
            recv_sem=rc_sem.at[slot, i],
            device_id=(i2, j),
            device_id_type=MESH,
        )

    def column_send(act):
        for di in range(1, n_sy):
            i2 = lax.rem(i + di, n_sy)

            @pl.when(i2 > 0)
            def _(di=di):
                act(column_copy(0, di, -1))

            @pl.when(i2 < n_sy - 1)
            def _(di=di):
                act(column_copy(1, di, 1))

    def landed(slot, src):
        here = cinv_in.at[slot, src]
        pltpu.make_async_copy(here, here, rc_sem.at[slot, src]).wait()

    def row_copy(mate):
        return pltpu.make_async_remote_copy(
            src_ref=turned.at[pl.ds(pl.multiple_of(mate[1] * modes, 8), 3 * modes)],
            dst_ref=side_in.at[j],
            send_sem=ss_sem,
            recv_sem=rs_sem,
            device_id=mate,
            device_id_type=MESH,
        )

    def row_all():
        block = side_in.at[pl.ds(0, n_sx - 1)]
        return pltpu.make_async_remote_copy(
            src_ref=block,
            dst_ref=block,
            send_sem=ss_sem,
            recv_sem=rs_sem,
            device_id=row_mates[0],
            device_id_type=MESH,
        )

    turned[modes : (n_sx + 1) * modes, : n_sy * modes] = jnp.transpose(cinv_ref[...])

    for mate in row_mates:
        row_copy(mate).start()
    column_send(lambda copy: copy.start())
    side_in[j] = turned[pl.ds(pl.multiple_of(j * modes, 8), 3 * modes)]

    @pl.when(i > 0)
    def _():
        cinv_in[0, i] = cinv_ref[pl.ds(pl.multiple_of((i - 1) * modes, 8), modes)]

    @pl.when(i < n_sy - 1)
    def _():
        cinv_in[1, i] = cinv_ref[pl.ds(pl.multiple_of((i + 1) * modes, 8), modes)]

    b8 = jnp.transpose(jnp.concatenate([basis_side] * groups, axis=0))
    part_hi, part_lo = split(b8)
    b8_hi[...] = part_hi
    b8_lo[...] = part_lo

    slot_col[...] = jnp.transpose(slot_row[...].astype(F32)).astype(jnp.int32)
    slot_id = lax.broadcasted_iota(jnp.int32, (full, traces), 1)
    q[...] = (slot_id == slot_col[:, 0:1]).astype(F32).astype(BF16)

    flex_copy.wait()

    chunks = 3
    chunk = traces // chunks

    def permute(step, carry):
        at = pl.ds(pl.multiple_of(step * chunk, chunk), chunk)
        both = dot(jnp.concatenate(split(flex_v[at, :]), axis=0), q_t[...]).astype(BF16)
        a_hi[at, :] = both[:chunk]
        a_lo[at, :] = both[chunk:]
        return carry

    def flexed_of(vec):
        rows = vec.shape[0]
        traced = dot(jnp.concatenate(split(vec), axis=0), q[...]).astype(BF16)
        both = dot(traced, a_hi[...])
        return both[:rows] + both[rows:] + dot(traced[:rows], a_lo[...])

    early = 2
    lax.fori_loop(0, early, permute, 0)

    for s in range(4):
        @pl.when(exists[OPPOSITE[s]])
        def _(s=s):
            make_first[s](s).wait_recv()
    masks = [None] * 4
    for a, s in ((0, 0), (1, 2)):
        start_side[s] = -recv_a[s, :cols]
        masks[s] = recv_a[s, cols + modes : cols + modes + 1]
        masks[s + 1] = own_mask[a]
    mask = jnp.concatenate(masks, axis=1)
    res = jnp.concatenate(start_side, axis=1)

    side_row = lax.broadcasted_iota(jnp.int32, (cols, halves * LANES), 0)
    side_lane = lax.broadcasted_iota(jnp.int32, (cols, halves * LANES), 1)
    on_col = jnp.where(lax.div(side_lane, modes) == side_row, 1.0, 0.0).astype(F32)
    bit_row = lax.broadcasted_iota(jnp.int32, (cols, LANES), 0)
    bit_lane = lax.broadcasted_iota(jnp.int32, (cols, LANES), 1)
    pick = jnp.where(lax.div(bit_lane, modes) == lax.rem(bit_row, groups), 1.0, 0.0).astype(F32)
    slot_of = lax.rem(lax.broadcasted_iota(jnp.int32, (1, LANES), 1), modes)
    in_half = lax.div(bit_row, groups)
    in_group = lax.rem(bit_row, groups)

    def to_row(column):
        return jnp.sum(column * on_col, axis=0, keepdims=True)

    def pack(rows):
        tile = jnp.zeros((1, LANES), F32)
        for v, row in enumerate(rows):
            for h in range(halves):
                tile = tile + jnp.where(slot_of == v * halves + h, row[:, h * LANES : (h + 1) * LANES], 0.0)
        return tile

    def unpack(phase, count):
        tile = jnp.sum(five_all[phase - 1, pl.ds(n_sx, n), 0, halves * wide :], axis=0, keepdims=True)
        columns = []
        for v in range(count):
            spot = jnp.where(bit_lane == in_group * modes + v * halves + in_half, 1.0, 0.0)
            columns.append(jnp.sum(tile * spot, axis=1, keepdims=True))
        return columns

    def send_all(src, dst, send_sem, recv_sem):
        def send(step, carry):
            o = n - step
            pltpu.make_async_remote_copy(
                src_ref=src,
                dst_ref=dst,
                send_sem=send_sem,
                recv_sem=recv_sem,
                device_id=device(o),
                device_id_type=MESH,
            ).start()
            return carry

        lax.fori_loop(1, n, send, 0)

    def all_of(block, send_sem, recv_sem):
        return pltpu.make_async_remote_copy(
            src_ref=block,
            dst_ref=block,
            send_sem=send_sem,
            recv_sem=recv_sem,
            device_id=device(1),
            device_id_type=MESH,
        )

    def all_coarse(phase):
        block = c_all.at[pl.ds(0, n - 1)] if phase == 0 else five_all.at[phase - 1, pl.ds(0, n - 1)]
        return all_of(block, sag_sem.at[phase], rag_sem.at[phase])

    def coarse_send(vec):
        product = dot3(vec, b8_hi[...], b8_lo[...]) * pick
        pieces = [
            jnp.sum(product[h * groups : (h + 1) * groups], axis=0, keepdims=True) for h in range(halves)
        ]
        message = jnp.concatenate(pieces, axis=1)
        c_send[...] = message
        c_all[me] = message
        pl.semaphore_wait(ready_sem, n_sx - 1)
        send_all(c_send, c_all.at[me], sag_sem.at[0], rag_sem.at[0])

    def five_send_all(phase, message):
        five_send[phase - 1] = message
        five_all[phase - 1, n_sx + me] = message
        send_all(
            five_send.at[phase - 1], five_all.at[phase - 1, n_sx + me], sag_sem.at[phase], rag_sem.at[phase]
        )

    unroll = 8
    shifts = (1, 0, -1, n_sx, -n_sx)

    def coarse_row(phase, d, h):
        if phase == 0:
            return c_all[d, :, h * LANES : (h + 1) * LANES]
        row = None
        for q, shift in enumerate(shifts):
            at = h * wide + q * LANES
            part = five_all[phase - 1, d + (n_sx + shift), :, at : at + LANES]
            row = part if row is None else row + part
        return row

    def coarse_take(phase):
        all_coarse(phase).wait_recv()

        def add(step, totals):
            totals = list(totals)
            for u in range(unroll):
                d = step * unroll + u
                rows = cr[d]
                for h in range(halves):
                    totals[h] = totals[h] + rows * coarse_row(phase, d, h)
            return tuple(totals)

        zero = jnp.zeros((five * modes, LANES), F32)
        return lax.fori_loop(0, n // unroll, add, (zero,) * halves)

    def weights_of(totals):
        gather = pick[:groups].astype(BF16)
        parts = []
        for total in totals:
            hi, lo = split(total)
            parts.append(dot_nt(gather, hi) + dot_nt(gather, lo))
        return jnp.concatenate(parts, axis=0)

    same_row = lax.broadcasted_iota(jnp.int32, (LANES, LANES), 0)
    same_lane = lax.broadcasted_iota(jnp.int32, (LANES, LANES), 1)
    same = (lax.div(same_row, modes) == lax.div(same_lane, modes)).astype(F32).astype(BF16)
    mode_row = lax.broadcasted_iota(jnp.int32, (modes, LANES), 0)
    mode_lane = lax.broadcasted_iota(jnp.int32, (modes, LANES), 1)
    on_mode = jnp.where(lax.rem(mode_lane, modes) == mode_row, 1.0, 0.0).astype(F32)
    repeat = on_col.astype(BF16)

    rows = five * modes

    def widened(blocks):
        sums = dot_exact(jnp.concatenate(blocks, axis=0), same)
        width = sums.shape[0] // halves
        return jnp.concatenate([sums[h * width : (h + 1) * width] for h in range(halves)], axis=1)

    def coupled(weights):
        hi, lo = split(weights)
        return dot3(coupling, hi, lo)

    def blocks_of(result):
        pieces = []
        for h in range(halves):
            for v in range(five):
                block = result[v * modes : (v + 1) * modes, h * LANES : (h + 1) * LANES]
                pieces.append(jnp.sum(block * on_mode, axis=0, keepdims=True))
        return pieces

    def column_sum(x, y):
        return jnp.sum(x * y, axis=0, keepdims=True)

    def swap(phase, s):
        return pltpu.make_async_remote_copy(
            src_ref=g_send.at[phase, s],
            dst_ref=g_recv.at[phase, OPPOSITE[s]],
            send_sem=sg_sem.at[phase, s],
            recv_sem=rg_sem.at[phase, OPPOSITE[s]],
            device_id=place[s],
            device_id_type=MESH,
        )

    def swap_start(phase, out):
        for s in range(4):
            g_send[phase, s] = out[:, s * pad : (s + 1) * pad]
        for s in range(4):
            @pl.when(exists[s])
            def _(s=s):
                swap(phase, s).start()

    def dual_take(phase, out):
        for s in range(4):
            @pl.when(exists[OPPOSITE[s]])
            def _(s=s):
                swap(phase, s).wait_recv()
        other = jnp.concatenate([g_recv[phase, s] for s in range(4)], axis=1)
        return (out - other) * mask

    def own_dot(x, y):
        total = x[:, pad : 2 * pad] * y[:, pad : 2 * pad] + x[:, 3 * pad :] * y[:, 3 * pad :]
        return jnp.sum(total, axis=1, keepdims=True)

    coarse_send(res)

    own_part = basis_side * mask
    lanes_at = lax.broadcasted_iota(jnp.int32, (modes, full), 1)
    nbr = jnp.concatenate([recv_a[s, cols : cols + modes] for s in range(4)], axis=1) * mask
    blocks = [jnp.where(lax.div(lanes_at, pad) == s, -nbr, 0.0) for s in range(4)]
    blocks.insert(1, own_part)
    basis_five = jnp.concatenate(blocks, axis=0)
    part_hi, part_lo = split(basis_five)
    bb_hi[...] = part_hi
    bb_lo[...] = part_lo

    lax.fori_loop(early, chunks, permute, 0)
    flexed = flexed_of(jnp.concatenate([basis_five, res], axis=0))
    flexed_basis = flexed[:rows]
    flexed_res = flexed[rows:]
    part_hi, part_lo = split(flexed_basis)
    ka_hi[...] = part_hi
    ka_lo[...] = part_lo
    res_hi, res_lo = split(res)
    coupling = dot3_nt(flexed_basis, bb_hi[...], bb_lo[...])
    known = dot_exact(dot3_nt(jnp.concatenate([flexed_basis, own_part], axis=0), res_hi, res_lo), repeat)
    known0 = known[:rows]
    coarse0 = known[rows:]
    square = to_row(own_dot(res, res))
    bend = to_row(jnp.sum(res * flexed_res, axis=1, keepdims=True))
    for di in range(1, n_sy):
        src = lax.rem(i + di, n_sy)

        @pl.when(i > 0)
        def _(src=src):
            landed(0, src)

        @pl.when(i < n_sy - 1)
        def _(src=src):
            landed(1, src)

    pick_row = lax.broadcasted_iota(jnp.int32, (LANES, LANES), 0)
    pick_lane = lax.broadcasted_iota(jnp.int32, (LANES, LANES), 1)

    def widen(block, group):
        at = (group // groups) * LANES
        chosen = pick_row == group % groups * modes + lax.rem(pick_lane, modes)
        value = block[..., at : at + LANES]
        wide_value = dot_exact(value.reshape(-1, LANES), chosen.astype(F32).astype(BF16))
        return wide_value.reshape(value.shape)

    for j2 in range(n_sx):
        block = widen(cinv_in[...], j2)
        for i2 in range(n_sy):
            for v in range(2):
                cr[i2 * n_sx + j2, (3 + v) * modes : (4 + v) * modes] = block[v, i2]
    row_all().wait_recv()
    for i2 in range(n_sy):
        cr[i2 * n_sx : (i2 + 1) * n_sx, : 3 * modes] = widen(side_in[...], i2)

    totals = coarse_take(0)
    weights = weights_of(totals)
    out0 = flexed_res + dot3(weights, ka_hi[...], ka_lo[...])
    swap_start(0, out0)
    weights0 = widened(totals)
    result0 = coupled(weights0) + known0
    norm_row = square + column_sum(coarse0, weights0[modes : 2 * modes])
    curve_row = bend + column_sum(weights0, result0 + known0)
    five_send_all(1, jnp.concatenate(blocks_of(result0) + [pack([norm_row, curve_row])], axis=1))
    for phase in range(2):
        edge = jnp.zeros((n_sx, 1, halves * wide + LANES), F32)
        five_all[phase, pl.ds(0, n_sx)] = edge
        five_all[phase, pl.ds(n_sx + n, n_sx)] = edge

    cor0 = res + dot3(weights, bb_hi[...], bb_lo[...])
    image0 = dual_take(0, out0)
    image_hi, image_lo = split(image0)
    known1 = dot_exact(dot3_nt(flexed_basis, image_hi, image_lo), repeat)
    flexed_image = flexed_of(image0)

    totals = coarse_take(1)
    own_rows = [coarse_row(1, me, h) * on_mode for h in range(halves)]
    sides = []
    for h in range(halves):
        sides += [totals[h], own_rows[h]]
    sides = widened(sides)
    weights1 = sides[:rows]
    coarse1 = sides[rows:]
    result1 = coupled(weights1) + known1
    norm0, curve0 = unpack(1, 2)
    step0 = norm0 / curve0
    step_row = to_row(step0)
    res1 = res - step0 * image0
    flexed_res1 = flexed_res - step0 * flexed_image
    square = to_row(own_dot(res1, res1))
    bend = to_row(jnp.sum(res1 * flexed_res1, axis=1, keepdims=True))
    change = weights0 - step_row * weights1
    norm_row = square + column_sum(coarse0 - step_row * coarse1, change[modes : 2 * modes])
    curve_row = bend + column_sum(change, (result0 + known0) - step_row * (result1 + known1))
    five_send_all(2, jnp.concatenate(blocks_of(result1) + [pack([norm_row, curve_row])], axis=1))
    weights = weights_of(totals)
    out1 = flexed_image + dot3(weights, ka_hi[...], ka_lo[...])
    swap_start(1, out1)
    pre_image0 = image0 + dot3(weights, bb_hi[...], bb_lo[...])
    cor1 = cor0 - step0 * pre_image0
    image1 = dual_take(1, out1)

    totals = coarse_take(2)
    norm1, curve1 = unpack(2, 2)
    beta = norm1 / norm0
    step1 = norm1 / (curve1 - beta * beta * curve0)
    total = step0 * cor0 + step1 * (cor1 + beta * cor0)
    near = cor1 - step1 * ((1.0 + beta) * pre_image0 - step0 * image1)
    weights = weights_of(totals)
    cor2 = near + (step1 * step0) * dot3(weights, bb_hi[...], bb_lo[...])
    for a in range(2):
        at = (2 * a + 1) * pad
        both_ref[0, a] = total[:, at : at + side] * signs[a]
        both_ref[1, a] = cor2[:, at : at + side] * signs[a]

    for s in range(4):
        @pl.when(exists[s])
        def _(s=s):
            make_first[s](s).wait_send()
            swap(0, s).wait_send()
            swap(1, s).wait_send()
    column_send(lambda copy: copy.wait_send())
    row_all().wait_send()
    for phase in range(3):
        all_coarse(phase).wait_send()


def lay_out(both_ref, mult_ref, prec_ref):
    for a in range(2):
        mult_ref[a, :, 0, :] = both_ref[0, a]
        prec_ref[a, :, 0, :] = both_ref[1, a]


def per_device(n_sy, n_sx, loads, flex, basis, coarse_inv, pair_size, owner, trace_slot):
    cols, side = loads.shape[1], loads.shape[3]
    modes, traces = basis.shape[2], basis.shape[3]
    pad = side
    full = 4 * pad
    n = n_sy * n_sx
    width = cols * modes
    turned_width = pl.cdiv(coarse_inv.shape[0], LANES) * LANES
    dma = pltpu.SemaphoreType.DMA
    vmem = pl.BlockSpec(memory_space=pltpu.VMEM)
    both = pl.pallas_call(
        functools.partial(kernel, n_sy, n_sx, side, pad),
        out_shape=pltpu.VMEM((2, 2, cols, side), F32),
        in_specs=[pl.BlockSpec(memory_space=pl.ANY)] * 7,
        out_specs=vmem,
        scratch_shapes=[
            pltpu.VMEM(loads.shape, F32),
            pltpu.VMEM(basis.shape, F32),
            pltpu.VMEM(coarse_inv.shape, F32),
            pltpu.SMEM((1, 1, 2), jnp.int32),
            pltpu.SMEM((1, 1, 2), jnp.int32),
            pltpu.VMEM(trace_slot.shape, jnp.int32),
            pltpu.VMEM((traces, traces), F32),
            pltpu.VMEM((full, traces), BF16),
            pltpu.VMEM((traces, full), BF16),
            pltpu.VMEM((8, full), jnp.int32),
            pltpu.VMEM((full, 8), jnp.int32),
            pltpu.VMEM((traces, full), BF16),
            pltpu.VMEM((traces, full), BF16),
            pltpu.VMEM((full, LANES), BF16),
            pltpu.VMEM((full, LANES), BF16),
            pltpu.VMEM((5 * modes, full), BF16),
            pltpu.VMEM((5 * modes, full), BF16),
            pltpu.VMEM((5 * modes, full), BF16),
            pltpu.VMEM((5 * modes, full), BF16),
            pltpu.VMEM((2, cols, pad), F32),
            pltpu.VMEM((4, cols + modes + 8, pad), F32),
            pltpu.VMEM((4, cols + modes + 8, pad), F32),
            pltpu.VMEM((2, n_sy, modes, coarse_inv.shape[1]), F32),
            pltpu.VMEM(((n_sx + 2) * modes, turned_width), F32),
            pltpu.VMEM((n_sx, 3 * modes, turned_width), F32),
            pltpu.VMEM((n, 5 * modes, LANES), F32),
            pltpu.VMEM((2, 4, cols, pad), F32),
            pltpu.VMEM((2, 4, cols, pad), F32),
            pltpu.VMEM((1, width), F32),
            pltpu.VMEM((n, 1, width), F32),
            pltpu.VMEM((2, 1, 5 * width + LANES), F32),
            pltpu.VMEM((2, n + 2 * n_sx, 1, 5 * width + LANES), F32),
            pltpu.SemaphoreType.REGULAR,
            dma,
            dma((6,)),
            dma((4,)),
            dma((4,)),
            dma((2, n_sy)),
            dma((2, n_sy)),
            dma,
            dma,
            dma((2, 4)),
            dma((2, 4)),
            dma((3,)),
            dma((3,)),
        ],
        compiler_params=pltpu.CompilerParams(
            collective_id=0, has_side_effects=True, vmem_limit_bytes=60 * 1024 * 1024
        ),
    )(
        loads, flex, basis, coarse_inv,
        jnp.transpose(pair_size, (1, 2, 0)), jnp.transpose(owner, (1, 2, 0)), trace_slot,
    )

    out = jax.ShapeDtypeStruct(loads.shape, F32)
    return pl.pallas_call(
        lay_out, out_shape=(out, out), in_specs=[vmem], out_specs=(vmem, vmem)
    )(pltpu.with_memory_space_constraint(both, pltpu.VMEM))


def solution(mesh):
    return jax.shard_map(
        functools.partial(per_device, mesh.shape["sy"], mesh.shape["sx"]),
        mesh=mesh,
        in_specs=(
            P(None, None, "sy", "sx"),
            P("sy", "sx", None, None),
            P("sy", "sx", None, None),
            P("sx", "sy"),
            P(None, "sy", "sx"),
            P(None, "sy", "sx"),
            P(None, "sy", "sx"),
        ),
        out_specs=(P(None, None, "sy", "sx"), P(None, None, "sy", "sx")),
        check_vma=False,
    )
```

```python
import functools

import jax
import jax.numpy as jnp
from jax import lax
from jax.experimental import pallas as pl
from jax.experimental.pallas import tpu as pltpu
from jax.sharding import PartitionSpec as P

LANES = 128
MESH = pl.DeviceIdType.MESH
OPPOSITE = (1, 0, 3, 2)
F32 = jnp.float32
BF16 = jnp.bfloat16


def dot(a, b):
    return jnp.dot(a, b, preferred_element_type=F32)


def dot_nt(a, b):
    return lax.dot_general(a, b, (((1,), (1,)), ((), ())), preferred_element_type=F32)


def split(x):
    hi = x.astype(BF16)
    return hi, (x - hi.astype(F32)).astype(BF16)


def dot3_nt(x, w_hi, w_lo):
    rows = x.shape[0]
    hi, lo = split(x)
    both = dot_nt(jnp.concatenate([hi, lo], axis=0), w_hi)
    return both[:rows] + both[rows:] + dot_nt(hi, w_lo)


def dot_exact(x, ones):
    rows = x.shape[0]
    both = dot(jnp.concatenate(split(x), axis=0), ones)
    return both[:rows] + both[rows:]


def dot3(x, w_hi, w_lo):
    rows = x.shape[0]
    hi, lo = split(x)
    both = dot(jnp.concatenate([hi, lo], axis=0), w_hi)
    return both[:rows] + both[rows:] + dot(hi, w_lo)


def kernel(
    n_sy, n_sx, side, pad,
    loads_in, flex_in, basis_in, cinv_own, size_in, owner_in, slot_in,
    both_ref,
    loads_ref, basis_ref, cinv_ref, size_ref, owner_ref, slot_ref,
    flex_v, q, q_t, slot_row, slot_col, a_hi, a_lo,
    b8_hi, b8_lo, bb_hi, bb_lo, ka_hi, ka_lo, loads_s, send_a, recv_a, cinv_in, turned, side_in, cr,
    g_send, g_recv, c_send, c_all, five_send, five_all,
    ready_sem, flex_sem, in_sem, sa_sem, ra_sem, sc_sem, rc_sem, ss_sem, rs_sem, sg_sem, rg_sem,
    sag_sem, rag_sem,
):
    cols = loads_ref.shape[1]
    modes = basis_ref.shape[2]
    traces = flex_v.shape[0]
    full = 4 * pad
    groups = LANES // modes
    halves = cols // groups
    n = n_sy * n_sx
    i = lax.axis_index("sy")
    j = lax.axis_index("sx")
    me = i * n_sx + j
    exists = (j > 0, j < n_sx - 1, i > 0, i < n_sy - 1)
    place = ((i, j - 1), (i, j + 1), (i - 1, j), (i + 1, j))

    barrier = pltpu.get_barrier_semaphore()
    row_mates = [(i, lax.rem(j + o, n_sx)) for o in range(1, n_sx)]
    column_mates = [(lax.rem(i + o, n_sy), j) for o in range(1, n_sy)]
    for mate in row_mates + column_mates:
        pl.semaphore_signal(barrier, inc=1, device_id=mate, device_id_type=MESH)

    fetches = [
        pltpu.make_async_copy(src, dst, in_sem.at[q])
        for q, (src, dst) in enumerate(
            (
                (slot_in, slot_ref), (basis_in, basis_ref), (cinv_own, cinv_ref), (loads_in, loads_ref),
                (size_in, size_ref), (owner_in, owner_ref),
            )
        )
    ]
    for fetch in fetches:
        fetch.start()
    flex_copy = pltpu.make_async_copy(flex_in.at[0, 0], flex_v, flex_sem)
    flex_copy.start()
    for s in range(4):
        @pl.when(jnp.logical_not(exists[s]))
        def _(s=s):
            recv_a[s] = jnp.zeros(recv_a.shape[1:], F32)
            for phase in range(2):
                g_recv[phase, s] = jnp.zeros(g_recv.shape[2:], F32)
            if s >= 2:
                cinv_in[s - 2] = jnp.zeros(cinv_in.shape[1:], F32)

    turned[...] = jnp.zeros_like(turned)
    five = 1 + len(exists)
    wide = five * LANES
    def shifted(at, o, size):
        return lax.bitwise_xor(at, o) if size & (size - 1) == 0 else lax.rem(at + o, size)

    def device(o):
        return (shifted(i, lax.rem(o, n_sy), n_sy), shifted(j, lax.div(o, n_sy), n_sx))

    for fetch in fetches:
        fetch.wait()
    slot_row[...] = jnp.full_like(slot_row, -1)
    for s in range(4):
        slot_row[:, s * pad : s * pad + side] = jnp.broadcast_to(slot_ref[s], (8, side))
    trace_id = lax.broadcasted_iota(jnp.int32, (traces, full), 0)
    q_t[...] = (trace_id == slot_row[0:1, :]).astype(F32).astype(BF16)

    basis_hi, basis_lo = split(basis_ref[0, 0])
    both = dot(jnp.concatenate([basis_hi, basis_lo], axis=0), q_t[...])
    basis_side = both[:modes] + both[modes:]

    lane = lax.broadcasted_iota(jnp.int32, (1, pad), 1)
    signs = [(1 - 2 * owner_ref[0, 0, a]).astype(F32) for a in range(2)]
    own_mask = [jnp.where(lane < size_ref[0, 0, a], 1.0, 0.0).astype(F32) for a in range(2)]
    loads_s[...] = jnp.zeros_like(loads_s)
    for a in range(2):
        loads_s[a, :, :side] = loads_ref[a, :, 0, :]
    for s in range(4):
        send_a[s, cols : cols + modes] = basis_side[:, s * pad : (s + 1) * pad]
    start_side = [None] * 4
    for a, s in ((0, 1), (1, 3)):
        start_side[s] = loads_s[a] * (own_mask[a] * signs[a])
        send_a[s, :cols] = start_side[s]
        send_a[s, cols + modes :] = jnp.broadcast_to(own_mask[a], (8, pad))

    pl.semaphore_wait(barrier, n_sx + n_sy - 2)
    for mate in row_mates:
        pl.semaphore_signal(ready_sem, inc=1, device_id=mate, device_id_type=MESH)

    def first(s):
        return pltpu.make_async_remote_copy(
            src_ref=send_a.at[s],
            dst_ref=recv_a.at[OPPOSITE[s]],
            send_sem=sa_sem.at[s],
            recv_sem=ra_sem.at[OPPOSITE[s]],
            device_id=place[s],
            device_id_type=MESH,
        )

    def first_back(s):
        return pltpu.make_async_remote_copy(
            src_ref=send_a.at[s, pl.ds(cols, modes)],
            dst_ref=recv_a.at[OPPOSITE[s], pl.ds(cols, modes)],
            send_sem=sa_sem.at[s],
            recv_sem=ra_sem.at[OPPOSITE[s]],
            device_id=place[s],
            device_id_type=MESH,
        )

    make_first = (first_back, first, first_back, first)
    for s in range(4):
        @pl.when(exists[s])
        def _(s=s):
            make_first[s](s).start()

    def column_copy(slot, di, shift):
        i2 = lax.rem(i + di, n_sy)
        return pltpu.make_async_remote_copy(
            src_ref=cinv_ref.at[pl.ds(pl.multiple_of((i2 + shift) * modes, 8), modes)],
            dst_ref=cinv_in.at[slot, i],
            send_sem=sc_sem.at[slot, i2],
            recv_sem=rc_sem.at[slot, i],
            device_id=(i2, j),
            device_id_type=MESH,
        )

    def column_send(act):
        for di in range(1, n_sy):
            i2 = lax.rem(i + di, n_sy)

            @pl.when(i2 > 0)
            def _(di=di):
                act(column_copy(0, di, -1))

            @pl.when(i2 < n_sy - 1)
            def _(di=di):
                act(column_copy(1, di, 1))

    def landed(slot, src):
        here = cinv_in.at[slot, src]
        pltpu.make_async_copy(here, here, rc_sem.at[slot, src]).wait()

    def row_copy(mate):
        return pltpu.make_async_remote_copy(
            src_ref=turned.at[pl.ds(pl.multiple_of(mate[1] * modes, 8), 3 * modes)],
            dst_ref=side_in.at[j],
            send_sem=ss_sem,
            recv_sem=rs_sem,
            device_id=mate,
            device_id_type=MESH,
        )

    def row_all():
        block = side_in.at[pl.ds(0, n_sx - 1)]
        return pltpu.make_async_remote_copy(
            src_ref=block,
            dst_ref=block,
            send_sem=ss_sem,
            recv_sem=rs_sem,
            device_id=row_mates[0],
            device_id_type=MESH,
        )

    turned[modes : (n_sx + 1) * modes, : n_sy * modes] = jnp.transpose(cinv_ref[...])

    for mate in row_mates:
        row_copy(mate).start()
    column_send(lambda copy: copy.start())
    side_in[j] = turned[pl.ds(pl.multiple_of(j * modes, 8), 3 * modes)]

    @pl.when(i > 0)
    def _():
        cinv_in[0, i] = cinv_ref[pl.ds(pl.multiple_of((i - 1) * modes, 8), modes)]

    @pl.when(i < n_sy - 1)
    def _():
        cinv_in[1, i] = cinv_ref[pl.ds(pl.multiple_of((i + 1) * modes, 8), modes)]

    b8 = jnp.transpose(jnp.concatenate([basis_side] * groups, axis=0))
    part_hi, part_lo = split(b8)
    b8_hi[...] = part_hi
    b8_lo[...] = part_lo

    slot_col[...] = jnp.transpose(slot_row[...].astype(F32)).astype(jnp.int32)
    slot_id = lax.broadcasted_iota(jnp.int32, (full, traces), 1)
    q[...] = (slot_id == slot_col[:, 0:1]).astype(F32).astype(BF16)

    flex_copy.wait()

    chunks = 3
    chunk = traces // chunks

    def permute(step, carry):
        at = pl.ds(pl.multiple_of(step * chunk, chunk), chunk)
        both = dot(jnp.concatenate(split(flex_v[at, :]), axis=0), q_t[...]).astype(BF16)
        a_hi[at, :] = both[:chunk]
        a_lo[at, :] = both[chunk:]
        return carry

    def flexed_of(vec):
        rows = vec.shape[0]
        traced = dot(jnp.concatenate(split(vec), axis=0), q[...]).astype(BF16)
        both = dot(traced, a_hi[...])
        return both[:rows] + both[rows:] + dot(traced[:rows], a_lo[...])

    early = 2
    lax.fori_loop(0, early, permute, 0)

    for s in range(4):
        @pl.when(exists[OPPOSITE[s]])
        def _(s=s):
            make_first[s](s).wait_recv()
    masks = [None] * 4
    for a, s in ((0, 0), (1, 2)):
        start_side[s] = -recv_a[s, :cols]
        masks[s] = recv_a[s, cols + modes : cols + modes + 1]
        masks[s + 1] = own_mask[a]
    mask = jnp.concatenate(masks, axis=1)
    res = jnp.concatenate(start_side, axis=1)

    side_row = lax.broadcasted_iota(jnp.int32, (cols, halves * LANES), 0)
    side_lane = lax.broadcasted_iota(jnp.int32, (cols, halves * LANES), 1)
    on_col = jnp.where(lax.div(side_lane, modes) == side_row, 1.0, 0.0).astype(F32)
    bit_row = lax.broadcasted_iota(jnp.int32, (cols, LANES), 0)
    bit_lane = lax.broadcasted_iota(jnp.int32, (cols, LANES), 1)
    pick = jnp.where(lax.div(bit_lane, modes) == lax.rem(bit_row, groups), 1.0, 0.0).astype(F32)
    slot_of = lax.rem(lax.broadcasted_iota(jnp.int32, (1, LANES), 1), modes)
    in_half = lax.div(bit_row, groups)
    in_group = lax.rem(bit_row, groups)

    def to_row(column):
        return jnp.sum(column * on_col, axis=0, keepdims=True)

    def pack(rows):
        tile = jnp.zeros((1, LANES), F32)
        for v, row in enumerate(rows):
            for h in range(halves):
                tile = tile + jnp.where(slot_of == v * halves + h, row[:, h * LANES : (h + 1) * LANES], 0.0)
        return tile

    def unpack(phase, count):
        tile = jnp.sum(five_all[phase - 1, pl.ds(n_sx, n), 0, halves * wide :], axis=0, keepdims=True)
        columns = []
        for v in range(count):
            spot = jnp.where(bit_lane == in_group * modes + v * halves + in_half, 1.0, 0.0)
            columns.append(jnp.sum(tile * spot, axis=1, keepdims=True))
        return columns

    def send_all(src, dst, send_sem, recv_sem):
        def send(step, carry):
            o = n - step
            pltpu.make_async_remote_copy(
                src_ref=src,
                dst_ref=dst,
                send_sem=send_sem,
                recv_sem=recv_sem,
                device_id=device(o),
                device_id_type=MESH,
            ).start()
            return carry

        lax.fori_loop(1, n, send, 0)

    def all_of(block, send_sem, recv_sem):
        return pltpu.make_async_remote_copy(
            src_ref=block,
            dst_ref=block,
            send_sem=send_sem,
            recv_sem=recv_sem,
            device_id=device(1),
            device_id_type=MESH,
        )

    def all_coarse(phase):
        block = c_all.at[pl.ds(0, n - 1)] if phase == 0 else five_all.at[phase - 1, pl.ds(0, n - 1)]
        return all_of(block, sag_sem.at[phase], rag_sem.at[phase])

    def coarse_send(vec):
        product = dot3(vec, b8_hi[...], b8_lo[...]) * pick
        pieces = [
            jnp.sum(product[h * groups : (h + 1) * groups], axis=0, keepdims=True) for h in range(halves)
        ]
        message = jnp.concatenate(pieces, axis=1)
        c_send[...] = message
        c_all[me] = message
        pl.semaphore_wait(ready_sem, n_sx - 1)
        send_all(c_send, c_all.at[me], sag_sem.at[0], rag_sem.at[0])

    def five_send_all(phase, message):
        five_send[phase - 1] = message
        five_all[phase - 1, n_sx + me] = message
        send_all(
            five_send.at[phase - 1], five_all.at[phase - 1, n_sx + me], sag_sem.at[phase], rag_sem.at[phase]
        )

    unroll = 8
    shifts = (1, 0, -1, n_sx, -n_sx)

    def coarse_row(phase, d, h):
        if phase == 0:
            return c_all[d, :, h * LANES : (h + 1) * LANES]
        row = None
        for q, shift in enumerate(shifts):
            at = h * wide + q * LANES
            part = five_all[phase - 1, d + (n_sx + shift), :, at : at + LANES]
            row = part if row is None else row + part
        return row

    def coarse_take(phase):
        all_coarse(phase).wait_recv()

        def add(step, totals):
            totals = list(totals)
            for u in range(unroll):
                d = step * unroll + u
                rows = cr[d]
                for h in range(halves):
                    totals[h] = totals[h] + rows * coarse_row(phase, d, h)
            return tuple(totals)

        zero = jnp.zeros((five * modes, LANES), F32)
        return lax.fori_loop(0, n // unroll, add, (zero,) * halves)

    def weights_of(totals):
        gather = pick[:groups].astype(BF16)
        parts = []
        for total in totals:
            hi, lo = split(total)
            parts.append(dot_nt(gather, hi) + dot_nt(gather, lo))
        return jnp.concatenate(parts, axis=0)

    same_row = lax.broadcasted_iota(jnp.int32, (LANES, LANES), 0)
    same_lane = lax.broadcasted_iota(jnp.int32, (LANES, LANES), 1)
    same = (lax.div(same_row, modes) == lax.div(same_lane, modes)).astype(F32).astype(BF16)
    mode_row = lax.broadcasted_iota(jnp.int32, (modes, LANES), 0)
    mode_lane = lax.broadcasted_iota(jnp.int32, (modes, LANES), 1)
    on_mode = jnp.where(lax.rem(mode_lane, modes) == mode_row, 1.0, 0.0).astype(F32)
    repeat = on_col.astype(BF16)

    rows = five * modes

    def widened(blocks):
        sums = dot_exact(jnp.concatenate(blocks, axis=0), same)
        width = sums.shape[0] // halves
        return jnp.concatenate([sums[h * width : (h + 1) * width] for h in range(halves)], axis=1)

    def coupled(weights):
        hi, lo = split(weights)
        return dot3(coupling, hi, lo)

    def blocks_of(result):
        pieces = []
        for h in range(halves):
            for v in range(five):
                block = result[v * modes : (v + 1) * modes, h * LANES : (h + 1) * LANES]
                pieces.append(jnp.sum(block * on_mode, axis=0, keepdims=True))
        return pieces

    def column_sum(x, y):
        return jnp.sum(x * y, axis=0, keepdims=True)

    def swap(phase, s):
        return pltpu.make_async_remote_copy(
            src_ref=g_send.at[phase, s],
            dst_ref=g_recv.at[phase, OPPOSITE[s]],
            send_sem=sg_sem.at[phase, s],
            recv_sem=rg_sem.at[phase, OPPOSITE[s]],
            device_id=place[s],
            device_id_type=MESH,
        )

    def swap_start(phase, out):
        for s in range(4):
            g_send[phase, s] = out[:, s * pad : (s + 1) * pad]
        for s in range(4):
            @pl.when(exists[s])
            def _(s=s):
                swap(phase, s).start()

    def dual_take(phase, out):
        for s in range(4):
            @pl.when(exists[OPPOSITE[s]])
            def _(s=s):
                swap(phase, s).wait_recv()
        other = jnp.concatenate([g_recv[phase, s] for s in range(4)], axis=1)
        return (out - other) * mask

    def own_dot(x, y):
        total = x[:, pad : 2 * pad] * y[:, pad : 2 * pad] + x[:, 3 * pad :] * y[:, 3 * pad :]
        return jnp.sum(total, axis=1, keepdims=True)

    coarse_send(res)

    own_part = basis_side * mask
    lanes_at = lax.broadcasted_iota(jnp.int32, (modes, full), 1)
    nbr = jnp.concatenate([recv_a[s, cols : cols + modes] for s in range(4)], axis=1) * mask
    blocks = [jnp.where(lax.div(lanes_at, pad) == s, -nbr, 0.0) for s in range(4)]
    blocks.insert(1, own_part)
    basis_five = jnp.concatenate(blocks, axis=0)
    part_hi, part_lo = split(basis_five)
    bb_hi[...] = part_hi
    bb_lo[...] = part_lo

    lax.fori_loop(early, chunks, permute, 0)
    flexed = flexed_of(jnp.concatenate([basis_five, res], axis=0))
    flexed_basis = flexed[:rows]
    flexed_res = flexed[rows:]
    part_hi, part_lo = split(flexed_basis)
    ka_hi[...] = part_hi
    ka_lo[...] = part_lo
    res_hi, res_lo = split(res)
    coupling = dot3_nt(flexed_basis, bb_hi[...], bb_lo[...])
    known = dot_exact(dot3_nt(jnp.concatenate([flexed_basis, own_part], axis=0), res_hi, res_lo), repeat)
    known0 = known[:rows]
    coarse0 = known[rows:]
    square = to_row(own_dot(res, res))
    bend = to_row(jnp.sum(res * flexed_res, axis=1, keepdims=True))
    for di in range(1, n_sy):
        src = lax.rem(i + di, n_sy)

        @pl.when(i > 0)
        def _(src=src):
            landed(0, src)

        @pl.when(i < n_sy - 1)
        def _(src=src):
            landed(1, src)

    pick_row = lax.broadcasted_iota(jnp.int32, (LANES, LANES), 0)
    pick_lane = lax.broadcasted_iota(jnp.int32, (LANES, LANES), 1)

    def widen(block, group):
        at = (group // groups) * LANES
        chosen = pick_row == group % groups * modes + lax.rem(pick_lane, modes)
        value = block[..., at : at + LANES]
        wide_value = dot_exact(value.reshape(-1, LANES), chosen.astype(F32).astype(BF16))
        return wide_value.reshape(value.shape)

    for j2 in range(n_sx):
        block = widen(cinv_in[...], j2)
        for i2 in range(n_sy):
            for v in range(2):
                cr[i2 * n_sx + j2, (3 + v) * modes : (4 + v) * modes] = block[v, i2]
    row_all().wait_recv()
    for i2 in range(n_sy):
        cr[i2 * n_sx : (i2 + 1) * n_sx, : 3 * modes] = widen(side_in[...], i2)

    totals = coarse_take(0)
    weights = weights_of(totals)
    out0 = flexed_res + dot3(weights, ka_hi[...], ka_lo[...])
    swap_start(0, out0)
    weights0 = widened(totals)
    result0 = coupled(weights0) + known0
    norm_row = square + column_sum(coarse0, weights0[modes : 2 * modes])
    curve_row = bend + column_sum(weights0, result0 + known0)
    five_send_all(1, jnp.concatenate(blocks_of(result0) + [pack([norm_row, curve_row])], axis=1))
    for phase in range(2):
        edge = jnp.zeros((n_sx, 1, halves * wide + LANES), F32)
        five_all[phase, pl.ds(0, n_sx)] = edge
        five_all[phase, pl.ds(n_sx + n, n_sx)] = edge

    cor0 = res + dot3(weights, bb_hi[...], bb_lo[...])
    image0 = dual_take(0, out0)
    image_hi, image_lo = split(image0)
    known1 = dot_exact(dot3_nt(flexed_basis, image_hi, image_lo), repeat)
    flexed_image = flexed_of(image0)

    totals = coarse_take(1)
    own_rows = [coarse_row(1, me, h) * on_mode for h in range(halves)]
    sides = []
    for h in range(halves):
        sides += [totals[h], own_rows[h]]
    sides = widened(sides)
    weights1 = sides[:rows]
    coarse1 = sides[rows:]
    result1 = coupled(weights1) + known1
    norm0, curve0 = unpack(1, 2)
    step0 = norm0 / curve0
    step_row = to_row(step0)
    res1 = res - step0 * image0
    flexed_res1 = flexed_res - step0 * flexed_image
    square = to_row(own_dot(res1, res1))
    bend = to_row(jnp.sum(res1 * flexed_res1, axis=1, keepdims=True))
    change = weights0 - step_row * weights1
    norm_row = square + column_sum(coarse0 - step_row * coarse1, change[modes : 2 * modes])
    curve_row = bend + column_sum(change, (result0 + known0) - step_row * (result1 + known1))
    five_send_all(2, jnp.concatenate(blocks_of(result1) + [pack([norm_row, curve_row])], axis=1))
    weights = weights_of(totals)
    out1 = flexed_image + dot3(weights, ka_hi[...], ka_lo[...])
    pre_image0 = image0 + dot3(weights, bb_hi[...], bb_lo[...])
    cor1 = cor0 - step0 * pre_image0
    swap_start(1, out1)
    image1 = dual_take(1, out1)

    totals = coarse_take(2)
    norm1, curve1 = unpack(2, 2)
    beta = norm1 / norm0
    step1 = norm1 / (curve1 - beta * beta * curve0)
    total = step0 * cor0 + step1 * (cor1 + beta * cor0)
    near = cor1 - step1 * ((1.0 + beta) * pre_image0 - step0 * image1)
    weights = weights_of(totals)
    cor2 = near + (step1 * step0) * dot3(weights, bb_hi[...], bb_lo[...])
    for a in range(2):
        at = (2 * a + 1) * pad
        both_ref[0, a] = total[:, at : at + side] * signs[a]
        both_ref[1, a] = cor2[:, at : at + side] * signs[a]

    for s in range(4):
        @pl.when(exists[s])
        def _(s=s):
            make_first[s](s).wait_send()
            swap(0, s).wait_send()
            swap(1, s).wait_send()
    column_send(lambda copy: copy.wait_send())
    row_all().wait_send()
    for phase in range(3):
        all_coarse(phase).wait_send()


def lay_out(both_ref, mult_ref, prec_ref):
    for a in range(2):
        mult_ref[a, :, 0, :] = both_ref[0, a]
        prec_ref[a, :, 0, :] = both_ref[1, a]


def per_device(n_sy, n_sx, loads, flex, basis, coarse_inv, pair_size, owner, trace_slot):
    cols, side = loads.shape[1], loads.shape[3]
    modes, traces = basis.shape[2], basis.shape[3]
    pad = side
    full = 4 * pad
    n = n_sy * n_sx
    width = cols * modes
    turned_width = pl.cdiv(coarse_inv.shape[0], LANES) * LANES
    dma = pltpu.SemaphoreType.DMA
    vmem = pl.BlockSpec(memory_space=pltpu.VMEM)
    both = pl.pallas_call(
        functools.partial(kernel, n_sy, n_sx, side, pad),
        out_shape=pltpu.VMEM((2, 2, cols, side), F32),
        in_specs=[pl.BlockSpec(memory_space=pl.ANY)] * 7,
        out_specs=vmem,
        scratch_shapes=[
            pltpu.VMEM(loads.shape, F32),
            pltpu.VMEM(basis.shape, F32),
            pltpu.VMEM(coarse_inv.shape, F32),
            pltpu.SMEM((1, 1, 2), jnp.int32),
            pltpu.SMEM((1, 1, 2), jnp.int32),
            pltpu.VMEM(trace_slot.shape, jnp.int32),
            pltpu.VMEM((traces, traces), F32),
            pltpu.VMEM((full, traces), BF16),
            pltpu.VMEM((traces, full), BF16),
            pltpu.VMEM((8, full), jnp.int32),
            pltpu.VMEM((full, 8), jnp.int32),
            pltpu.VMEM((traces, full), BF16),
            pltpu.VMEM((traces, full), BF16),
            pltpu.VMEM((full, LANES), BF16),
            pltpu.VMEM((full, LANES), BF16),
            pltpu.VMEM((5 * modes, full), BF16),
            pltpu.VMEM((5 * modes, full), BF16),
            pltpu.VMEM((5 * modes, full), BF16),
            pltpu.VMEM((5 * modes, full), BF16),
            pltpu.VMEM((2, cols, pad), F32),
            pltpu.VMEM((4, cols + modes + 8, pad), F32),
            pltpu.VMEM((4, cols + modes + 8, pad), F32),
            pltpu.VMEM((2, n_sy, modes, coarse_inv.shape[1]), F32),
            pltpu.VMEM(((n_sx + 2) * modes, turned_width), F32),
            pltpu.VMEM((n_sx, 3 * modes, turned_width), F32),
            pltpu.VMEM((n, 5 * modes, LANES), F32),
            pltpu.VMEM((2, 4, cols, pad), F32),
            pltpu.VMEM((2, 4, cols, pad), F32),
            pltpu.VMEM((1, width), F32),
            pltpu.VMEM((n, 1, width), F32),
            pltpu.VMEM((2, 1, 5 * width + LANES), F32),
            pltpu.VMEM((2, n + 2 * n_sx, 1, 5 * width + LANES), F32),
            pltpu.SemaphoreType.REGULAR,
            dma,
            dma((6,)),
            dma((4,)),
            dma((4,)),
            dma((2, n_sy)),
            dma((2, n_sy)),
            dma,
            dma,
            dma((2, 4)),
            dma((2, 4)),
            dma((3,)),
            dma((3,)),
        ],
        compiler_params=pltpu.CompilerParams(
            collective_id=0, has_side_effects=True, vmem_limit_bytes=60 * 1024 * 1024
        ),
    )(
        loads, flex, basis, coarse_inv,
        jnp.transpose(pair_size, (1, 2, 0)), jnp.transpose(owner, (1, 2, 0)), trace_slot,
    )

    out = jax.ShapeDtypeStruct(loads.shape, F32)
    return pl.pallas_call(
        lay_out, out_shape=(out, out), in_specs=[vmem], out_specs=(vmem, vmem)
    )(pltpu.with_memory_space_constraint(both, pltpu.VMEM))


def solution(mesh):
    return jax.shard_map(
        functools.partial(per_device, mesh.shape["sy"], mesh.shape["sx"]),
        mesh=mesh,
        in_specs=(
            P(None, None, "sy", "sx"),
            P("sy", "sx", None, None),
            P("sy", "sx", None, None),
            P("sx", "sy"),
            P(None, "sy", "sx"),
            P(None, "sy", "sx"),
            P(None, "sy", "sx"),
        ),
        out_specs=(P(None, None, "sy", "sx"), P(None, None, "sy", "sx")),
        check_vma=False,
    )
```
